32 devices in a mesh: batch: 8 (over z, x), head: 4 (over y, core).
Axes of the slice: x: 2, y: 2, z: 4, core: 2. Of those that a mesh axis runs over, the one named last changes fastest.
Arguments:
- tokens: bfloat16 [8, 2048, 768], P('batch', 'head'), may hold values from -6 to 6
- lengths: int32 [8], P('batch'), may hold values from 1024 to 2048, as said below
- w_query: bfloat16 [768, 768], P(None, 'head'), may hold values from -0.3125 to 0.3125
- w_key: bfloat16 [768, 768], P(None, 'head'), may hold values from -0.3125 to 0.3125
- w_value: bfloat16 [768, 768], P(None, 'head'), may hold values from -0.21875 to 0.21875
- w_out: bfloat16 [768, 768], P('head'), may hold values from -0.4375 to 0.4375
- conv_taps: float32 [12, 65], P('head'), may hold values from -0.875 to 0.875
- w_up: bfloat16 [768, 3072], P(None, 'head'), may hold values from -0.21875 to 0.21875
- b_up: float32 [3072], P('head'), may hold values from -3 to 3
- w_down: bfloat16 [3072, 768], P('head'), may hold values from -0.109375 to 0.109375
- gain_attn: float32 [768], replicated, may hold values from 0.5 to 1.5
- shift_attn: float32 [768], replicated, may hold values from -1.75 to 1.75
- gain_ffn: float32 [768], replicated, may hold values from 0.5 to 1.5
- shift_ffn: float32 [768], replicated, may hold values from -1.75 to 1.75
- grad_out: bfloat16 [8, 2048, 768], P('batch', 'head'), may hold values from -6 to 6
Outputs:
- output: bfloat16 [8, 2048, 768], P('batch', 'head')
- d_tokens: float32 [8, 2048, 768], P('batch', 'head')
- d_w_query: float32 [768, 768], P(None, 'head')
- d_w_key: float32 [768, 768], P(None, 'head')
- d_w_value: float32 [768, 768], P(None, 'head')
- d_w_out: float32 [768, 768], P('head')
- d_conv_taps: float32 [12, 65], P('head')
- d_w_up: float32 [768, 3072], P(None, 'head')
- d_b_up: float32 [3072], P('head')
- d_w_down: float32 [3072, 768], P('head')
- d_gain_attn: float32 [768], replicated
- d_shift_attn: float32 [768], replicated
- d_gain_ffn: float32 [768], replicated
- d_shift_ffn: float32 [768], replicated
The draws below stay inside these ranges and needn't reach their ends.
Inputs may be any that keep to these rules, and one draw needn't show every extreme that they name: `lengths`: the true length of each sequence; in every draw one sequence is exactly 2048 long.
All inputs are finite; a program needn't handle non-finite values.
Results may differ from the reference program's by a relative error of at most 0.015.
Values may be sent and summed in bfloat16 or wider, within the bound.
No kernel may reach another device: no remote copies, remote signals or barrier semaphores. Data moves between devices by JAX's collectives and lax.ppermute only.
A program may use at most 320 MiB of HBM per device.

```python
import jax
import jax.numpy as jnp
from jax import lax

D = 768
HEADS = 12
HEAD_DIM = 64
FF = 3072
LANDMARKS = 64
CONV = 65
NEWTON = 6
SEQ_LEN = 2048
SEQS = 8


def draw_lengths(key, part):
    key_values, key_place = jax.random.split(jax.random.fold_in(key, 11))
    values = jax.random.randint(key_values, (SEQS,), SEQ_LEN // 2, SEQ_LEN + 1, dtype=jnp.int32)
    chosen = jax.random.randint(key_place, (), 0, SEQS, dtype=jnp.int32)
    return jnp.where(jnp.arange(SEQS, dtype=jnp.int32) == chosen, SEQ_LEN, values).astype(jnp.int32)


def shard_levels(key, dims, cuts, smallest, largest):
    level, own = 1.0, jax.random.fold_in(key, 6)
    for dim, blocks in cuts:
        steps = jnp.exp(jax.random.uniform(jax.random.fold_in(own, dim), (blocks,), jnp.float32, smallest / len(cuts), largest / len(cuts)))
        level = level * jnp.repeat(steps, dims[dim] // blocks).reshape([-1 if axis == dim else 1 for axis in range(len(dims))])
    return level


def centred(key, dims, deviation, limit, cuts=(), kind=jnp.bfloat16):
    values = jax.random.normal(key, dims, jnp.float32) * deviation
    if len(cuts) > 0:
        values = shard_levels(key, dims, cuts, -0.22, 0.18) * values
    return jnp.clip(values, min=-limit, max=limit).astype(kind)


def setup_inputs(seed: int = 0) -> dict:
    splits = jax.random.split(jax.random.key(seed), 16)
    return {
        "tokens": centred(splits[0], (SEQS, SEQ_LEN, D), 1.0, 6.0, ((0, 8), (1, 4))),
        "lengths": draw_lengths(jax.random.fold_in(splits[15], 71), 0),
        "w_query": centred(splits[2], (D, D), (D // 2) ** -0.5, 0.3125, ((1, 4),)),
        "w_key": centred(splits[3], (D, D), (D // 2) ** -0.5, 0.3125, ((1, 4),)),
        "w_value": centred(splits[4], (D, D), D ** -0.5, 0.21875, ((1, 4),)),
        "w_out": centred(splits[5], (D, D), (D // 4) ** -0.5, 0.4375, ((0, 4),)),
        "conv_taps": centred(splits[6], (HEADS, CONV), 0.15, 0.875, ((0, 4),), jnp.float32),
        "w_up": centred(splits[7], (D, FF), D ** -0.5, 0.21875, ((1, 4),)),
        "b_up": centred(splits[8], (FF,), 0.5, 3.0, ((0, 4),), jnp.float32),
        "w_down": centred(splits[9], (FF, D), FF ** -0.5, 0.109375, ((0, 4),)),
        "gain_attn": jnp.clip(1.0 + 0.1 * jax.random.normal(splits[10], (D,), jnp.float32), 0.5, 1.5),
        "shift_attn": centred(splits[11], (D,), 0.3, 1.75, (), jnp.float32),
        "gain_ffn": jnp.clip(1.0 + 0.1 * jax.random.normal(splits[12], (D,), jnp.float32), 0.5, 1.5),
        "shift_ffn": centred(splits[13], (D,), 0.3, 1.75, (), jnp.float32),
        "grad_out": centred(splits[14], (SEQS, SEQ_LEN, D), 1.0, 6.0, ((0, 8), (1, 4))),
    }


@jax.custom_vjp
def low(v):
    return lax.optimization_barrier(v.astype(jnp.bfloat16)).astype(jnp.float32)

@jax.custom_vjp
def low_back(v):
    return v

def low_keep(v):
    return (low(v), None)

def low_pass(kept, grad):
    return (grad,)

def back_keep(v):
    return (v, None)

def back_low(kept, grad):
    return (low(grad),)
low.defvjp(low_keep, low_pass)
low_back.defvjp(back_keep, back_low)

def matmul(left, right):
    return jnp.dot(left, right, precision=lax.Precision.HIGHEST)

def sequence_masks(length, seq_total):
    positions = jnp.arange(seq_total, dtype=jnp.int32)
    landmark_ids = jnp.arange(LANDMARKS + 1, dtype=jnp.int32)
    bounds = landmark_ids * length // LANDMARKS
    member = (positions[None, :] >= bounds[:-1, None]) & (positions[None, :] < bounds[1:, None])
    widths = (bounds[1:] - bounds[:-1]).astype(jnp.float32)
    pool_matrix = member.astype(jnp.float32) / widths[:, None]
    valid_mask = (positions < length).astype(jnp.float32)
    return (valid_mask, pool_matrix)

def newton_inverse(matrix):
    identity = jnp.eye(matrix.shape[0], dtype=matrix.dtype)
    column_top = jnp.max(lax.optimization_barrier(jnp.sum(matrix, axis=0)))
    row_top = jnp.max(lax.optimization_barrier(jnp.sum(matrix, axis=1)))
    iterate = matrix.T / (column_top * row_top)
    for iteration in range(NEWTON):
        product = matmul(matrix, iterate)
        inner = 7.0 * identity - product
        inner = 15.0 * identity - matmul(product, inner)
        inner = 13.0 * identity - matmul(product, inner)
        iterate = 0.25 * matmul(iterate, inner)
    return iterate

def depthwise(values, taps):
    tap_count = taps.shape[0]
    half_width = tap_count // 2
    row_total = values.shape[0]
    padded = jnp.pad(values, ((half_width, half_width), (0, 0)))
    summed = taps[0] * padded[0:row_total]
    for offset in range(1, tap_count):
        summed = summed + taps[offset] * padded[offset:offset + row_total]
    return summed

def nystrom_head(query, key_rows, value_rows, taps, valid_mask, pool_matrix):
    scaling = query.shape[-1] ** (-0.25)
    query_scaled = query * (scaling * valid_mask[:, None])
    key_scaled = key_rows * (scaling * valid_mask[:, None])
    value_masked = value_rows * valid_mask[:, None]
    query_land = matmul(pool_matrix, query_scaled)
    key_land = matmul(pool_matrix, key_scaled)
    first_kernel = jax.nn.softmax(matmul(query_scaled, key_land.T), axis=-1)
    middle_kernel = jax.nn.softmax(matmul(query_land, key_land.T), axis=-1)
    third_scores = matmul(query_land, key_scaled.T)
    third_kernel = jax.nn.softmax(jnp.where(valid_mask[None, :] > 0.5, third_scores, -1e+30), axis=-1)
    inverse = newton_inverse(middle_kernel)
    mixed = matmul(first_kernel, matmul(inverse, matmul(third_kernel, value_masked)))
    return mixed + depthwise(value_masked, taps)

def layer_norm(values, gain, shift):
    centered = values - lax.optimization_barrier(jnp.mean(values, axis=-1, keepdims=True))
    variance = lax.optimization_barrier(jnp.mean(centered * centered, axis=-1, keepdims=True))
    return centered * lax.rsqrt(variance + 1e-05) * gain + shift

def split_heads(block):
    return block.reshape(block.shape[0], HEADS, HEAD_DIM).transpose(1, 0, 2)

def forward(inputs, w_query, w_key, w_value, w_out, conv_taps, w_up, b_up, w_down, gain_attn, shift_attn, gain_ffn, shift_ffn, valid_mask, pool_matrix):
    query = low_back(low(matmul(inputs, w_query)))
    key_rows = low_back(low(matmul(inputs, w_key)))
    value_rows = low_back(low(matmul(inputs, w_value)))
    heads_out = jax.vmap(nystrom_head, in_axes=(0, 0, 0, 0, None, None))(split_heads(query), split_heads(key_rows), split_heads(value_rows), conv_taps, valid_mask, pool_matrix)
    context = low(heads_out.transpose(1, 0, 2).reshape(inputs.shape[0], D))
    attended = low_back(matmul(context, w_out))
    normed = layer_norm(inputs + attended, gain_attn, shift_attn)
    upward = low_back(matmul(low(normed), w_up) + b_up)
    hidden = low(jax.nn.gelu(upward, approximate=False))
    downward = low_back(matmul(hidden, w_down))
    return layer_norm(normed + downward, gain_ffn, shift_ffn)

def reference(tokens, lengths, w_query, w_key, w_value, w_out, conv_taps, w_up, b_up, w_down, gain_attn, shift_attn, gain_ffn, shift_ffn, grad_out):
    weights = tuple((weight.astype(jnp.float32) for weight in (w_query, w_key, w_value, w_out, conv_taps, w_up, b_up, w_down, gain_attn, shift_attn, gain_ffn, shift_ffn)))

    def one_sequence(carry, item):
        seq_tokens, seq_length, seq_grad = item
        valid_mask, pool_matrix = sequence_masks(seq_length, SEQ_LEN)

        def apply_layer(inputs, *params):
            return forward(inputs, *params, valid_mask, pool_matrix)
        result, backward = jax.vjp(apply_layer, seq_tokens.astype(jnp.float32), *weights)
        grads = backward(seq_grad.astype(jnp.float32))
        carry = tuple((held + grad for held, grad in zip(carry, grads[1:])))
        return (carry, (result.astype(jnp.bfloat16), grads[0]))
    zeros = tuple((jnp.zeros_like(weight) for weight in weights))
    summed, stacked = lax.scan(one_sequence, zeros, (tokens, lengths, grad_out))
    return (stacked[0], stacked[1], summed[0], summed[1], summed[2], summed[3], summed[4], summed[5], summed[6], summed[7], summed[8], summed[9], summed[10], summed[11])
```

```python
import functools

import jax
import jax.numpy as jnp
from jax import lax
from jax.experimental import pallas as pl
from jax.experimental.pallas import tpu as pltpu
from jax.sharding import PartitionSpec as P

f32 = jnp.float32
bf16 = jnp.bfloat16
HEAD_DIM = 64
LANDMARKS = 64
NEWTON = 6
TAPS = 65
HALO = TAPS // 2
GROUP = 256
NN = ((1,), (0,))
NT = ((1,), (1,))
TN = ((0,), (0,))
VMEM = pltpu.VMEM
ANY = pl.ANY


def dot(a, b, dims=NN):
    return lax.dot_general(a, b, (dims, ((), ())), preferred_element_type=f32)


def split(x):
    high = x.astype(bf16)
    return high, (x - high.astype(f32)).astype(bf16)


def mm(a, b, dims=NN):
    a_high, a_low = split(a)
    b_high, b_low = split(b)
    return dot(a_high, b_high, dims) + (dot(a_high, b_low, dims) + dot(a_low, b_high, dims))


def mm_left(a, b, dims=NN):
    a_high, a_low = split(a)
    return dot(a_high, b, dims) + dot(a_low, b, dims)


def iota(shape, dim):
    return lax.broadcasted_iota(jnp.int32, shape, dim)


def call(body, outs, ins, scratch=(), flops=0, size=0, limit=40, name=None, smem=()):
    specs = [
        pl.BlockSpec(memory_space=pltpu.SMEM) if i in smem else pl.BlockSpec(memory_space=space)
        for i, (space, _) in enumerate(ins)
    ]
    return pl.pallas_call(
        body,
        out_shape=[jax.ShapeDtypeStruct(s, d) for s, d in outs],
        in_specs=specs,
        out_specs=[pl.BlockSpec(memory_space=VMEM)] * len(outs),
        scratch_shapes=list(scratch),
        compiler_params=pltpu.CompilerParams(vmem_limit_bytes=limit << 20),
        cost_estimate=pl.CostEstimate(flops=flops, bytes_accessed=size, transcendentals=0),
        name=name,
    )(*[value for _, value in ins])


def block_mask():
    return (iota((GROUP, GROUP), 0) >> 6) == (iota((GROUP, GROUP), 1) >> 6)


def spread(x):
    return jnp.where(block_mask(), jnp.concatenate([x, x, x, x], axis=0), 0.0)


def fold(x):
    kept = jnp.where(block_mask(), x, 0.0)
    return kept[0:64] + kept[64:128] + kept[128:192]


def rows_of(info, count, first):
    return info[1] + first + iota((count, 1), 0)


def landmark_kernel(p0, p1, p2, p3, wt, lm, chain):
    pooled = p0[...] + p1[...] + p2[...] + p3[...]
    high, low = split(pooled)
    both = jnp.concatenate([high, low], axis=0)
    lm[...] = jnp.zeros_like(lm)
    matrices, starts = [], []
    for head in range(3):
        pair = []
        for kind in range(2):
            rows = wt[kind * 192 + head * 64 : kind * 192 + head * 64 + 64]
            out = dot(both, rows, NT)
            out = out[0:64] + out[64:128]
            lm[:, kind * GROUP + head * 64 : kind * GROUP + head * 64 + 64] = out
            pair.append(out)
        scores = mm(pair[0], pair[1], NT) * 0.125
        raised = jnp.exp(scores - jnp.max(scores, axis=1, keepdims=True))
        matrix = raised / jnp.sum(raised, axis=1, keepdims=True)
        column = jnp.max(jnp.sum(matrix, axis=0, keepdims=True), axis=1, keepdims=True)
        row = jnp.max(jnp.sum(matrix, axis=1, keepdims=True), axis=0, keepdims=True)
        matrices.append(matrix)
        starts.append(matrix.T / (column * row))
    eye = (iota((64, 64), 0) == iota((64, 64), 1)).astype(f32)

    def step(it, iterates):
        results = []
        for head in range(3):
            z = iterates[head]
            product = mm(matrices[head], z)
            inner1 = 7.0 * eye - product
            inner2 = 15.0 * eye - mm(product, inner1)
            inner3 = 13.0 * eye - mm(product, inner2)
            chain[it, 0, head] = z
            chain[it, 1, head] = product
            chain[it, 2, head] = inner2
            chain[it, 3, head] = inner3
            results.append(0.25 * mm(z, inner3))
        return tuple(results)

    finals = lax.fori_loop(0, NEWTON, step, tuple(starts))
    for head in range(3):
        lm[:, 2 * GROUP + head * 64 : 2 * GROUP + head * 64 + 64] = finals[head]


def inverse_back_kernel(x0, x1, x2, x3, wst, lm, chain, out):
    total = x0[...] + x1[...] + x2[...] + x3[...]
    eye = (iota((64, 64), 0) == iota((64, 64), 1)).astype(f32)
    weight = wst[...]
    out[...] = jnp.zeros_like(out)
    grads, matrices, queries, keys = [], [], [], []
    for head in range(3):
        at = slice(head * 64, head * 64 + 64)
        grads.append(mm(total[:, at], weight[:, at], NT))
        query = lm[:, head * 64 : head * 64 + 64]
        key = lm[:, GROUP + head * 64 : GROUP + head * 64 + 64]
        scores = mm(query, key, NT) * 0.125
        raised = jnp.exp(scores - jnp.max(scores, axis=1, keepdims=True))
        matrices.append(raised / jnp.sum(raised, axis=1, keepdims=True))
        queries.append(query)
        keys.append(key)

    def step(count, carried):
        it = NEWTON - 1 - count
        results = []
        for head in range(3):
            dz_next, da = carried[2 * head], carried[2 * head + 1]
            z = chain[it, 0, head]
            product = chain[it, 1, head]
            inner1 = 7.0 * eye - product
            inner2 = chain[it, 2, head]
            inner3 = chain[it, 3, head]
            dz_next = 0.25 * dz_next
            dz = mm(dz_next, inner3, NT)
            d3 = -mm(z, dz_next, TN)
            d2 = -mm(product, d3, TN)
            d1 = mm(product, d2, TN)
            dp = mm(d3, inner2, NT) + mm(d2, inner1, NT) - d1
            da = da + mm(dp, z, NT)
            dz = dz + mm(matrices[head], dp, TN)
            results += [dz, da]
        return tuple(results)

    first = []
    for head in range(3):
        first += [grads[head], jnp.zeros((64, 64), f32)]
    last = lax.fori_loop(0, NEWTON, step, tuple(first))
    for head in range(3):
        dz, da = last[2 * head], last[2 * head + 1]
        matrix = matrices[head]
        columns = jnp.sum(matrix, axis=0, keepdims=True)
        rows = jnp.sum(matrix, axis=1, keepdims=True)
        column = jnp.max(columns, axis=1, keepdims=True)
        row = jnp.max(rows, axis=0, keepdims=True)
        scale = 1.0 / (column * row)
        da = da + dz.T * scale
        d_scale = -jnp.sum(jnp.sum(dz * matrix.T, axis=1, keepdims=True), axis=0, keepdims=True) * scale * scale
        column_hit = (columns == column).astype(f32)
        row_hit = (rows == row).astype(f32)
        da = da + d_scale * row * column_hit / jnp.sum(column_hit, axis=1, keepdims=True)
        da = da + d_scale * column * row_hit / jnp.sum(row_hit, axis=0, keepdims=True)
        ds = matrix * (da - jnp.sum(da * matrix, axis=1, keepdims=True)) * 0.125
        out[:, head * 64 : head * 64 + 64] = mm(ds, keys[head])
        out[:, GROUP + head * 64 : GROUP + head * 64 + 64] = mm(ds, queries[head], TN)


def fetch_projection(weights, held, sems):
    for i in range(4):
        for kind in range(3):
            pltpu.make_async_copy(
                weights[i].at[pl.ds(kind * 192, 192)], held.at[i, pl.ds(kind * GROUP, 192)], sems.at[i, kind]
            ).start()
            held[i, kind * GROUP + 192 : kind * GROUP + 256, :] = jnp.zeros((64, held.shape[2]), bf16)


def await_projection(weights, held, sems, i):
    for kind in range(3):
        pltpu.make_async_copy(
            weights[0].at[pl.ds(kind * 192, 192)], held.at[i, pl.ds(kind * GROUP, 192)], sems.at[i, kind]
        ).wait()


def project_kernel(info, tokens, before, after, w0, w1, w2, w3, q_out, k_out, v_out, held, sems):
    count = tokens.shape[0]
    fetch_projection((w0, w1, w2, w3), held, sems)
    valid = (rows_of(info, count, 0) < info[0]).astype(f32)
    valid_before = (rows_of(info, HALO, -HALO) < info[0]).astype(f32)
    valid_after = (rows_of(info, HALO, count) < info[0]).astype(f32)

    def body(i, _):
        await_projection((w0, w1, w2, w3), held, sems, i)
        for kind, out in ((0, q_out), (1, k_out)):
            out[i] = (dot(tokens[...], held[i, kind * GROUP : kind * GROUP + GROUP], NT) * valid).astype(bf16)
        wv = held[i, 2 * GROUP : 3 * GROUP]
        v_out[i, HALO : HALO + count] = (dot(tokens[...], wv, NT) * valid).astype(bf16)
        v_out[i, 0:HALO] = (dot(before[...], wv, NT) * valid_before).astype(bf16)
        v_out[i, HALO + count : 2 * HALO + count] = (dot(after[...], wv, NT) * valid_after).astype(bf16)
        v_out[i, 2 * HALO + count :] = jnp.zeros((v_out.shape[1] - 2 * HALO - count, GROUP), bf16)
        return 0

    lax.fori_loop(0, 4, body, 0)


def third_scores(info, lm, k_ref, i):
    count = k_ref.shape[1]
    valid = info[1] + iota((1, count), 1) < info[0]
    queries = spread(lm[i, :, 0:GROUP])
    return jnp.where(valid, mm_left(queries, k_ref[i], NT) * 0.125, -1e30)


def third_kernel(info, lm, k_ref, v_ref, pay):
    count = k_ref.shape[1]
    lane = iota((64, GROUP), 1)

    def body(i, _):
        scores = third_scores(info, lm, k_ref, i)
        top = jnp.max(scores, axis=1, keepdims=True)
        raised = jnp.exp(scores - top)
        total = jnp.sum(raised, axis=1, keepdims=True)
        packed = fold(mm_left(raised, v_ref[i, HALO : HALO + count]))
        for head in range(3):
            packed = jnp.where(lane == 192 + head, top[head * 64 : head * 64 + 64], packed)
            packed = jnp.where(lane == 196 + head, total[head * 64 : head * 64 + 64], packed)
        pay[i] = packed
        return 0

    lax.fori_loop(0, 4, body, 0)


def first_scores(lm, q_ref, i):
    keys = spread(lm[i, :, GROUP : 2 * GROUP])
    count = q_ref.shape[1]
    scores = (mm_left(keys, q_ref[i], NT) * 0.125).reshape(4, 64, count)
    raised = jnp.exp(scores - jnp.max(scores, axis=1, keepdims=True))
    return raised / jnp.sum(raised, axis=1, keepdims=True)


def toeplitz(row):
    return pltpu.roll(jnp.broadcast_to(row, (128, GROUP)), 0, 1, stride=1, stride_axis=0)


def head_select(x, rows):
    lane = iota((rows, GROUP), 1) >> 6
    out = jnp.where(lane == 0, x[0:rows], 0.0)
    out = jnp.where(lane == 1, x[rows : 2 * rows], out)
    return jnp.where(lane == 2, x[2 * rows : 3 * rows], out)


def context_kernel(p0, p1, p2, p3, lm, q_ref, v_ref, small, ctx, wst, x_out):
    count = q_ref.shape[1]
    lane = iota((64, GROUP), 1)

    def body(i, _):
        parts = [p0[i], p1[i ^ 1], p2[i ^ 2], p3[i ^ 3]]
        factors = [jnp.zeros((64, GROUP), f32) for _ in range(4)]
        stats = jnp.zeros((64, GROUP), f32)
        for head in range(3):
            tops = [part[:, 192 + head : 193 + head] for part in parts]
            top = jnp.maximum(jnp.maximum(tops[0], tops[1]), jnp.maximum(tops[2], tops[3]))
            scales = [jnp.exp(t - top) for t in tops]
            total = sum(part[:, 196 + head : 197 + head] * s for part, s in zip(parts, scales))
            mine = (lane >> 6) == head
            factors = [jnp.where(mine, s / total, f) for s, f in zip(scales, factors)]
            stats = jnp.where(lane == 192 + head, top, stats)
            stats = jnp.where(lane == 196 + head, total, stats)
        weight = sum(part * f for part, f in zip(parts, factors))
        wst[i] = jnp.where(lane < 192, weight, stats)
        mixed = mm(spread(lm[i, :, 2 * GROUP : 3 * GROUP]), spread(weight))
        x_out[i] = fold(mixed)
        first = first_scores(lm, q_ref, i).reshape(GROUP, count)
        main = mm(first, mixed, TN)
        bands = [toeplitz(small[i, 1 + head : 2 + head, 0:GROUP]) for head in range(3)]
        high, low = split(jnp.concatenate(bands, axis=0))
        for block in range(count // 128):
            window = v_ref[i, block * 128 : block * 128 + 256]
            conv = dot(high, window) + dot(low, window)
            ctx[i, block * 128 : block * 128 + 128] = (
                main[block * 128 : block * 128 + 128] + head_select(conv, 128)
            ).astype(bf16)
        return 0

    lax.fori_loop(0, 4, body, 0)


def first_back_kernel(
    g_ref, before, after, o0, o1, o2, o3, lm, q_ref, v_ref, small, x_in, dx, dq, dkl, dv, dtaps, held, sems, ext, dctx
):
    count = g_ref.shape[0]
    width = g_ref.shape[1]
    weights = (o0, o1, o2, o3)
    for i in range(4):
        pltpu.make_async_copy(weights[i], held.at[i, pl.ds(0, 192)], sems.at[i]).start()
        held[i, 192:256, :] = jnp.zeros((64, width), bf16)
    ext[0:HALO] = before[...]
    ext[HALO : HALO + count] = g_ref[...]
    ext[HALO + count : 2 * HALO + count] = after[...]
    ext[2 * HALO + count :] = jnp.zeros((ext.shape[0] - 2 * HALO - count, width), bf16)
    lane = iota((128, GROUP), 1) >> 6
    flip = (iota((128, 128), 0) + iota((128, 128), 1) == 127).astype(bf16)

    def body(i, _):
        pltpu.make_async_copy(weights[0], held.at[i, pl.ds(0, 192)], sems.at[i]).wait()
        dctx[...] = dot(ext[...], held[i], NT)
        own = dctx[HALO : HALO + count]
        own_high, own_low = split(own)
        first = first_scores(lm, q_ref, i)
        flat = first.reshape(GROUP, count)
        flat_high, flat_low = split(flat)
        dx[i] = fold(dot(flat_high, own_high) + (dot(flat_high, own_low) + dot(flat_low, own_high)))
        x_high, x_low = split(spread(x_in[i]))
        dfirst = dot(x_high, own_high, NT) + (dot(x_high, own_low, NT) + dot(x_low, own_high, NT))
        dfirst = dfirst.reshape(4, 64, count)
        ds = first * (dfirst - jnp.sum(first * dfirst, axis=1, keepdims=True)) * 0.125
        ds_high, ds_low = split(ds.reshape(GROUP, count))
        keys_high, keys_low = split(spread(lm[i, :, GROUP : 2 * GROUP]))
        dq[i] = dot(ds_high, keys_high, TN) + (dot(ds_high, keys_low, TN) + dot(ds_low, keys_high, TN))
        dkl[i] = fold(dot(ds_high, q_ref[i]) + dot(ds_low, q_ref[i]))
        bands = [toeplitz(small[i, 4 + head : 5 + head, 0:GROUP]) for head in range(3)]
        high, low = split(jnp.concatenate(bands, axis=0))
        gram = jnp.zeros((384, GROUP), f32)
        for block in range(count // 128):
            window_high, window_low = split(dctx[block * 128 : block * 128 + 256])
            conv = dot(high, window_high) + (dot(high, window_low) + dot(low, window_high))
            dv[i, block * 128 : block * 128 + 128] = head_select(conv, 128)
            piece = dctx[HALO + block * 128 : HALO + block * 128 + 128]
            stacked = jnp.concatenate([jnp.where(lane == head, piece, 0.0) for head in range(3)], axis=0)
            gram = gram + mm_left(stacked, v_ref[i, block * 128 : block * 128 + 256], NT)
        dtaps[i] = jnp.zeros((8, GROUP), f32)
        for head in range(3):
            part_high, part_low = split(gram[head * 128 : head * 128 + 128])
            upturned = dot(flip, part_high) + dot(flip, part_low)
            straight = pltpu.roll(upturned, GROUP - 127, 1, stride=1, stride_axis=0)
            summed = jnp.sum(straight, axis=0, keepdims=True)
            dtaps[i, 1 + head : 2 + head, :] = jnp.where(iota((1, GROUP), 1) < TAPS, summed, 0.0)
        return 0

    lax.fori_loop(0, 4, body, 0)


def third_back_kernel(info, x0, x1, x2, x3, lm, wst, k_ref, v_ref, dvc, dk, dql, dv):
    count = k_ref.shape[1]
    valid = (rows_of(info, count, 0) < info[0]).astype(f32)
    none = jnp.zeros((64, 1), f32)

    def body(i, _):
        dx = spread(x0[i] + x1[i ^ 1] + x2[i ^ 2] + x3[i ^ 3])
        dweight = mm(spread(lm[i, :, 2 * GROUP : 3 * GROUP]), dx, TN)
        stats = wst[i]
        weight = spread(jnp.where(iota((64, GROUP), 1) < 192, stats, 0.0))
        inner = jnp.sum(dweight * weight, axis=1, keepdims=True)
        top = jnp.concatenate([stats[:, 192 + head : 193 + head] for head in range(3)] + [none], axis=0)
        total = jnp.concatenate([stats[:, 196 + head : 197 + head] for head in range(3)] + [none + 1.0], axis=0)
        scores = third_scores(info, lm, k_ref, i)
        third = jnp.exp(scores - top) / total
        dw_high, dw_low = split(dweight)
        values = v_ref[i, HALO : HALO + count]
        dthird = dot(dw_high, values, NT) + dot(dw_low, values, NT)
        ds_high, ds_low = split(third * (dthird - inner) * 0.125)
        queries_high, queries_low = split(spread(lm[i, :, 0:GROUP]))
        dk[i] = dot(ds_high, queries_high, TN) + (dot(ds_high, queries_low, TN) + dot(ds_low, queries_high, TN))
        dql[i] = fold(dot(ds_high, k_ref[i]) + dot(ds_low, k_ref[i]))
        third_high, third_low = split(third)
        dvalues = dot(third_high, dw_high, TN) + (dot(third_high, dw_low, TN) + dot(third_low, dw_high, TN))
        dv[i] = ((dvalues + dvc[i]) * valid).astype(bf16)
        return 0

    lax.fori_loop(0, 4, body, 0)


def joint_back_kernel(info, l0, l1, dq, dk, dv, out):
    count = dq.shape[1]
    mark = iota((1, 64), 1)
    low = (mark * info[0]) >> 6
    high = ((mark + 1) * info[0]) >> 6
    pos = rows_of(info, count, 0)
    member = ((pos >= low) & (pos < high)).astype(bf16)
    member = jnp.concatenate([member, member], axis=1)
    valid = (pos < info[0]).astype(f32)
    row = iota((64, 1), 0)
    width = ((((row + 1) * info[0]) >> 6) - ((row * info[0]) >> 6)).astype(f32)

    def body(i, _):
        pooled = (l0[i].astype(f32) + l1[i ^ 1].astype(f32)) / width
        pooled_high, pooled_low = split(pooled)
        spreads = dot(member, jnp.concatenate([pooled_high, pooled_low], axis=0))
        out[i, :, 0:GROUP] = (dq[i] * valid + spreads[:, 0:GROUP]).astype(bf16)
        out[i, :, GROUP : 2 * GROUP] = (dk[i] * valid + spreads[:, GROUP : 2 * GROUP]).astype(bf16)
        out[i, :, 2 * GROUP : 3 * GROUP] = dv[i]
        return 0

    lax.fori_loop(0, 4, body, 0)


def token_back_kernel(joint, dres, w0, w1, w2, w3, out, held, sems):
    fetch_projection((w0, w1, w2, w3), held, sems)
    out[...] = dres[...]

    def body(i, _):
        await_projection((w0, w1, w2, w3), held, sems, i)
        out[...] += dot(joint[i], held[i])
        return 0

    lax.fori_loop(0, 4, body, 0)


def fetch_all(weights, held, sems):
    for i in range(4):
        pltpu.make_async_copy(weights[i], held.at[i], sems.at[i]).start()


def await_one(weights, held, sems, i):
    pltpu.make_async_copy(weights[0], held.at[i], sems.at[i]).wait()


def moments(x):
    centered = x - jnp.mean(x, axis=-1, keepdims=True)
    variance = jnp.mean(centered * centered, axis=-1, keepdims=True)
    inverse = lax.rsqrt(variance + 1e-05)
    return centered * inverse, inverse


def attended_kernel(ctx, tokens, gain, shift, o0, o1, o2, o3, pre, normed, low, held, sems):
    width = tokens.shape[1]
    weights = (o0, o1, o2, o3)
    for i in range(4):
        pltpu.make_async_copy(weights[i], held.at[i, pl.ds(0, 192)], sems.at[i]).start()
        held[i, 192:256, :] = jnp.zeros((64, width), bf16)
    pre[...] = tokens[...].astype(f32)

    def body(i, _):
        pltpu.make_async_copy(weights[0], held.at[i, pl.ds(0, 192)], sems.at[i]).wait()
        pre[...] += dot(ctx[i], held[i])
        return 0

    lax.fori_loop(0, 4, body, 0)
    unit, _ = moments(pre[...])
    result = unit * gain[...] + shift[...]
    normed[...] = result
    low[...] = result.astype(bf16)


def gelu_parts(u):
    cdf = 0.5 + 0.5 * lax.erf(u * 0.7071067811865476)
    pdf = jnp.exp(u * u * -0.5) * 0.3989422804014327
    return u * cdf, cdf + u * pdf


def up_kernel(low, small, w0, w1, w2, w3, hidden, slope, held, sems):
    fetch_all((w0, w1, w2, w3), held, sems)

    def body(i, _):
        await_one((w0, w1, w2, w3), held, sems, i)
        for chunk in range(3):
            at = slice(chunk * 256, chunk * 256 + 256)
            upward = dot(low[...], held[i, :, at]) + small[i, 0:1, at]
            value, derivative = gelu_parts(upward)
            hidden[i, :, at] = value.astype(bf16)
            slope[i, :, at] = derivative.astype(bf16)
        return 0

    lax.fori_loop(0, 4, body, 0)


def norm_back(g, gain, unit, inverse):
    scaled = g * gain
    mean1 = jnp.mean(scaled, axis=-1, keepdims=True)
    mean2 = jnp.mean(scaled * unit, axis=-1, keepdims=True)
    return (scaled - mean1 - unit * mean2) * inverse


def down_kernel(hidden, normed, grad, gain, shift, w0, w1, w2, w3, out, dsum, dlow, sums, held, sems, acc):
    fetch_all((w0, w1, w2, w3), held, sems)
    acc[...] = normed[...]

    def body(i, _):
        await_one((w0, w1, w2, w3), held, sems, i)
        acc[...] += dot(hidden[i], held[i])
        return 0

    lax.fori_loop(0, 4, body, 0)
    unit, inverse = moments(acc[...])
    out[...] = (unit * gain[...] + shift[...]).astype(bf16)
    g = grad[...].astype(f32)
    back = norm_back(g, gain[...], unit, inverse)
    dsum[...] = back
    dlow[...] = back.astype(bf16)
    sums[...] = jnp.zeros_like(sums)
    sums[0:1] = jnp.sum(g * unit, axis=0, keepdims=True)
    sums[1:2] = jnp.sum(g, axis=0, keepdims=True)


def hidden_back_kernel(dlow, slope, w0, w1, w2, w3, du, sums, held, sems):
    fetch_all((w0, w1, w2, w3), held, sems)
    sums[...] = jnp.zeros_like(sums)

    def body(i, _):
        await_one((w0, w1, w2, w3), held, sems, i)
        for chunk in range(3):
            at = slice(chunk * 256, chunk * 256 + 256)
            back = dot(dlow[...], held[i, at, :], NT) * slope[i, :, at].astype(f32)
            back = back.astype(bf16)
            du[i, :, at] = back
            sums[i, 0:1, at] = jnp.sum(back.astype(f32), axis=0, keepdims=True)
        return 0

    lax.fori_loop(0, 4, body, 0)


def residual_back_kernel(du, dsum, pre, gain, w0, w1, w2, w3, dres, dlow, sums, held, sems, acc):
    fetch_all((w0, w1, w2, w3), held, sems)
    acc[...] = dsum[...]

    def body(i, _):
        await_one((w0, w1, w2, w3), held, sems, i)
        acc[...] += dot(du[i], held[i], NT)
        return 0

    lax.fori_loop(0, 4, body, 0)
    unit, inverse = moments(pre[...])
    g = acc[...]
    back = norm_back(g, gain[...], unit, inverse)
    dres[...] = back
    dlow[...] = back.astype(bf16)
    sums[...] = jnp.zeros_like(sums)
    sums[0:1] = jnp.sum(g * unit, axis=0, keepdims=True)
    sums[1:2] = jnp.sum(g, axis=0, keepdims=True)


def weight_grad_kernel(rows, left_a, left_b, right_a, right_b, out):
    left_a, left_b = left_a[...].reshape(left_a.shape[-2:]), left_b[...].reshape(left_b.shape[-2:])
    right_a, right_b = right_a[...].reshape(right_a.shape[-2:]), right_b[...].reshape(right_b.shape[-2:])
    total = dot(left_a, right_a, TN) + dot(left_b, right_b, TN)
    out[0] = total[0:rows].astype(bf16)


def weight_grad(left_a, left_b, right_a, right_b, chunk, rows, name):
    count = left_a.shape[-2]
    many = left_a.ndim == 3
    width = left_a.shape[-1]
    right_width = right_a.shape[-1]
    steps = width // chunk
    if many:
        left_spec = pl.BlockSpec((1, count, chunk), lambda j, c: (j, 0, c))
        right_spec = pl.BlockSpec((count, right_width), lambda j, c: (0, 0))
    else:
        left_spec = pl.BlockSpec((count, chunk), lambda j, c: (0, c))
        right_spec = pl.BlockSpec((1, count, right_width), lambda j, c: (j, 0, 0))
    return pl.pallas_call(
        functools.partial(weight_grad_kernel, rows),
        grid=(2, steps),
        out_shape=jax.ShapeDtypeStruct((2, steps * rows, right_width), bf16),
        in_specs=[left_spec, left_spec, right_spec, right_spec],
        out_specs=pl.BlockSpec((1, rows, right_width), lambda j, c: (j, c, 0)),
        compiler_params=pltpu.CompilerParams(vmem_limit_bytes=40 << 20),
        cost_estimate=pl.CostEstimate(
            flops=2 * 2 * 2 * count * width * right_width, bytes_accessed=12 << 20, transcendentals=0
        ),
        name=name,
    )(left_a, left_b, right_a, right_b)


HOP = {1: 2, 2: 1, 3: 3}


def hop(x, step):
    return lax.ppermute(x, "head", [(i, i ^ HOP[step]) for i in range(4)])


def gather(x):
    across = hop(x, 1)
    return [x, across, hop(x, 2), hop(across, 2)]


def batch_total(x, count):
    step = 1
    while step < count:
        x = x + lax.ppermute(x, "batch", [(i, i ^ step) for i in range(count)])
        step *= 2
    return x


def batch_total_large(x, count):
    rows = x.shape[0]
    pieces = lax.all_to_all(x, "batch", split_axis=0, concat_axis=0, tiled=True)
    piece = jnp.sum(pieces.reshape(count, rows // count, x.shape[1]).astype(f32), axis=0).astype(bf16)
    return lax.all_gather(piece, "batch", axis=0, tiled=True)


def neighbours(x):
    before = lax.ppermute(x[-HALO:], "head", [(i, i + 1) for i in range(3)])
    after = lax.ppermute(x[:HALO], "head", [(i + 1, i) for i in range(3)])
    return before, after


def local(
    batch_count,
    tokens,
    lengths,
    w_query,
    w_key,
    w_value,
    w_out,
    conv_taps,
    w_up,
    b_up,
    w_down,
    gain_attn,
    shift_attn,
    gain_ffn,
    shift_ffn,
    grad_out,
):
    tokens = tokens[0]
    grad_out = grad_out[0]
    count, width = tokens.shape
    ext = count + 128
    length = lengths[0]
    info = jnp.stack([length, lax.axis_index("head") * count]).astype(jnp.int32)
    gain_attn, shift_attn, gain_ffn, shift_ffn = (
        x.reshape(1, width) for x in (gain_attn, shift_attn, gain_ffn, shift_ffn)
    )

    marks = jnp.arange(LANDMARKS + 1, dtype=jnp.int32) * length // LANDMARKS
    positions = info[1] + jnp.arange(count, dtype=jnp.int32)
    member = (positions[None, :] >= marks[:-1, None]) & (positions[None, :] < marks[1:, None])
    pooled = jnp.dot(member.astype(bf16), tokens, preferred_element_type=f32)
    pooled = pooled / (marks[1:] - marks[:-1]).astype(f32)[:, None]
    pools = [pooled, hop(pooled, 1), hop(pooled, 2), hop(pooled, 3)]

    wt_own = jnp.concatenate([w_query.T, w_key.T, w_value.T], axis=0)
    taps = jnp.pad(conv_taps, ((0, 0), (0, width - TAPS)))
    taps_back = jnp.pad(conv_taps[:, ::-1], ((0, 0), (0, width - TAPS)))
    small_own = jnp.concatenate([b_up[None], taps, taps_back, jnp.zeros((1, width), f32)], axis=0)
    before, after = neighbours(tokens)
    wt = gather(wt_own)
    small = jnp.stack(gather(small_own))
    wo = gather(w_out)
    wu = gather(w_up)
    wd = gather(w_down)
    tokens_other = hop(tokens, 2)

    vm, an = VMEM, ANY
    lm_own, chain = call(
        landmark_kernel,
        [((64, 3 * GROUP), f32), ((NEWTON, 4, 3, 64, 64), f32)],
        [(vm, p) for p in pools] + [(vm, wt_own)],
        flops=int(1e9),
        size=4 << 20,
        name="landmarks",
    )
    lm = jnp.stack(gather(lm_own))
    q, k, v = call(
        project_kernel,
        [((4, count, GROUP), bf16), ((4, count, GROUP), bf16), ((4, ext, GROUP), bf16)],
        [(vm, info), (vm, tokens), (vm, before), (vm, after)] + [(an, w) for w in wt],
        [pltpu.VMEM((4, 3 * GROUP, width), bf16), pltpu.SemaphoreType.DMA((4, 3))],
        flops=2 * count * width * 3072,
        size=8 << 20,
        smem=(0,),
        name="project",
    )
    (pay,) = call(
        third_kernel,
        [((4, 64, GROUP), f32)],
        [(vm, info), (vm, lm), (vm, k), (vm, v)],
        flops=int(1e9),
        size=3 << 20,
        smem=(0,),
        name="third",
    )
    pays = [pay, hop(pay, 1), hop(pay, 2), hop(pay, 3)]
    ctx, wst, x_mid = call(
        context_kernel,
        [((4, count, GROUP), bf16), ((4, 64, GROUP), f32), ((4, 64, GROUP), f32)],
        [(vm, p) for p in pays] + [(vm, lm), (vm, q), (vm, v), (vm, small)],
        flops=int(3e9),
        size=5 << 20,
        name="context",
    )
    out_scratch = [pltpu.VMEM((4, GROUP, width), bf16), pltpu.SemaphoreType.DMA((4,))]
    wide = [pltpu.VMEM((4, width, width), bf16), pltpu.SemaphoreType.DMA((4,))]
    acc = [pltpu.VMEM((count, width), f32)]
    pre, normed, normed_low = call(
        attended_kernel,
        [((count, width), f32), ((count, width), f32), ((count, width), bf16)],
        [(vm, ctx), (vm, tokens), (vm, gain_attn), (vm, shift_attn)] + [(an, w) for w in wo],
        out_scratch,
        flops=2 * count * width * width,
        size=6 << 20,
        name="attended",
    )
    normed_other = hop(normed_low, 2)
    hidden, slope = call(
        up_kernel,
        [((4, count, width), bf16), ((4, count, width), bf16)],
        [(vm, normed_low), (vm, small)] + [(an, w) for w in wu],
        wide,
        flops=2 * count * width * 3072,
        size=12 << 20,
        name="up",
    )
    hidden_keep, hidden_send = hidden[0:2], hidden[2:4]
    hidden_other = hop(hidden_send, 2)
    output, d_sum, gd, sums_ffn = call(
        down_kernel,
        [((count, width), bf16), ((count, width), f32), ((count, width), bf16), ((8, width), f32)],
        [(vm, hidden), (vm, normed), (vm, grad_out), (vm, gain_ffn), (vm, shift_ffn)] + [(an, w) for w in wd],
        wide + acc,
        flops=2 * count * width * 3072,
        size=14 << 20,
        name="down",
    )
    gd_other = hop(gd, 2)
    du, sums_up = call(
        hidden_back_kernel,
        [((4, count, width), bf16), ((4, 8, width), f32)],
        [(vm, gd), (vm, slope)] + [(an, w) for w in wd],
        wide,
        flops=2 * count * width * 3072,
        size=12 << 20,
        name="hidden_back",
    )
    du_other = hop(du[2:4], 2)
    g_down = weight_grad(hidden_keep, hidden_other, gd, gd_other, 256, 256, "grad_down")
    d_res, ga, sums_attn = call(
        residual_back_kernel,
        [((count, width), f32), ((count, width), bf16), ((8, width), f32)],
        [(vm, du), (vm, d_sum), (vm, pre), (vm, gain_attn)] + [(an, w) for w in wu],
        wide + acc,
        flops=2 * count * width * 3072,
        size=14 << 20,
        name="residual_back",
    )
    ga_other = hop(ga, 2)
    ga_before, ga_after = neighbours(ga)
    g_up = weight_grad(normed_low, normed_other, du[0:2], du_other, 256, 256, "grad_up")
    dx, dq, dkl, dv_conv, dtaps = call(
        first_back_kernel,
        [
            ((4, 64, GROUP), f32),
            ((4, count, GROUP), f32),
            ((4, 64, GROUP), f32),
            ((4, count, GROUP), f32),
            ((4, 8, GROUP), f32),
        ],
        [(vm, ga), (vm, ga_before), (vm, ga_after)]
        + [(an, w) for w in wo]
        + [(vm, lm), (vm, q), (vm, v), (vm, small), (vm, x_mid)],
        out_scratch + [pltpu.VMEM((ext, width), bf16), pltpu.VMEM((ext, GROUP), f32)],
        flops=int(5e9),
        size=10 << 20,
        name="first_back",
    )
    dxs = [dx, hop(dx, 1), hop(dx, 2), hop(dx, 3)]
    g_out = weight_grad(ctx[0:2], hop(ctx[2:4], 2), ga, ga_other, GROUP, 192, "grad_out")
    dk, dql, dv = call(
        third_back_kernel,
        [((4, count, GROUP), f32), ((4, 64, GROUP), f32), ((4, count, GROUP), bf16)],
        [(vm, info)] + [(vm, d) for d in dxs] + [(vm, lm), (vm, wst), (vm, k), (vm, v), (vm, dv_conv)],
        flops=int(5e9),
        size=8 << 20,
        smem=(0,),
        name="third_back",
    )
    (own_back,) = call(
        inverse_back_kernel,
        [((64, 2 * GROUP), f32)],
        [(vm, d[i]) for i, d in enumerate(dxs)] + [(vm, wst[0]), (vm, lm_own), (vm, chain)],
        flops=int(1e9),
        size=4 << 20,
        name="inverse_back",
    )
    landmark_back = jnp.concatenate([dql, dkl], axis=2)
    landmark_back = landmark_back.at[0].add(own_back)
    other = hop(landmark_back, 2)
    paired = (landmark_back + jnp.concatenate([other[2:4], other[0:2]], axis=0)).astype(bf16)
    across = hop(paired, 1)
    (joint,) = call(
        joint_back_kernel,
        [((4, count, 3 * GROUP), bf16)],
        [(vm, info), (vm, paired), (vm, across), (vm, dq), (vm, dk), (vm, dv)],
        flops=int(1e9),
        size=8 << 20,
        smem=(0,),
        name="joint_back",
    )
    joint_other = hop(joint[2:4], 2)
    (d_tokens,) = call(
        token_back_kernel,
        [((count, width), f32)],
        [(vm, joint), (vm, d_res)] + [(an, w) for w in wt],
        [pltpu.VMEM((4, 3 * GROUP, width), bf16), pltpu.SemaphoreType.DMA((4, 3))],
        flops=2 * count * width * 3072,
        size=10 << 20,
        name="token_back",
    )
    g_joint = weight_grad(joint[0:2], joint_other, tokens, tokens_other, GROUP, 192, "grad_joint")

    def reduce_grad(g):
        own = (g[0].astype(f32) + hop(g[1], 1).astype(f32)).astype(bf16)
        return batch_total_large(own, batch_count)

    d_w_down = reduce_grad(g_down).astype(f32)
    d_w_up = reduce_grad(g_up).astype(f32)
    d_w_out = reduce_grad(g_out).astype(f32)
    d_joint = reduce_grad(g_joint).astype(f32)
    heads = width // 4
    d_w_query, d_w_key, d_w_value = (d_joint[i * heads : (i + 1) * heads].T for i in range(3))

    norms = jnp.concatenate([sums_attn[0:2], sums_ffn[0:2]], axis=0)
    dtaps = jnp.pad(dtaps[:, 1:4], ((0, 0), (0, 0), (0, width - GROUP)))
    minor = jnp.concatenate([sums_up[:, 0:1], dtaps, jnp.broadcast_to(norms, (4, 4, width))], axis=1)
    minor = minor[0] + hop(minor[1], 1) + hop(minor[2], 2) + hop(minor[3], 3)
    minor = batch_total(minor, batch_count)
    return (
        output[None],
        d_tokens[None],
        d_w_query,
        d_w_key,
        d_w_value,
        d_w_out,
        minor[1:4, 0:TAPS],
        d_w_up,
        minor[0],
        d_w_down,
        minor[4],
        minor[5],
        minor[6],
        minor[7],
    )


def solution(mesh):
    return jax.shard_map(
        functools.partial(local, mesh.shape["batch"]),
        mesh=mesh,
        in_specs=(
            P("batch", "head", None),
            P("batch"),
            P(None, "head"),
            P(None, "head"),
            P(None, "head"),
            P("head", None),
            P("head", None),
            P(None, "head"),
            P("head"),
            P("head", None),
            P(),
            P(),
            P(),
            P(),
            P("batch", "head", None),
        ),
        out_specs=(
            P("batch", "head", None),
            P("batch", "head", None),
            P(None, "head"),
            P(None, "head"),
            P(None, "head"),
            P("head", None),
            P("head", None),
            P(None, "head"),
            P("head"),
            P("head", None),
            P(),
            P(),
            P(),
            P(),
        ),
        check_vma=False,
    )
```

```python
import functools

import jax
import jax.numpy as jnp
from jax import lax
from jax.experimental import pallas as pl
from jax.experimental.pallas import tpu as pltpu
from jax.sharding import PartitionSpec as P

f32 = jnp.float32
bf16 = jnp.bfloat16
HEAD_DIM = 64
LANDMARKS = 64
NEWTON = 6
TAPS = 65
HALO = TAPS // 2
EARLY = 1
LATE = 0
GROUP = 256
NN = ((1,), (0,))
NT = ((1,), (1,))
TN = ((0,), (0,))
VMEM = pltpu.VMEM
ANY = pl.ANY


def dot(a, b, dims=NN):
    return lax.dot_general(a, b, (dims, ((), ())), preferred_element_type=f32)


def split(x):
    high = x.astype(bf16)
    return high, (x - high.astype(f32)).astype(bf16)


def mm(a, b, dims=NN):
    a_high, a_low = split(a)
    b_high, b_low = split(b)
    return dot(a_high, b_high, dims) + (dot(a_high, b_low, dims) + dot(a_low, b_high, dims))


def mm_left(a, b, dims=NN):
    a_high, a_low = split(a)
    return dot(a_high, b, dims) + dot(a_low, b, dims)


def iota(shape, dim):
    return lax.broadcasted_iota(jnp.int32, shape, dim)


def call(body, outs, ins, scratch=(), flops=0, size=0, limit=40, name=None, smem=()):
    specs = [
        pl.BlockSpec(memory_space=pltpu.SMEM) if i in smem else pl.BlockSpec(memory_space=space)
        for i, (space, _) in enumerate(ins)
    ]
    return pl.pallas_call(
        body,
        out_shape=[jax.ShapeDtypeStruct(s, d) for s, d in outs],
        in_specs=specs,
        out_specs=[pl.BlockSpec(memory_space=VMEM)] * len(outs),
        scratch_shapes=list(scratch),
        compiler_params=pltpu.CompilerParams(vmem_limit_bytes=limit << 20),
        cost_estimate=pl.CostEstimate(flops=flops, bytes_accessed=size, transcendentals=0),
        name=name,
    )(*[value for _, value in ins])


def call_many(parts, name):
    ins = [value for part in parts for value in part[2]]
    outs = [value for part in parts for value in part[1]]
    scratch = [value for part in parts for value in part[3]]
    smem, first = [], 0
    for part in parts:
        smem += [first + i for i in part[4]]
        first += len(part[2])

    def body(*refs):
        groups = [refs[: len(ins)], refs[len(ins) : len(ins) + len(outs)], refs[len(ins) + len(outs) :]]
        at = [0, 0, 0]
        for part in parts:
            mine = []
            for group, kind in ((0, 2), (1, 1), (2, 3)):
                mine += groups[group][at[group] : at[group] + len(part[kind])]
                at[group] += len(part[kind])
            part[0](*mine)

    results = call(body, outs, ins, scratch, flops=int(5e9), size=10 << 20, name=name, smem=tuple(smem), limit=48)
    split_results, first = [], 0
    for part in parts:
        split_results.append(results[first : first + len(part[1])])
        first += len(part[1])
    return split_results


def block_mask():
    return (iota((GROUP, GROUP), 0) >> 6) == (iota((GROUP, GROUP), 1) >> 6)


def spread(x):
    return jnp.where(block_mask(), jnp.concatenate([x, x, x, x], axis=0), 0.0)


def fold(x):
    kept = jnp.where(block_mask(), x, 0.0)
    return kept[0:64] + kept[64:128] + kept[128:192]


def rows_of(info, count, first):
    return info[1] + first + iota((count, 1), 0)


def landmark_kernel(p0, p1, wt, lm, chain):
    pooled = p0[...] + p1[...]
    high, low = split(pooled)
    both = jnp.concatenate([high, low], axis=0)
    lm[...] = jnp.zeros_like(lm)
    matrices, starts = [], []
    for head in range(3):
        pair = []
        for kind in range(2):
            rows = wt[kind * 192 + head * 64 : kind * 192 + head * 64 + 64]
            out = dot(both, rows, NT)
            out = out[0:64] + out[64:128]
            lm[:, kind * GROUP + head * 64 : kind * GROUP + head * 64 + 64] = out
            pair.append(out)
        scores = mm(pair[0], pair[1], NT) * 0.125
        raised = jnp.exp(scores - jnp.max(scores, axis=1, keepdims=True))
        matrix = raised / jnp.sum(raised, axis=1, keepdims=True)
        column = jnp.max(jnp.sum(matrix, axis=0, keepdims=True), axis=1, keepdims=True)
        row = jnp.max(jnp.sum(matrix, axis=1, keepdims=True), axis=0, keepdims=True)
        matrices.append(matrix)
        starts.append(matrix.T / (column * row))
    eye = (iota((64, 64), 0) == iota((64, 64), 1)).astype(f32)

    def step(it, iterates):
        results = []
        for head in range(3):
            z = iterates[head]
            product = mm(matrices[head], z)
            inner1 = 7.0 * eye - product
            inner2 = 15.0 * eye - mm(product, inner1)
            inner3 = 13.0 * eye - mm(product, inner2)
            chain[it, 0, head] = z
            chain[it, 1, head] = product
            chain[it, 2, head] = inner2
            chain[it, 3, head] = inner3
            results.append(0.25 * mm(z, inner3))
        return tuple(results)

    finals = lax.fori_loop(0, NEWTON, step, tuple(starts))
    for head in range(3):
        lm[:, 2 * GROUP + head * 64 : 2 * GROUP + head * 64 + 64] = finals[head]


def inverse_back_kernel(x0, x1, wst_all, lm, chain, partial, out):
    total = x0[0] + x1[1]
    eye = (iota((64, 64), 0) == iota((64, 64), 1)).astype(f32)
    weight = wst_all[0]
    out[...] = partial[...].astype(bf16)
    grads, matrices, queries, keys = [], [], [], []
    for head in range(3):
        at = slice(head * 64, head * 64 + 64)
        grads.append(mm(total[:, at], weight[:, at], NT))
        query = lm[:, head * 64 : head * 64 + 64]
        key = lm[:, GROUP + head * 64 : GROUP + head * 64 + 64]
        scores = mm(query, key, NT) * 0.125
        raised = jnp.exp(scores - jnp.max(scores, axis=1, keepdims=True))
        matrices.append(raised / jnp.sum(raised, axis=1, keepdims=True))
        queries.append(query)
        keys.append(key)

    def step(count, carried):
        it = NEWTON - 1 - count
        results = []
        for head in range(3):
            dz_next, da = carried[2 * head], carried[2 * head + 1]
            z = chain[it, 0, head]
            product = chain[it, 1, head]
            inner1 = 7.0 * eye - product
            inner2 = chain[it, 2, head]
            inner3 = chain[it, 3, head]
            dz_next = 0.25 * dz_next
            dz = mm(dz_next, inner3, NT)
            d3 = -mm(z, dz_next, TN)
            d2 = -mm(product, d3, TN)
            d1 = mm(product, d2, TN)
            dp = mm(d3, inner2, NT) + mm(d2, inner1, NT) - d1
            da = da + mm(dp, z, NT)
            dz = dz + mm(matrices[head], dp, TN)
            results += [dz, da]
        return tuple(results)

    first = []
    for head in range(3):
        first += [grads[head], jnp.zeros((64, 64), f32)]
    last = lax.fori_loop(0, NEWTON, step, tuple(first))
    for head in range(3):
        dz, da = last[2 * head], last[2 * head + 1]
        matrix = matrices[head]
        columns = jnp.sum(matrix, axis=0, keepdims=True)
        rows = jnp.sum(matrix, axis=1, keepdims=True)
        column = jnp.max(columns, axis=1, keepdims=True)
        row = jnp.max(rows, axis=0, keepdims=True)
        scale = 1.0 / (column * row)
        da = da + dz.T * scale
        d_scale = -jnp.sum(jnp.sum(dz * matrix.T, axis=1, keepdims=True), axis=0, keepdims=True) * scale * scale
        column_hit = (columns == column).astype(f32)
        row_hit = (rows == row).astype(f32)
        da = da + d_scale * row * column_hit / jnp.sum(column_hit, axis=1, keepdims=True)
        da = da + d_scale * column * row_hit / jnp.sum(row_hit, axis=0, keepdims=True)
        ds = matrix * (da - jnp.sum(da * matrix, axis=1, keepdims=True)) * 0.125
        for at, value in ((head * 64, mm(ds, keys[head])), (GROUP + head * 64, mm(ds, queries[head], TN))):
            out[0, :, at : at + 64] = (partial[0, :, at : at + 64] + value).astype(bf16)


PROJECTION = ((0, 192, 0), (192, 192, GROUP), (384, 192, 2 * GROUP))


def split_copies(refs, parts, held, sems, side):
    own, across, across_x, other, both, both_x = refs
    half = own.shape[1] // 2
    mine = pl.ds(pl.multiple_of(side * half, half), half)
    rest = pl.ds(pl.multiple_of((1 - side) * half, half), half)
    blocks = [[], [], [], []]
    for n, (row, rows, to) in enumerate(parts):
        first = pl.ds(row - parts[0][0], rows)
        source, to = pl.ds(row, rows), pl.ds(to, rows)
        blocks[0].append(pltpu.make_async_copy(own.at[first], held.at[0, to], sems.at[0, n, 0]))
        blocks[2].append(pltpu.make_async_copy(other.at[source], held.at[2, to], sems.at[2, n, 0]))
        for i, near, far in ((1, across, across_x), (3, both, both_x)):
            blocks[i].append(pltpu.make_async_copy(near.at[source], held.at[i, to, mine], sems.at[i, n, 0]))
            blocks[i].append(pltpu.make_async_copy(far.at[source], held.at[i, to, rest], sems.at[i, n, 1]))
    return blocks


def start(copies):
    for block in copies:
        for copy in block:
            copy.start()


def wait(copies, i):
    for block in range(4):

        @pl.when(i == block)
        def _():
            for copy in copies[block]:
                copy.wait()


def zero_gaps(held, kinds):
    for i in range(4):
        for kind in range(kinds):
            held[i, kind * GROUP + 192 : kind * GROUP + 256, :] = jnp.zeros((64, held.shape[2]), bf16)


def project_kernel(info, tokens, before, after, w0, w1, w2, w3, w4, w5, q_out, k_out, v_out, held, sems):
    count = tokens.shape[0]
    copies = split_copies((w0, w1, w2, w3, w4, w5), PROJECTION, held, sems, info[2])
    start(copies)
    zero_gaps(held, 3)
    valid = (rows_of(info, count, 0) < info[0]).astype(f32)
    valid_before = (rows_of(info, HALO, -HALO) < info[0]).astype(f32)
    valid_after = (rows_of(info, HALO, count) < info[0]).astype(f32)

    def body(i, _):
        wait(copies, i)
        for kind, out in ((0, q_out), (1, k_out)):
            out[i] = (dot(tokens[...], held[i, kind * GROUP : kind * GROUP + GROUP], NT) * valid).astype(bf16)
        wv = held[i, 2 * GROUP : 3 * GROUP]
        v_out[i, HALO : HALO + count] = (dot(tokens[...], wv, NT) * valid).astype(bf16)
        v_out[i, 0:HALO] = (dot(before[...], wv, NT) * valid_before).astype(bf16)
        v_out[i, HALO + count : 2 * HALO + count] = (dot(after[...], wv, NT) * valid_after).astype(bf16)
        v_out[i, 2 * HALO + count :] = jnp.zeros((v_out.shape[1] - 2 * HALO - count, GROUP), bf16)
        return 0

    lax.fori_loop(0, 4, body, 0)


def third_scores(info, lm, k_ref, i):
    count = k_ref.shape[1]
    valid = info[1] + iota((1, count), 1) < info[0]
    queries = spread(lm[i, :, 0:GROUP])
    return jnp.where(valid, mm_left(queries, k_ref[i], NT) * 0.125, -1e30)


def third_kernel(info, lm, k_ref, v_ref, pay):
    count = k_ref.shape[1]
    lane = iota((64, GROUP), 1)

    def body(i, _):
        scores = third_scores(info, lm, k_ref, i)
        top = jnp.max(scores, axis=1, keepdims=True)
        raised = jnp.exp(scores - top)
        total = jnp.sum(raised, axis=1, keepdims=True)
        packed = fold(mm_left(raised, v_ref[i, HALO : HALO + count]) / total)
        for stat, base in ((top, 192), (total, 216)):
            for term in range(3):
                part = stat.astype(bf16).astype(f32)
                stat = stat - part
                for head in range(3):
                    packed = jnp.where(lane == base + 8 * term + head, part[head * 64 : head * 64 + 64], packed)
        pay[i] = packed.astype(bf16)
        return 0

    lax.fori_loop(0, 4, body, 0)


def first_scores(lm, q_ref, i):
    keys = spread(lm[i, :, GROUP : 2 * GROUP])
    count = q_ref.shape[1]
    scores = (mm_left(keys, q_ref[i], NT) * 0.125).reshape(4, 64, count)
    raised = jnp.exp(scores - jnp.max(scores, axis=1, keepdims=True))
    return raised / jnp.sum(raised, axis=1, keepdims=True)


def toeplitz(row):
    return pltpu.roll(jnp.broadcast_to(row, (128, GROUP)), 0, 1, stride=1, stride_axis=0)


def head_select(x, rows):
    lane = iota((rows, GROUP), 1) >> 6
    out = jnp.where(lane == 0, x[0:rows], 0.0)
    out = jnp.where(lane == 1, x[rows : 2 * rows], out)
    return jnp.where(lane == 2, x[2 * rows : 3 * rows], out)


def context_kernel(p0, p1, p2, p3, lm, q_ref, v_ref, small, ctx, wst, x_out):
    count = q_ref.shape[1]
    lane = iota((64, GROUP), 1)

    def body(i, _):
        parts = [p[i ^ n].astype(f32) for n, p in enumerate((p0, p1, p2, p3))]

        def stat(part, at):
            return part[:, at : at + 1] + part[:, at + 8 : at + 9] + part[:, at + 16 : at + 17]

        factors = [jnp.zeros((64, GROUP), f32) for _ in range(4)]
        stats = jnp.zeros((64, GROUP), f32)
        for head in range(3):
            tops = [stat(part, 192 + head) for part in parts]
            top = jnp.maximum(jnp.maximum(tops[0], tops[1]), jnp.maximum(tops[2], tops[3]))
            scales = [stat(part, 216 + head) * jnp.exp(t - top) for part, t in zip(parts, tops)]
            total = sum(scales)
            mine = (lane >> 6) == head
            factors = [jnp.where(mine, s / total, f) for s, f in zip(scales, factors)]
            stats = jnp.where(lane == 192 + head, top, stats)
            stats = jnp.where(lane == 196 + head, total, stats)
        weight = sum(part * f for part, f in zip(parts, factors))
        wst[i] = jnp.where(lane < 192, weight, stats)
        mixed = mm(spread(lm[i, :, 2 * GROUP : 3 * GROUP]), spread(weight))
        x_out[i] = fold(mixed)
        first = first_scores(lm, q_ref, i).reshape(GROUP, count)
        main = mm(first, mixed, TN)
        bands = [toeplitz(small[i, 1 + head : 2 + head, 0:GROUP]) for head in range(3)]
        high, low = split(jnp.concatenate(bands, axis=0))
        for block in range(count // 128):
            window = v_ref[i, block * 128 : block * 128 + 256]
            conv = dot(high, window) + dot(low, window)
            ctx[i, block * 128 : block * 128 + 128] = (
                main[block * 128 : block * 128 + 128] + head_select(conv, 128)
            ).astype(bf16)
        return 0

    lax.fori_loop(0, 4, body, 0)


def first_back_kernel(
    info, g_ref, before, after, o0, o1, o2, o3, o4, o5, lm, q_ref, v_ref, small, x_in, dx, dq, dkl, dv, dtaps, held, sems, ext, dctx
):
    count = g_ref.shape[0]
    width = g_ref.shape[1]
    copies = split_copies((o0, o1, o2, o3, o4, o5), ((0, 192, 0),), held, sems, info[2])
    start(copies)
    zero_gaps(held, 1)
    valid = (rows_of(info, count, 0) < info[0]).astype(f32)
    ext[0:HALO] = before[...]
    ext[HALO : HALO + count] = g_ref[...]
    ext[HALO + count : 2 * HALO + count] = after[...]
    ext[2 * HALO + count :] = jnp.zeros((ext.shape[0] - 2 * HALO - count, width), bf16)
    lane = iota((128, GROUP), 1) >> 6
    flip = (iota((128, 128), 0) + iota((128, 128), 1) == 127).astype(bf16)

    def body(i, _):
        wait(copies, i)
        dctx[...] = dot(ext[...], held[i], NT)
        own = dctx[HALO : HALO + count]
        own_high = own.astype(bf16)
        first = first_scores(lm, q_ref, i)
        flat = first.reshape(GROUP, count)
        dx[i] = fold(dot(flat.astype(bf16), own_high))
        dfirst = dot(spread(x_in[i]).astype(bf16), own_high, NT)
        dfirst = dfirst.reshape(4, 64, count)
        ds = first * (dfirst - jnp.sum(first * dfirst, axis=1, keepdims=True)) * 0.125
        ds = ds.reshape(GROUP, count).astype(bf16)
        keys = (spread(lm[i, :, GROUP : 2 * GROUP])).astype(bf16)
        dquery = dot(ds, keys, TN)
        dq[i] = (dquery * valid).astype(bf16)
        dkl[i] = fold(dot(ds, q_ref[i]))
        bands = [toeplitz(small[i, 4 + head : 5 + head, 0:GROUP]) for head in range(3)]
        high = jnp.concatenate(bands, axis=0).astype(bf16)
        gram = jnp.zeros((384, GROUP), f32)
        for block in range(count // 128):
            conv = dot(high, dctx[block * 128 : block * 128 + 256].astype(bf16))
            dv[i, block * 128 : block * 128 + 128] = head_select(conv, 128)
            piece = dctx[HALO + block * 128 : HALO + block * 128 + 128]
            stacked = jnp.concatenate([jnp.where(lane == head, piece, 0.0) for head in range(3)], axis=0)
            gram = gram + dot(stacked.astype(bf16), v_ref[i, block * 128 : block * 128 + 256], NT)
        dtaps[i] = jnp.zeros((8, GROUP), f32)
        for head in range(3):
            part_high, part_low = split(gram[head * 128 : head * 128 + 128])
            upturned = dot(flip, part_high) + dot(flip, part_low)
            straight = pltpu.roll(upturned, GROUP - 127, 1, stride=1, stride_axis=0)
            summed = jnp.sum(straight, axis=0, keepdims=True)
            dtaps[i, 1 + head : 2 + head, :] = jnp.where(iota((1, GROUP), 1) < TAPS, summed, 0.0)
        return 0

    lax.fori_loop(0, 4, body, 0)


def third_back_kernel(info, x0, x1, lm, wst, k_ref, v_ref, dvc, dq, dkl, ctx, joint, send, partial):
    count = k_ref.shape[1]
    valid = (rows_of(info, count, 0) < info[0]).astype(f32)
    none = jnp.zeros((64, 1), f32)

    def body(i, _):
        dx = spread(x0[i] + x1[i ^ 1])
        dweight = mm(spread(lm[i, :, 2 * GROUP : 3 * GROUP]), dx, TN)
        stats = wst[i]
        weight = spread(jnp.where(iota((64, GROUP), 1) < 192, stats, 0.0))
        inner = jnp.sum(dweight * weight, axis=1, keepdims=True)
        top = jnp.concatenate([stats[:, 192 + head : 193 + head] for head in range(3)] + [none], axis=0)
        total = jnp.concatenate([stats[:, 196 + head : 197 + head] for head in range(3)] + [none + 1.0], axis=0)
        scores = third_scores(info, lm, k_ref, i)
        third = jnp.exp(scores - top) / total
        dw_high = dweight.astype(bf16)
        values = v_ref[i, HALO : HALO + count]
        dthird = dot(dw_high, values, NT)
        ds = (third * (dthird - inner) * 0.125).astype(bf16)
        queries = (spread(lm[i, :, 0:GROUP])).astype(bf16)
        dkey = dot(ds, queries, TN)
        partial[i, :, 0:GROUP] = fold(dot(ds, k_ref[i]))
        partial[i, :, GROUP : 2 * GROUP] = dkl[i]
        dvalues = dot(third.astype(bf16), dw_high, TN)
        joint[i, :, 0:GROUP] = dq[i]
        joint[i, :, GROUP : 2 * GROUP] = (dkey * valid).astype(bf16)
        joint[i, :, 2 * GROUP : 3 * GROUP] = ((dvalues + dvc[i]) * valid).astype(bf16)

        @pl.when(i >= 2)
        def _():
            send[i - 2, :, 0 : 3 * GROUP] = joint[i]
            send[i - 2, :, 3 * GROUP : 4 * GROUP] = ctx[i]

        return 0

    lax.fori_loop(0, 4, body, 0)


def token_back_kernel(info, l0, l1, joint, dres, w0, w1, w2, w3, w4, w5, out, held, sems):
    copies = split_copies((w0, w1, w2, w3, w4, w5), PROJECTION, held, sems, info[2])
    start(copies)
    zero_gaps(held, 3)
    count = joint.shape[1]
    mark = iota((1, 64), 1)
    low = (mark * info[0]) >> 6
    high = ((mark + 1) * info[0]) >> 6
    pos = rows_of(info, count, 0)
    member = ((pos >= low) & (pos < high)).astype(bf16)
    row = iota((64, 1), 0)
    width = ((((row + 1) * info[0]) >> 6) - ((row * info[0]) >> 6)).astype(f32)
    out[...] = dres[...]

    def body(i, pooled):
        wait(copies, i)
        out[...] += dot(joint[i], held[i])
        marks = (l0[i].astype(f32) + l1[i ^ 1].astype(f32)) / width
        return pooled + mm_left(marks, held[i, 0 : 2 * GROUP])

    pooled = lax.fori_loop(0, 4, body, jnp.zeros((64, out.shape[1]), f32))
    pooled_high, pooled_low = split(pooled)
    out[...] += dot(member, pooled_high) + dot(member, pooled_low)


def moments(x):
    centered = x - jnp.mean(x, axis=-1, keepdims=True)
    variance = jnp.mean(centered * centered, axis=-1, keepdims=True)
    inverse = lax.rsqrt(variance + 1e-05)
    return centered * inverse, inverse


def attended_kernel(info, ctx, tokens, gain, shift, o0, o1, o2, o3, o4, o5, pre, normed, low, held, sems):
    copies = split_copies((o0, o1, o2, o3, o4, o5), ((0, 192, 0),), held, sems, info[2])
    start(copies)
    zero_gaps(held, 1)
    pre[...] = tokens[...].astype(f32)

    def body(i, _):
        wait(copies, i)
        pre[...] += dot(ctx[i], held[i])
        return 0

    lax.fori_loop(0, 4, body, 0)
    unit, _ = moments(pre[...])
    result = unit * gain[...] + shift[...]
    normed[...] = result
    low[...] = result.astype(bf16)


def gelu_parts(u):
    cdf = 0.5 + 0.5 * lax.erf(u * 0.7071067811865476)
    pdf = jnp.exp(u * u * -0.5) * 0.3989422804014327
    return u * cdf, cdf + u * pdf


def up_kernel(info, low, small, w0, w1, w2, w3, w4, w5, hidden, slope, send, held, sems):
    copies = split_copies((w0, w1, w2, w3, w4, w5), ((192, held.shape[1], 0),), held, sems, info[2])
    start(copies)

    def body(i, _):
        wait(copies, i)
        for chunk in range(3):
            at = slice(chunk * 256, chunk * 256 + 256)
            upward = dot(low[...], held[i, :, at]) + small[i, 0:1, at]
            value, derivative = gelu_parts(upward)
            hidden[i, :, at] = value.astype(bf16)
            slope[i, :, at] = derivative.astype(bf16)

        @pl.when(i >= 2)
        def _():
            send[i - 2] = hidden[i]

        return 0

    send[2] = low[...]
    lax.fori_loop(0, 4, body, 0)


def norm_back(g, gain, unit, inverse):
    scaled = g * gain
    mean1 = jnp.mean(scaled, axis=-1, keepdims=True)
    mean2 = jnp.mean(scaled * unit, axis=-1, keepdims=True)
    return (scaled - mean1 - unit * mean2) * inverse


def down_kernel(info, hidden, normed, grad, gain, shift, w0, w1, w2, w3, w4, w5, out, dsum, dlow, sums, held, sems, acc):
    copies = split_copies((w0, w1, w2, w3, w4, w5), ((0, held.shape[1], 0),), held, sems, info[2])
    start(copies)
    acc[...] = normed[...]

    def body(i, _):
        wait(copies, i)
        acc[...] += dot(hidden[i], held[i])
        return 0

    lax.fori_loop(0, 4, body, 0)
    unit, inverse = moments(acc[...])
    out[...] = (unit * gain[...] + shift[...]).astype(bf16)
    g = grad[...].astype(f32)
    back = norm_back(g, gain[...], unit, inverse)
    dsum[...] = back
    dlow[...] = back.astype(bf16)
    sums[...] = jnp.zeros_like(sums)
    sums[0:1] = jnp.sum(g * unit, axis=0, keepdims=True)
    sums[1:2] = jnp.sum(g, axis=0, keepdims=True)


def hidden_back_kernel(info, dlow, slope, w0, w1, w2, w3, w4, w5, du, send, sums, held, sems):
    copies = split_copies((w0, w1, w2, w3, w4, w5), ((0, held.shape[1], 0),), held, sems, info[2])
    start(copies)
    sums[...] = jnp.zeros_like(sums)

    def body(i, _):
        wait(copies, i)
        for chunk in range(3):
            at = slice(chunk * 256, chunk * 256 + 256)
            back = dot(dlow[...], held[i, at, :], NT) * slope[i, :, at].astype(f32)
            back = back.astype(bf16)
            du[i, :, at] = back
            sums[i, 0:1, at] = jnp.sum(back.astype(f32), axis=0, keepdims=True)

        @pl.when(i >= 2)
        def _():
            send[i - 2] = du[i]

        return 0

    send[2] = dlow[...]
    lax.fori_loop(0, 4, body, 0)


def residual_back_kernel(info, du, dsum, pre, gain, w0, w1, w2, w3, w4, w5, dres, dlow, sums, held, sems, acc):
    copies = split_copies((w0, w1, w2, w3, w4, w5), ((192, held.shape[1], 0),), held, sems, info[2])
    start(copies)
    acc[...] = dsum[...]

    def body(i, _):
        wait(copies, i)
        acc[...] += dot(du[i], held[i], NT)
        return 0

    lax.fori_loop(0, 4, body, 0)
    unit, inverse = moments(pre[...])
    g = acc[...]
    back = norm_back(g, gain[...], unit, inverse)
    dres[...] = back
    dlow[...] = back.astype(bf16)
    sums[...] = jnp.zeros_like(sums)
    sums[0:1] = jnp.sum(g * unit, axis=0, keepdims=True)
    sums[1:2] = jnp.sum(g, axis=0, keepdims=True)


def feed_grad_kernel(
    pick, hidden, hidden_other, gd, du_other, du, low, down0, down1, up0, up1, left, right, sems
):
    half = left.shape[-1]
    copies = []

    def bring(source, target):
        copy = pltpu.make_async_copy(source, target, sems.at[len(copies)])
        copy.start()
        copies.append(copy)

    for part, sources in ((0, (hidden.at[0], hidden_other.at[0], hidden.at[1], hidden_other.at[1])), (1, (low, hidden_other.at[2]))):
        columns = pl.ds(pl.multiple_of(pick[part] * half, half), half)
        for n, source in enumerate(sources):
            bring(source.at[:, columns], left.at[4 * part + n])
        if part == 0:
            bring(gd, right.at[0])
            bring(du_other.at[2], right.at[1])
        else:
            for j in range(2):
                bring(du.at[j], right.at[2 + 2 * j])
                bring(du_other.at[j], right.at[3 + 2 * j])
    for copy in copies[:6]:
        copy.wait()
    for j, out in ((0, down0), (1, down1)):
        out[...] = (dot(left[2 * j], right[0], TN) + dot(left[2 * j + 1], right[1], TN)).astype(bf16)
    for copy in copies[6:]:
        copy.wait()
    for j, out in ((0, up0), (1, up1)):
        out[...] = (dot(left[4], right[2 + 2 * j], TN) + dot(left[5], right[3 + 2 * j], TN)).astype(bf16)


def feed_grad(pick, hidden, hidden_other, gd, du_other, du, low):
    count, width = gd.shape
    return (
        feed_grad_kernel,
        [((width // 2, width), bf16)] * 4,
        [(VMEM, pick.astype(jnp.int32))] + [(ANY, x) for x in (hidden, hidden_other, gd, du_other, du, low)],
        [
            pltpu.VMEM((6, count, width // 2), bf16),
            pltpu.VMEM((6, count, width), bf16),
            pltpu.SemaphoreType.DMA((12,)),
        ],
        (0,),
    )


def joint_grad_kernel(joint, other, ctx, tokens, tokens_other, g, g_other, first, second):
    for kind in range(4):
        at = slice(kind * GROUP, kind * GROUP + GROUP)
        if kind < 3:
            total = dot(joint[0, :, at], tokens[...], TN) + dot(other[0, :, at], tokens_other[...], TN)
        else:
            total = dot(ctx[0], g[...], TN) + dot(other[0, :, at], g_other[...], TN)
        out = first if kind < 2 else second
        out[kind % 2 * 192 : kind % 2 * 192 + 192] = total[0:192].astype(bf16)


def joint_grad(joint, other, ctx, tokens, tokens_other, g, g_other, block, name):
    count, width = tokens.shape
    whole = pl.BlockSpec((count, width), lambda j: (0, 0))
    return pl.pallas_call(
        joint_grad_kernel,
        grid=(1,),
        out_shape=[jax.ShapeDtypeStruct((width // 2, width), bf16)] * 2,
        in_specs=[
            pl.BlockSpec((1, count, 3 * GROUP), lambda j: (block, 0, 0)),
            pl.BlockSpec((1, count, 4 * GROUP), lambda j: (block, 0, 0)),
            pl.BlockSpec((1, count, GROUP), lambda j: (block, 0, 0)),
            whole,
            whole,
            whole,
            whole,
        ],
        out_specs=[pl.BlockSpec((width // 2, width), lambda j: (0, 0))] * 2,
        compiler_params=pltpu.CompilerParams(vmem_limit_bytes=40 << 20),
        cost_estimate=pl.CostEstimate(flops=16 * count * GROUP * width, bytes_accessed=8 << 20, transcendentals=0),
        name=name,
    )(joint, other, ctx, tokens, tokens_other, g, g_other)


HOP = {1: 2, 2: 1, 3: 3}


def hop(x, step):
    return lax.ppermute(x, "head", [(i, i ^ HOP[step]) for i in range(4)])


def after(x, *deps):
    return lax.optimization_barrier((x,) + deps)[0]


def local(
    batch_count,
    tokens,
    lengths,
    w_query,
    w_key,
    w_value,
    w_out,
    conv_taps,
    w_up,
    b_up,
    w_down,
    gain_attn,
    shift_attn,
    gain_ffn,
    shift_ffn,
    grad_out,
):
    tokens = tokens[0]
    grad_out = grad_out[0]
    count, width = tokens.shape
    ext = count + 128
    length = lengths[0]
    place = lax.axis_index("head")
    batch = lax.axis_index("batch")
    core = place & 1
    side = batch & 1
    info = jnp.stack([length, place * count, side]).astype(jnp.int32)
    gain_attn, shift_attn, gain_ffn, shift_ffn = (
        x.reshape(1, width) for x in (gain_attn, shift_attn, gain_ffn, shift_ffn)
    )
    vm, an = VMEM, ANY

    def hop_batch(x, step):
        return lax.ppermute(x, "batch", [(i, i ^ step) for i in range(batch_count)])

    def neighbours(x, other):
        first = core == 0
        far = lax.ppermute(jnp.where(first, x[:HALO], x[-HALO:]), "head", [(1, 2), (2, 1)])
        return jnp.where(first, far, other[-HALO:]), jnp.where(first, other[:HALO], far)

    marks = jnp.arange(LANDMARKS + 1, dtype=jnp.int32) * length // LANDMARKS
    positions = info[1] + jnp.arange(count, dtype=jnp.int32)
    member = (positions[None, :] >= marks[:-1, None]) & (positions[None, :] < marks[1:, None])
    pooled = jnp.dot(member.astype(bf16), tokens, preferred_element_type=f32)
    pooled = pooled / (marks[1:] - marks[:-1]).astype(f32)[:, None]
    pooled = pooled + hop(pooled, 2)
    pooled_across = hop(pooled, 1)

    taps = jnp.pad(conv_taps, ((0, 0), (0, width - TAPS)))
    taps_back = jnp.pad(conv_taps[:, ::-1], ((0, 0), (0, width - TAPS)))
    small_own = jnp.concatenate([b_up[None], taps, taps_back, jnp.zeros((1, width), f32)], axis=0)
    term1 = small_own.astype(bf16)
    rest = small_own - lax.reduce_precision(small_own, 8, 7)
    term2 = rest.astype(bf16)
    term3 = (rest - lax.reduce_precision(rest, 8, 7)).astype(bf16)
    wt_own = jnp.concatenate(
        [w_query.T, w_key.T, w_value.T, term1, term2, term3, jnp.zeros((8, width), bf16)], axis=0
    )
    tokens_other = hop(tokens, 2)
    before, behind = neighbours(tokens, tokens_other)

    def column_half(own):
        return lax.dynamic_slice_in_dim(own, side * (width // 2), width // 2, 1)

    wt_other = hop(wt_own, 2)
    wt_across = hop(column_half(wt_own), 1)
    lm_own, iterates = call(
        landmark_kernel,
        [((64, 3 * GROUP), f32), ((NEWTON, 4, 3, 64, 64), f32)],
        [(vm, pooled), (vm, pooled_across), (vm, wt_own)],
        flops=int(1e9),
        size=4 << 20,
        name="landmarks",
    )
    lm_across = hop(lm_own, 1)
    lm = jnp.stack([lm_own, lm_across, hop(lm_own, 2), hop(lm_across, 2)])
    pooled_low = (pooled + pooled_across).astype(bf16)
    wt_across_x = hop_batch(wt_across, 1)
    wt = [wt_own, wt_across, wt_across_x, wt_other, hop(wt_across, 2), hop(wt_across_x, 2)]

    def small_of(block):
        return sum(block[576 + 8 * n : 584 + 8 * n].astype(f32) for n in range(3))

    def small_joined(near, far):
        near, far = small_of(near), small_of(far)
        first = side == 0
        return jnp.concatenate([jnp.where(first, near, far), jnp.where(first, far, near)], axis=1)

    small = jnp.stack(
        [small_of(wt[0]), small_joined(wt[1], wt[2]), small_of(wt[3]), small_joined(wt[4], wt[5])]
    )
    out_up_own = jnp.concatenate([w_out, after(w_up, pooled)], axis=0)
    out_up_across = hop(after(column_half(out_up_own), pooled_across), 1)
    down_across = hop(after(column_half(w_down), lm_across), 1)
    q, k, v = call(
        project_kernel,
        [((4, count, GROUP), bf16), ((4, count, GROUP), bf16), ((4, ext, GROUP), bf16)],
        [(vm, info), (vm, tokens), (vm, before), (vm, behind)] + [(an, w) for w in wt],
        [pltpu.VMEM((4, 3 * GROUP, width), bf16), pltpu.SemaphoreType.DMA((4, 3, 2))],
        flops=2 * count * width * 3072,
        size=8 << 20,
        smem=(0,),
        name="project",
    )
    out_up_across_x = hop_batch(after(out_up_across, q), 1)
    (pay,) = call(
        third_kernel,
        [((4, 64, GROUP), bf16)],
        [(vm, info), (vm, lm), (vm, k), (vm, v)],
        flops=int(1e9),
        size=3 << 20,
        smem=(0,),
        name="third",
    )
    pays = [pay, hop(pay, 1), hop(pay, 2), hop(pay, 3)]
    ctx, wst, x_mid = call(
        context_kernel,
        [((4, count, GROUP), bf16), ((4, 64, GROUP), f32), ((4, 64, GROUP), f32)],
        [(vm, p) for p in pays] + [(vm, lm), (vm, q), (vm, v), (vm, small)],
        flops=int(3e9),
        size=5 << 20,
        name="context",
    )
    out_up_far = after((out_up_across, out_up_across_x), ctx)
    out_up = [out_up_across, out_up_across_x, hop(after(out_up_own, q), 2), hop(out_up_far[0], 2), hop(out_up_far[1], 2)]
    down_across_x = hop_batch(after(down_across, ctx), 1)
    wo = [(an, w) for w in [w_out] + out_up]
    wu = [(an, w) for w in [w_up] + out_up]
    out_scratch = [pltpu.VMEM((4, GROUP, width), bf16), pltpu.SemaphoreType.DMA((4, 1, 2))]
    wide = [pltpu.VMEM((4, width, width), bf16), pltpu.SemaphoreType.DMA((4, 1, 2))]
    acc = [pltpu.VMEM((count, width), f32)]

    pre, normed, normed_low = call(
        attended_kernel,
        [((count, width), f32), ((count, width), f32), ((count, width), bf16)],
        [(vm, info), (vm, ctx), (vm, tokens), (vm, gain_attn), (vm, shift_attn)] + wo,
        out_scratch,
        flops=2 * count * width * width,
        size=6 << 20,
        smem=(0,),
        name="attended",
    )
    down_far = after((down_across, down_across_x), normed_low)
    down = [down_across, down_across_x, hop(after(w_down, ctx), 2), hop(down_far[0], 2), hop(down_far[1], 2)]
    wd = [(an, w) for w in [w_down] + down]
    hidden, slope, hidden_send = call(
        up_kernel,
        [((4, count, width), bf16), ((4, count, width), bf16), ((3, count, width), bf16)],
        [(vm, info), (vm, normed_low), (vm, small)] + wu,
        wide,
        flops=2 * count * width * 3072,
        size=12 << 20,
        smem=(0,),
        name="up",
    )
    hidden_other = hop(hidden_send, 2)
    output, d_sum, gd, sums_ffn = call(
        down_kernel,
        [((count, width), bf16), ((count, width), f32), ((count, width), bf16), ((8, width), f32)],
        [(vm, info), (vm, hidden), (vm, normed), (vm, grad_out), (vm, gain_ffn), (vm, shift_ffn)] + wd,
        wide + acc,
        flops=2 * count * width * 3072,
        size=14 << 20,
        smem=(0,),
        name="down",
    )

    steps = [1 << n for n in range(batch_count.bit_length() - 1)]
    down_order = steps[:2] + ["y"] + steps[2:]
    up_order = steps[1:2] + steps[:1] + ["y"] + steps[2:]

    def bit(step):
        return (batch // step) & 1

    def send(x, step):
        return hop(x, 1) if step == "y" else hop_batch(x, step)

    def chain(pieces, step):
        received = [send(pieces[0], step)]
        for piece in pieces[1:]:
            received.append(send(after(piece, received[-1]), step))
        return received

    def add_all(kept, received):
        return [(a.astype(f32) + b.astype(f32)).astype(bf16) for a, b in zip(kept, received)]

    def split_for(pieces, step):
        if step == "y":
            return pieces[:1], pieces[1:]
        rows = pieces[0].shape[0] // 2
        kept = [lax.dynamic_slice_in_dim(x, bit(step) * rows, rows, 0) for x in pieces]
        sent = [lax.dynamic_slice_in_dim(x, (1 - bit(step)) * rows, rows, 0) for x in pieces]
        if len(pieces) > 1:
            sent = [jnp.stack(sent)]
        return kept, sent

    def exchange(pieces, step):
        kept, sent = split_for(pieces, step)
        received = send(sent[0], step)
        return kept, [received] if received.ndim == 2 else [received[n] for n in range(len(kept))]

    def grow(x, step):
        other = hop_batch(x, step)
        mine_last = bit(step) == 1
        return jnp.concatenate([jnp.where(mine_last, other, x), jnp.where(mine_last, x, other)], axis=0)

    def rest_of(order, done):
        back = [step for step in order if step != "y"][::-1]
        return [lambda x, step=step: add_all(*exchange(x, step)) for step in order[done:]] + [
            lambda x, step=step: [grow(x[0], step)] for step in back
        ]

    du, du_send, sums_up = call(
        hidden_back_kernel,
        [((4, count, width), bf16), ((3, count, width), bf16), ((4, 8, width), f32)],
        [(vm, info), (vm, gd), (vm, slope)] + wd,
        wide,
        flops=2 * count * width * 3072,
        size=12 << 20,
        smem=(0,),
        name="hidden_back",
    )
    du_other = hop(du_send, 2)
    mine = jnp.stack([bit(down_order[0]), bit(up_order[0])])
    operands = (hidden, hidden_other, gd, du_other, du, normed_low)
    ((down_sent0, down_sent1, up_sent0, up_sent1),) = call_many([feed_grad(1 - mine, *operands)], "grad_sent")
    down_first = send(down_sent0, down_order[0])
    up_first = send(up_sent0, up_order[0])
    kept, (d_res, ga, sums_attn) = call_many(
        [
            feed_grad(mine, hidden, hidden_other, after(gd, down_sent0), du_other, du, normed_low),
            (
                residual_back_kernel,
                [((count, width), f32), ((count, width), bf16), ((8, width), f32)],
                [(vm, info), (vm, du), (vm, d_sum), (vm, pre), (vm, gain_attn)] + wu,
                wide + acc,
                (0,),
            ),
        ],
        "grad_kept",
    )
    down_kept, up_kept = kept[:2], kept[2:]
    ga, down_first, up_first = after((ga, down_first, up_first), d_res)
    ga_other = hop(ga, 2)
    ga_before, ga_behind = neighbours(ga, ga_other)
    down_second = send(after(down_sent1, down_first), down_order[0])
    up_second = send(after(up_sent1, up_first), up_order[0])
    dx, dq, dkl, dv_conv, dtaps = call(
        first_back_kernel,
        [
            ((4, 64, GROUP), f32),
            ((4, count, GROUP), bf16),
            ((4, 64, GROUP), f32),
            ((4, count, GROUP), f32),
            ((4, 8, GROUP), f32),
        ],
        [(vm, info), (vm, after(ga, down_first, up_first)), (vm, ga_before), (vm, ga_behind)]
        + wo
        + [(vm, lm), (vm, q), (vm, v), (vm, small), (vm, x_mid)],
        out_scratch + [pltpu.VMEM((ext, width), bf16), pltpu.VMEM((ext, GROUP), f32)],
        flops=int(5e9),
        size=10 << 20,
        smem=(0,),
        name="first_back",
    )

    def swap_core(x):
        other = hop(x, 2)
        return x.astype(f32) + jnp.concatenate([other[2:4], other[0:2]], axis=0).astype(f32)

    dx, down_second, up_second = after((dx, down_second, up_second), dtaps)
    dx = swap_core(after(dx, down_second, up_second))
    down_sent, up_sent = [down_first, down_second], [up_first, up_second]
    d_down = exchange(add_all(down_kept, down_sent), down_order[1])
    d_up = exchange(add_all(up_kept, up_sent), up_order[1])
    dx_across = hop(dx, 1)
    dx, dx_across, d_down, d_up = after((dx, dx_across, d_down, d_up), dx_across)
    d_down = exchange(add_all(*d_down), down_order[2])
    d_up = exchange(add_all(*d_up), up_order[2])
    dx, dx_across = after((dx, dx_across), d_down[0], d_up[0])
    joint, joint_send, partial = call(
        third_back_kernel,
        [((4, count, 3 * GROUP), bf16), ((2, count, 4 * GROUP), bf16), ((4, 64, 2 * GROUP), f32)],
        [(vm, info), (vm, dx), (vm, dx_across), (vm, lm), (vm, wst), (vm, k), (vm, v), (vm, dv_conv), (vm, dq)]
        + [(vm, dkl), (vm, ctx)],
        flops=int(5e9),
        size=8 << 20,
        smem=(0,),
        name="third_back",
    )
    joint_other = hop(after(joint_send, d_down[1], d_up[1]), 2)
    d_down, d_up = after((d_down, d_up), partial)
    d_down, d_up = add_all(*d_down), add_all(*d_up)
    operands = (after(joint, *d_down, *d_up), joint_other, ctx, tokens, tokens_other, ga, ga_other)
    sent = joint_grad(*operands, 1, "grad_joint_sent")
    joint_first = send(sent[0], "y")
    d_down, d_up = after((d_down, d_up), *sent)
    d_down, d_up = exchange(d_down, down_order[3]), exchange(d_up, up_order[3])
    (partial,) = call(
        inverse_back_kernel,
        [((4, 64, 2 * GROUP), bf16)],
        [(vm, dx), (vm, dx_across), (vm, wst), (vm, lm_own), (vm, iterates), (vm, after(partial, *sent))],
        flops=int(1e9),
        size=4 << 20,
        name="inverse_back",
    )
    partial = after(partial, joint_first, d_down[1], d_up[1])
    d_down, d_up = after((d_down, d_up), partial)
    d_down, d_up = add_all(*d_down), add_all(*d_up)
    partial = swap_core(partial).astype(bf16)
    partial_across = hop(partial, 1)
    down_rest, up_rest = rest_of(down_order, 4), rest_of(up_order, 4)
    if EARLY >= 1:
        d_down, d_up = down_rest[0](d_down), up_rest[0](d_up)
        partial, partial_across = after((partial, partial_across), partial_across, d_down[0], d_up[0])
        down_rest, up_rest = down_rest[1:], up_rest[1:]
    else:
        partial, partial_across = after((partial, partial_across), partial_across)
    joint_second = send(after(sent[1], partial_across), "y")
    joint_sent = [joint_first, joint_second]
    joint_kept = joint_grad(*after(operands, partial), 0, "grad_joint_kept")
    if EARLY >= 2:
        d_down, d_up = down_rest[0](d_down), up_rest[0](d_up)
        down_rest, up_rest = down_rest[1:], up_rest[1:]
    (d_tokens,) = call(
        token_back_kernel,
        [((count, width), f32)],
        [(vm, info), (vm, partial), (vm, partial_across), (vm, joint), (vm, d_res)] + [(an, w) for w in wt],
        [pltpu.VMEM((4, 3 * GROUP, width), bf16), pltpu.SemaphoreType.DMA((4, 3, 2))],
        flops=2 * count * width * 3072,
        size=10 << 20,
        smem=(0,),
        name="token_back",
    )
    landmark_own = (partial[0].astype(f32) + partial_across[1].astype(f32)).astype(bf16)
    low_rank = dot(landmark_own, pooled_low, TN)
    low_rank = jnp.concatenate([low_rank[0:192], low_rank[GROUP : GROUP + 192]], axis=0)
    d_first = (joint_kept[0].astype(f32) + joint_sent[0].astype(f32) + low_rank).astype(bf16)
    d_second = (joint_kept[1].astype(f32) + joint_sent[1].astype(f32)).astype(bf16)
    norms = jnp.concatenate([sums_attn[0:2], sums_ffn[0:2]], axis=0)
    dtaps = jnp.pad(dtaps[:, 1:4], ((0, 0), (0, 0), (0, width - GROUP)))
    minor = jnp.concatenate([sums_up[:, 0:1], dtaps, jnp.broadcast_to(norms, (4, 4, width))], axis=1)
    minor = after(minor, joint_second)
    minor = minor[0:2] + hop(minor[2:4], 2)
    minor = minor[0] + hop(minor[1], 1)
    orders = [steps, steps[1:2] + steps[:1] + steps[2:]]
    values = [[d_first], [d_second], d_down, d_up, [minor]]
    tasks = [
        rest_of(orders[0], 0),
        rest_of(orders[1], 0),
        down_rest,
        up_rest,
        [lambda x: x] * LATE + [lambda x, step=step: [x[0] + hop_batch(x[0], step)] for step in steps],
    ]
    for turn in range(max(len(task) for task in tasks)):
        anchors = (values[0][0], values[1][0]) + ((d_tokens,) if turn == 0 else ())
        values = [
            task[turn](after(value, *anchors)) if turn < len(task) else value for value, task in zip(values, tasks)
        ]
    d_parts = [values[0][0].astype(f32), values[1][0].astype(f32)]
    d_w_down, d_w_up = values[2][0].astype(f32), values[3][0].astype(f32)
    minor = values[4][0]
    d_w_query, d_w_key = d_parts[0][0:192].T, d_parts[0][192:384].T
    d_w_value, d_w_out = d_parts[1][0:192].T, d_parts[1][192:384]

    return (
        output[None],
        d_tokens[None],
        d_w_query,
        d_w_key,
        d_w_value,
        d_w_out,
        minor[1:4, 0:TAPS],
        d_w_up,
        minor[0],
        d_w_down,
        minor[4],
        minor[5],
        minor[6],
        minor[7],
    )


def solution(mesh):
    return jax.shard_map(
        functools.partial(local, mesh.shape["batch"]),
        mesh=mesh,
        in_specs=(
            P("batch", "head", None),
            P("batch"),
            P(None, "head"),
            P(None, "head"),
            P(None, "head"),
            P("head", None),
            P("head", None),
            P(None, "head"),
            P("head"),
            P("head", None),
            P(),
            P(),
            P(),
            P(),
            P("batch", "head", None),
        ),
        out_specs=(
            P("batch", "head", None),
            P("batch", "head", None),
            P(None, "head"),
            P(None, "head"),
            P(None, "head"),
            P("head", None),
            P("head", None),
            P(None, "head"),
            P("head"),
            P("head", None),
            P(),
            P(),
            P(),
            P(),
        ),
        check_vma=False,
    )
```

```python
import functools

import jax
import jax.numpy as jnp
from jax import lax
from jax.experimental import pallas as pl
from jax.experimental.pallas import tpu as pltpu
from jax.sharding import PartitionSpec as P

f32 = jnp.float32
bf16 = jnp.bfloat16
HEAD_DIM = 64
LANDMARKS = 64
NEWTON = 6
TAPS = 65
HALO = TAPS // 2
EARLY = 1
LATE = 0
GROUP = 256
NN = ((1,), (0,))
NT = ((1,), (1,))
TN = ((0,), (0,))
VMEM = pltpu.VMEM
ANY = pl.ANY


def dot(a, b, dims=NN):
    return lax.dot_general(a, b, (dims, ((), ())), preferred_element_type=f32)


def split(x):
    high = x.astype(bf16)
    return high, (x - high.astype(f32)).astype(bf16)


def mm(a, b, dims=NN):
    a_high, a_low = split(a)
    b_high, b_low = split(b)
    return dot(a_high, b_high, dims) + (dot(a_high, b_low, dims) + dot(a_low, b_high, dims))


def mm_left(a, b, dims=NN):
    a_high, a_low = split(a)
    return dot(a_high, b, dims) + dot(a_low, b, dims)


def iota(shape, dim):
    return lax.broadcasted_iota(jnp.int32, shape, dim)


def call(body, outs, ins, scratch=(), flops=0, size=0, limit=40, name=None, smem=()):
    specs = [
        pl.BlockSpec(memory_space=pltpu.SMEM) if i in smem else pl.BlockSpec(memory_space=space)
        for i, (space, _) in enumerate(ins)
    ]
    return pl.pallas_call(
        body,
        out_shape=[jax.ShapeDtypeStruct(s, d) for s, d in outs],
        in_specs=specs,
        out_specs=[pl.BlockSpec(memory_space=VMEM)] * len(outs),
        scratch_shapes=list(scratch),
        compiler_params=pltpu.CompilerParams(vmem_limit_bytes=limit << 20),
        cost_estimate=pl.CostEstimate(flops=flops, bytes_accessed=size, transcendentals=0),
        name=name,
    )(*[value for _, value in ins])


def call_many(parts, name):
    ins = [value for part in parts for value in part[2]]
    outs = [value for part in parts for value in part[1]]
    scratch = [value for part in parts for value in part[3]]
    smem, first = [], 0
    for part in parts:
        smem += [first + i for i in part[4]]
        first += len(part[2])

    def body(*refs):
        groups = [refs[: len(ins)], refs[len(ins) : len(ins) + len(outs)], refs[len(ins) + len(outs) :]]
        at = [0, 0, 0]
        for part in parts:
            mine = []
            for group, kind in ((0, 2), (1, 1), (2, 3)):
                mine += groups[group][at[group] : at[group] + len(part[kind])]
                at[group] += len(part[kind])
            part[0](*mine)

    results = call(body, outs, ins, scratch, flops=int(5e9), size=10 << 20, name=name, smem=tuple(smem), limit=48)
    split_results, first = [], 0
    for part in parts:
        split_results.append(results[first : first + len(part[1])])
        first += len(part[1])
    return split_results


def block_mask():
    return (iota((GROUP, GROUP), 0) >> 6) == (iota((GROUP, GROUP), 1) >> 6)


def spread(x):
    return jnp.where(block_mask(), jnp.concatenate([x, x, x, x], axis=0), 0.0)


def fold(x):
    kept = jnp.where(block_mask(), x, 0.0)
    return kept[0:64] + kept[64:128] + kept[128:192]


def rows_of(info, count, first):
    return info[1] + first + iota((count, 1), 0)


def landmark_kernel(p0, p1, p2, p3, wt, lm, pool, chain):
    pooled = (p0[...].astype(f32) + p1[...].astype(f32)) + (p2[...].astype(f32) + p3[...].astype(f32))
    pool[...] = pooled.astype(bf16)
    high, low = split(pooled)
    both = jnp.concatenate([high, low], axis=0)
    lm[...] = jnp.zeros_like(lm)
    matrices, starts = [], []
    for head in range(3):
        pair = []
        for kind in range(2):
            rows = wt[kind * 192 + head * 64 : kind * 192 + head * 64 + 64]
            out = dot(both, rows, NT)
            out = out[0:64] + out[64:128]
            lm[:, kind * GROUP + head * 64 : kind * GROUP + head * 64 + 64] = out
            pair.append(out)
        scores = mm(pair[0], pair[1], NT) * 0.125
        raised = jnp.exp(scores - jnp.max(scores, axis=1, keepdims=True))
        matrix = raised / jnp.sum(raised, axis=1, keepdims=True)
        column = jnp.max(jnp.sum(matrix, axis=0, keepdims=True), axis=1, keepdims=True)
        row = jnp.max(jnp.sum(matrix, axis=1, keepdims=True), axis=0, keepdims=True)
        matrices.append(matrix)
        starts.append(matrix.T / (column * row))
    eye = (iota((64, 64), 0) == iota((64, 64), 1)).astype(f32)

    def step(it, iterates):
        results = []
        for head in range(3):
            z = iterates[head]
            product = mm(matrices[head], z)
            inner1 = 7.0 * eye - product
            inner2 = 15.0 * eye - mm(product, inner1)
            inner3 = 13.0 * eye - mm(product, inner2)
            chain[it, 0, head] = z
            chain[it, 1, head] = product
            chain[it, 2, head] = inner2
            chain[it, 3, head] = inner3
            results.append(0.25 * mm(z, inner3))
        return tuple(results)

    finals = lax.fori_loop(0, NEWTON, step, tuple(starts))
    for head in range(3):
        lm[:, 2 * GROUP + head * 64 : 2 * GROUP + head * 64 + 64] = finals[head]


def inverse_back_kernel(x0, x1, wst_all, lm, chain, partial, out):
    total = x0[0] + x1[1]
    eye = (iota((64, 64), 0) == iota((64, 64), 1)).astype(f32)
    weight = wst_all[0]
    out[...] = partial[...].astype(bf16)
    grads, matrices, queries, keys = [], [], [], []
    for head in range(3):
        at = slice(head * 64, head * 64 + 64)
        grads.append(mm(total[:, at], weight[:, at], NT))
        query = lm[:, head * 64 : head * 64 + 64]
        key = lm[:, GROUP + head * 64 : GROUP + head * 64 + 64]
        scores = mm(query, key, NT) * 0.125
        raised = jnp.exp(scores - jnp.max(scores, axis=1, keepdims=True))
        matrices.append(raised / jnp.sum(raised, axis=1, keepdims=True))
        queries.append(query)
        keys.append(key)

    def step(count, carried):
        it = NEWTON - 1 - count
        results = []
        for head in range(3):
            dz_next, da = carried[2 * head], carried[2 * head + 1]
            z = chain[it, 0, head]
            product = chain[it, 1, head]
            inner1 = 7.0 * eye - product
            inner2 = chain[it, 2, head]
            inner3 = chain[it, 3, head]
            dz_next = 0.25 * dz_next
            dz = mm(dz_next, inner3, NT)
            d3 = -mm(z, dz_next, TN)
            d2 = -mm(product, d3, TN)
            d1 = mm(product, d2, TN)
            dp = mm(d3, inner2, NT) + mm(d2, inner1, NT) - d1
            da = da + mm(dp, z, NT)
            dz = dz + mm(matrices[head], dp, TN)
            results += [dz, da]
        return tuple(results)

    first = []
    for head in range(3):
        first += [grads[head], jnp.zeros((64, 64), f32)]
    last = lax.fori_loop(0, NEWTON, step, tuple(first))
    for head in range(3):
        dz, da = last[2 * head], last[2 * head + 1]
        matrix = matrices[head]
        columns = jnp.sum(matrix, axis=0, keepdims=True)
        rows = jnp.sum(matrix, axis=1, keepdims=True)
        column = jnp.max(columns, axis=1, keepdims=True)
        row = jnp.max(rows, axis=0, keepdims=True)
        scale = 1.0 / (column * row)
        da = da + dz.T * scale
        d_scale = -jnp.sum(jnp.sum(dz * matrix.T, axis=1, keepdims=True), axis=0, keepdims=True) * scale * scale
        column_hit = (columns == column).astype(f32)
        row_hit = (rows == row).astype(f32)
        da = da + d_scale * row * column_hit / jnp.sum(column_hit, axis=1, keepdims=True)
        da = da + d_scale * column * row_hit / jnp.sum(row_hit, axis=0, keepdims=True)
        ds = matrix * (da - jnp.sum(da * matrix, axis=1, keepdims=True)) * 0.125
        for at, value in ((head * 64, mm(ds, keys[head])), (GROUP + head * 64, mm(ds, queries[head], TN))):
            out[0, :, at : at + 64] = (partial[0, :, at : at + 64] + value).astype(bf16)


PROJECTION = ((0, 192, 0), (192, 192, GROUP), (384, 192, 2 * GROUP))


def split_copies(refs, parts, held, sems, side):
    own, across, across_x, other, both, both_x = refs
    half = own.shape[1] // 2
    mine = pl.ds(pl.multiple_of(side * half, half), half)
    rest = pl.ds(pl.multiple_of((1 - side) * half, half), half)
    blocks = [[], [], [], []]
    for n, (row, rows, to) in enumerate(parts):
        first = pl.ds(row - parts[0][0], rows)
        source, to = pl.ds(row, rows), pl.ds(to, rows)
        blocks[0].append(pltpu.make_async_copy(own.at[first], held.at[0, to], sems.at[0, n, 0]))
        blocks[2].append(pltpu.make_async_copy(other.at[source], held.at[2, to], sems.at[2, n, 0]))
        for i, near, far in ((1, across, across_x), (3, both, both_x)):
            blocks[i].append(pltpu.make_async_copy(near.at[source], held.at[i, to, mine], sems.at[i, n, 0]))
            blocks[i].append(pltpu.make_async_copy(far.at[source], held.at[i, to, rest], sems.at[i, n, 1]))
    return blocks


def start(copies):
    for block in copies:
        for copy in block:
            copy.start()


def wait(copies, i):
    for block in range(4):

        @pl.when(i == block)
        def _():
            for copy in copies[block]:
                copy.wait()


def zero_gaps(held, kinds):
    for i in range(4):
        for kind in range(kinds):
            held[i, kind * GROUP + 192 : kind * GROUP + 256, :] = jnp.zeros((64, held.shape[2]), bf16)


def project_kernel(info, tokens, before, after, w0, w1, w2, w3, w4, w5, q_out, k_out, v_out, held, sems):
    count = tokens.shape[0]
    copies = split_copies((w0, w1, w2, w3, w4, w5), PROJECTION, held, sems, info[2])
    start(copies)
    zero_gaps(held, 3)
    valid = (rows_of(info, count, 0) < info[0]).astype(f32)
    valid_before = (rows_of(info, HALO, -HALO) < info[0]).astype(f32)
    valid_after = (rows_of(info, HALO, count) < info[0]).astype(f32)

    def body(i, _):
        wait(copies, i)
        for kind, out in ((0, q_out), (1, k_out)):
            out[i] = (dot(tokens[...], held[i, kind * GROUP : kind * GROUP + GROUP], NT) * valid).astype(bf16)
        wv = held[i, 2 * GROUP : 3 * GROUP]
        v_out[i, HALO : HALO + count] = (dot(tokens[...], wv, NT) * valid).astype(bf16)
        v_out[i, 0:HALO] = (dot(before[...], wv, NT) * valid_before).astype(bf16)
        v_out[i, HALO + count : 2 * HALO + count] = (dot(after[...], wv, NT) * valid_after).astype(bf16)
        v_out[i, 2 * HALO + count :] = jnp.zeros((v_out.shape[1] - 2 * HALO - count, GROUP), bf16)
        return 0

    lax.fori_loop(0, 4, body, 0)


def third_scores(info, lm, k_ref, i):
    count = k_ref.shape[1]
    valid = info[1] + iota((1, count), 1) < info[0]
    queries = spread(lm[i, :, 0:GROUP])
    return jnp.where(valid, mm_left(queries, k_ref[i], NT) * 0.125, -1e30)


def third_kernel(info, lm, k_ref, v_ref, pay):
    count = k_ref.shape[1]
    lane = iota((64, GROUP), 1)

    def body(i, _):
        scores = third_scores(info, lm, k_ref, i)
        top = jnp.max(scores, axis=1, keepdims=True)
        raised = jnp.exp(scores - top)
        total = jnp.sum(raised, axis=1, keepdims=True)
        packed = fold(mm_left(raised, v_ref[i, HALO : HALO + count]) / total)
        for stat, base in ((top, 192), (total, 216)):
            for term in range(3):
                part = stat.astype(bf16).astype(f32)
                stat = stat - part
                for head in range(3):
                    packed = jnp.where(lane == base + 8 * term + head, part[head * 64 : head * 64 + 64], packed)
        pay[i] = packed.astype(bf16)
        return 0

    lax.fori_loop(0, 4, body, 0)


def first_scores(lm, q_ref, i):
    keys = spread(lm[i, :, GROUP : 2 * GROUP])
    count = q_ref.shape[1]
    scores = (mm_left(keys, q_ref[i], NT) * 0.125).reshape(4, 64, count)
    raised = jnp.exp(scores - jnp.max(scores, axis=1, keepdims=True))
    return raised / jnp.sum(raised, axis=1, keepdims=True)


def toeplitz(row):
    return pltpu.roll(jnp.broadcast_to(row, (128, GROUP)), 0, 1, stride=1, stride_axis=0)


def head_select(x, rows):
    lane = iota((rows, GROUP), 1) >> 6
    out = jnp.where(lane == 0, x[0:rows], 0.0)
    out = jnp.where(lane == 1, x[rows : 2 * rows], out)
    return jnp.where(lane == 2, x[2 * rows : 3 * rows], out)


def context_kernel(p0, p1, p2, p3, lm, q_ref, v_ref, small, ctx, wst, x_out):
    count = q_ref.shape[1]
    lane = iota((64, GROUP), 1)

    def body(i, _):
        parts = [p[i ^ n].astype(f32) for n, p in enumerate((p0, p1, p2, p3))]

        def stat(part, at):
            return part[:, at : at + 1] + part[:, at + 8 : at + 9] + part[:, at + 16 : at + 17]

        factors = [jnp.zeros((64, GROUP), f32) for _ in range(4)]
        stats = jnp.zeros((64, GROUP), f32)
        for head in range(3):
            tops = [stat(part, 192 + head) for part in parts]
            top = jnp.maximum(jnp.maximum(tops[0], tops[1]), jnp.maximum(tops[2], tops[3]))
            scales = [stat(part, 216 + head) * jnp.exp(t - top) for part, t in zip(parts, tops)]
            total = sum(scales)
            mine = (lane >> 6) == head
            factors = [jnp.where(mine, s / total, f) for s, f in zip(scales, factors)]
            stats = jnp.where(lane == 192 + head, top, stats)
            stats = jnp.where(lane == 196 + head, total, stats)
        weight = sum(part * f for part, f in zip(parts, factors))
        wst[i] = jnp.where(lane < 192, weight, stats)
        mixed = mm(spread(lm[i, :, 2 * GROUP : 3 * GROUP]), spread(weight))
        x_out[i] = fold(mixed)
        first = first_scores(lm, q_ref, i).reshape(GROUP, count)
        main = mm(first, mixed, TN)
        bands = [toeplitz(small[i, 1 + head : 2 + head, 0:GROUP]) for head in range(3)]
        high, low = split(jnp.concatenate(bands, axis=0))
        for block in range(count // 128):
            window = v_ref[i, block * 128 : block * 128 + 256]
            conv = dot(high, window) + dot(low, window)
            ctx[i, block * 128 : block * 128 + 128] = (
                main[block * 128 : block * 128 + 128] + head_select(conv, 128)
            ).astype(bf16)
        return 0

    lax.fori_loop(0, 4, body, 0)


def first_back_kernel(
    info, g_ref, before, after, o0, o1, o2, o3, o4, o5, lm, q_ref, v_ref, small, x_in, dx, dq, dkl, dv, dtaps, held, sems, ext, dctx
):
    count = g_ref.shape[0]
    width = g_ref.shape[1]
    copies = split_copies((o0, o1, o2, o3, o4, o5), ((0, 192, 0),), held, sems, info[2])
    start(copies)
    zero_gaps(held, 1)
    valid = (rows_of(info, count, 0) < info[0]).astype(f32)
    ext[0:HALO] = before[...]
    ext[HALO : HALO + count] = g_ref[...]
    ext[HALO + count : 2 * HALO + count] = after[...]
    ext[2 * HALO + count :] = jnp.zeros((ext.shape[0] - 2 * HALO - count, width), bf16)
    lane = iota((128, GROUP), 1) >> 6
    flip = (iota((128, 128), 0) + iota((128, 128), 1) == 127).astype(bf16)

    def body(i, _):
        wait(copies, i)
        dctx[...] = dot(ext[...], held[i], NT)
        own = dctx[HALO : HALO + count]
        own_high = own.astype(bf16)
        first = first_scores(lm, q_ref, i)
        flat = first.reshape(GROUP, count)
        dx[i] = fold(dot(flat.astype(bf16), own_high))
        dfirst = dot(spread(x_in[i]).astype(bf16), own_high, NT)
        dfirst = dfirst.reshape(4, 64, count)
        ds = first * (dfirst - jnp.sum(first * dfirst, axis=1, keepdims=True)) * 0.125
        ds = ds.reshape(GROUP, count).astype(bf16)
        keys = (spread(lm[i, :, GROUP : 2 * GROUP])).astype(bf16)
        dquery = dot(ds, keys, TN)
        dq[i] = (dquery * valid).astype(bf16)
        dkl[i] = fold(dot(ds, q_ref[i]))
        bands = [toeplitz(small[i, 4 + head : 5 + head, 0:GROUP]) for head in range(3)]
        high = jnp.concatenate(bands, axis=0).astype(bf16)
        gram = jnp.zeros((384, GROUP), f32)
        for block in range(count // 128):
            conv = dot(high, dctx[block * 128 : block * 128 + 256].astype(bf16))
            dv[i, block * 128 : block * 128 + 128] = head_select(conv, 128)
            piece = dctx[HALO + block * 128 : HALO + block * 128 + 128]
            stacked = jnp.concatenate([jnp.where(lane == head, piece, 0.0) for head in range(3)], axis=0)
            gram = gram + dot(stacked.astype(bf16), v_ref[i, block * 128 : block * 128 + 256], NT)
        dtaps[i] = jnp.zeros((8, GROUP), f32)
        for head in range(3):
            part_high, part_low = split(gram[head * 128 : head * 128 + 128])
            upturned = dot(flip, part_high) + dot(flip, part_low)
            straight = pltpu.roll(upturned, GROUP - 127, 1, stride=1, stride_axis=0)
            summed = jnp.sum(straight, axis=0, keepdims=True)
            dtaps[i, 1 + head : 2 + head, :] = jnp.where(iota((1, GROUP), 1) < TAPS, summed, 0.0)
        return 0

    lax.fori_loop(0, 4, body, 0)


def third_back_kernel(info, x0, x1, lm, wst, k_ref, v_ref, dvc, dq, dkl, ctx, joint, send, partial):
    count = k_ref.shape[1]
    valid = (rows_of(info, count, 0) < info[0]).astype(f32)
    none = jnp.zeros((64, 1), f32)

    def body(i, _):
        dx = spread(x0[i] + x1[i ^ 1])
        dweight = mm(spread(lm[i, :, 2 * GROUP : 3 * GROUP]), dx, TN)
        stats = wst[i]
        weight = spread(jnp.where(iota((64, GROUP), 1) < 192, stats, 0.0))
        inner = jnp.sum(dweight * weight, axis=1, keepdims=True)
        top = jnp.concatenate([stats[:, 192 + head : 193 + head] for head in range(3)] + [none], axis=0)
        total = jnp.concatenate([stats[:, 196 + head : 197 + head] for head in range(3)] + [none + 1.0], axis=0)
        scores = third_scores(info, lm, k_ref, i)
        third = jnp.exp(scores - top) / total
        dw_high = dweight.astype(bf16)
        values = v_ref[i, HALO : HALO + count]
        dthird = dot(dw_high, values, NT)
        ds = (third * (dthird - inner) * 0.125).astype(bf16)
        queries = (spread(lm[i, :, 0:GROUP])).astype(bf16)
        dkey = dot(ds, queries, TN)
        partial[i, :, 0:GROUP] = fold(dot(ds, k_ref[i]))
        partial[i, :, GROUP : 2 * GROUP] = dkl[i]
        dvalues = dot(third.astype(bf16), dw_high, TN)
        joint[i, :, 0:GROUP] = dq[i]
        joint[i, :, GROUP : 2 * GROUP] = (dkey * valid).astype(bf16)
        joint[i, :, 2 * GROUP : 3 * GROUP] = ((dvalues + dvc[i]) * valid).astype(bf16)

        @pl.when(i >= 2)
        def _():
            send[i - 2, :, 0 : 3 * GROUP] = joint[i]
            send[i - 2, :, 3 * GROUP : 4 * GROUP] = ctx[i]

        return 0

    lax.fori_loop(0, 4, body, 0)


def token_back_kernel(info, l0, l1, joint, dres, w0, w1, w2, w3, w4, w5, out, held, sems):
    copies = split_copies((w0, w1, w2, w3, w4, w5), PROJECTION, held, sems, info[2])
    start(copies)
    zero_gaps(held, 3)
    count = joint.shape[1]
    mark = iota((1, 64), 1)
    low = (mark * info[0]) >> 6
    high = ((mark + 1) * info[0]) >> 6
    pos = rows_of(info, count, 0)
    member = ((pos >= low) & (pos < high)).astype(bf16)
    row = iota((64, 1), 0)
    width = ((((row + 1) * info[0]) >> 6) - ((row * info[0]) >> 6)).astype(f32)
    out[...] = dres[...]

    def body(i, pooled):
        wait(copies, i)
        out[...] += dot(joint[i], held[i])
        marks = (l0[i].astype(f32) + l1[i ^ 1].astype(f32)) / width
        return pooled + mm_left(marks, held[i, 0 : 2 * GROUP])

    pooled = lax.fori_loop(0, 4, body, jnp.zeros((64, out.shape[1]), f32))
    pooled_high, pooled_low = split(pooled)
    out[...] += dot(member, pooled_high) + dot(member, pooled_low)


def moments(x):
    centered = x - jnp.mean(x, axis=-1, keepdims=True)
    variance = jnp.mean(centered * centered, axis=-1, keepdims=True)
    inverse = lax.rsqrt(variance + 1e-05)
    return centered * inverse, inverse


def attended_kernel(info, ctx, tokens, gain, shift, o0, o1, o2, o3, o4, o5, pre, normed, low, held, sems):
    copies = split_copies((o0, o1, o2, o3, o4, o5), ((0, 192, 0),), held, sems, info[2])
    start(copies)
    zero_gaps(held, 1)
    pre[...] = tokens[...].astype(f32)

    def body(i, _):
        wait(copies, i)
        pre[...] += dot(ctx[i], held[i])
        return 0

    lax.fori_loop(0, 4, body, 0)
    unit, _ = moments(pre[...])
    result = unit * gain[...] + shift[...]
    normed[...] = result
    low[...] = result.astype(bf16)


def gelu_parts(u):
    cdf = 0.5 + 0.5 * lax.erf(u * 0.7071067811865476)
    pdf = jnp.exp(u * u * -0.5) * 0.3989422804014327
    return u * cdf, cdf + u * pdf


def up_kernel(info, low, small, w0, w1, w2, w3, w4, w5, hidden, slope, send, held, sems):
    copies = split_copies((w0, w1, w2, w3, w4, w5), ((192, held.shape[1], 0),), held, sems, info[2])
    start(copies)

    def body(i, _):
        wait(copies, i)
        for chunk in range(3):
            at = slice(chunk * 256, chunk * 256 + 256)
            upward = dot(low[...], held[i, :, at]) + small[i, 0:1, at]
            value, derivative = gelu_parts(upward)
            hidden[i, :, at] = value.astype(bf16)
            slope[i, :, at] = derivative.astype(bf16)

        @pl.when(i >= 2)
        def _():
            send[i - 2] = hidden[i]

        return 0

    send[2] = low[...]
    lax.fori_loop(0, 4, body, 0)


def norm_back(g, gain, unit, inverse):
    scaled = g * gain
    mean1 = jnp.mean(scaled, axis=-1, keepdims=True)
    mean2 = jnp.mean(scaled * unit, axis=-1, keepdims=True)
    return (scaled - mean1 - unit * mean2) * inverse


def down_kernel(info, hidden, normed, grad, gain, shift, w0, w1, w2, w3, w4, w5, out, dsum, dlow, sums, held, sems, acc):
    copies = split_copies((w0, w1, w2, w3, w4, w5), ((0, held.shape[1], 0),), held, sems, info[2])
    start(copies)
    acc[...] = normed[...]

    def body(i, _):
        wait(copies, i)
        acc[...] += dot(hidden[i], held[i])
        return 0

    lax.fori_loop(0, 4, body, 0)
    unit, inverse = moments(acc[...])
    out[...] = (unit * gain[...] + shift[...]).astype(bf16)
    g = grad[...].astype(f32)
    back = norm_back(g, gain[...], unit, inverse)
    dsum[...] = back
    dlow[...] = back.astype(bf16)
    sums[...] = jnp.zeros_like(sums)
    sums[0:1] = jnp.sum(g * unit, axis=0, keepdims=True)
    sums[1:2] = jnp.sum(g, axis=0, keepdims=True)


def hidden_back_kernel(info, dlow, slope, w0, w1, w2, w3, w4, w5, du, send, sums, held, sems):
    copies = split_copies((w0, w1, w2, w3, w4, w5), ((0, held.shape[1], 0),), held, sems, info[2])
    start(copies)
    sums[...] = jnp.zeros_like(sums)

    def body(i, _):
        wait(copies, i)
        for chunk in range(3):
            at = slice(chunk * 256, chunk * 256 + 256)
            back = dot(dlow[...], held[i, at, :], NT) * slope[i, :, at].astype(f32)
            back = back.astype(bf16)
            du[i, :, at] = back
            sums[i, 0:1, at] = jnp.sum(back.astype(f32), axis=0, keepdims=True)

        @pl.when(i >= 2)
        def _():
            send[i - 2] = du[i]

        return 0

    send[2] = dlow[...]
    lax.fori_loop(0, 4, body, 0)


def residual_back_kernel(info, du, dsum, pre, gain, w0, w1, w2, w3, w4, w5, dres, dlow, sums, held, sems, acc):
    copies = split_copies((w0, w1, w2, w3, w4, w5), ((192, held.shape[1], 0),), held, sems, info[2])
    start(copies)
    acc[...] = dsum[...]

    def body(i, _):
        wait(copies, i)
        acc[...] += dot(du[i], held[i], NT)
        return 0

    lax.fori_loop(0, 4, body, 0)
    unit, inverse = moments(pre[...])
    g = acc[...]
    back = norm_back(g, gain[...], unit, inverse)
    dres[...] = back
    dlow[...] = back.astype(bf16)
    sums[...] = jnp.zeros_like(sums)
    sums[0:1] = jnp.sum(g * unit, axis=0, keepdims=True)
    sums[1:2] = jnp.sum(g, axis=0, keepdims=True)


def feed_grad_kernel(
    pick, hidden, hidden_other, gd, du_other, du, low, down0, down1, up0, up1, left, right, sems
):
    half = left.shape[-1]
    copies = []

    def bring(source, target):
        copy = pltpu.make_async_copy(source, target, sems.at[len(copies)])
        copy.start()
        copies.append(copy)

    for part, sources in ((0, (hidden.at[0], hidden_other.at[0], hidden.at[1], hidden_other.at[1])), (1, (low, hidden_other.at[2]))):
        columns = pl.ds(pl.multiple_of(pick[part] * half, half), half)
        for n, source in enumerate(sources):
            bring(source.at[:, columns], left.at[4 * part + n])
        if part == 0:
            bring(gd, right.at[0])
            bring(du_other.at[2], right.at[1])
        else:
            for j in range(2):
                bring(du.at[j], right.at[2 + 2 * j])
                bring(du_other.at[j], right.at[3 + 2 * j])
    for copy in copies[:6]:
        copy.wait()
    for j, out in ((0, down0), (1, down1)):
        out[...] = (dot(left[2 * j], right[0], TN) + dot(left[2 * j + 1], right[1], TN)).astype(bf16)
    for copy in copies[6:]:
        copy.wait()
    for j, out in ((0, up0), (1, up1)):
        out[...] = (dot(left[4], right[2 + 2 * j], TN) + dot(left[5], right[3 + 2 * j], TN)).astype(bf16)


def feed_grad(pick, hidden, hidden_other, gd, du_other, du, low):
    count, width = gd.shape
    return (
        feed_grad_kernel,
        [((width // 2, width), bf16)] * 4,
        [(VMEM, pick.astype(jnp.int32))] + [(ANY, x) for x in (hidden, hidden_other, gd, du_other, du, low)],
        [
            pltpu.VMEM((6, count, width // 2), bf16),
            pltpu.VMEM((6, count, width), bf16),
            pltpu.SemaphoreType.DMA((12,)),
        ],
        (0,),
    )


def joint_grad_kernel(joint, other, ctx, tokens, tokens_other, g, g_other, first, second):
    for kind in range(4):
        at = slice(kind * GROUP, kind * GROUP + GROUP)
        if kind < 3:
            total = dot(joint[0, :, at], tokens[...], TN) + dot(other[0, :, at], tokens_other[...], TN)
        else:
            total = dot(ctx[0], g[...], TN) + dot(other[0, :, at], g_other[...], TN)
        out = first if kind < 2 else second
        out[kind % 2 * 192 : kind % 2 * 192 + 192] = total[0:192].astype(bf16)


def joint_grad(joint, other, ctx, tokens, tokens_other, g, g_other, block, name):
    count, width = tokens.shape
    whole = pl.BlockSpec((count, width), lambda j: (0, 0))
    return pl.pallas_call(
        joint_grad_kernel,
        grid=(1,),
        out_shape=[jax.ShapeDtypeStruct((width // 2, width), bf16)] * 2,
        in_specs=[
            pl.BlockSpec((1, count, 3 * GROUP), lambda j: (block, 0, 0)),
            pl.BlockSpec((1, count, 4 * GROUP), lambda j: (block, 0, 0)),
            pl.BlockSpec((1, count, GROUP), lambda j: (block, 0, 0)),
            whole,
            whole,
            whole,
            whole,
        ],
        out_specs=[pl.BlockSpec((width // 2, width), lambda j: (0, 0))] * 2,
        compiler_params=pltpu.CompilerParams(vmem_limit_bytes=40 << 20),
        cost_estimate=pl.CostEstimate(flops=16 * count * GROUP * width, bytes_accessed=8 << 20, transcendentals=0),
        name=name,
    )(joint, other, ctx, tokens, tokens_other, g, g_other)


HOP = {1: 2, 2: 1, 3: 3}


def hop(x, step):
    return lax.ppermute(x, "head", [(i, i ^ HOP[step]) for i in range(4)])


def after(x, *deps):
    return lax.optimization_barrier((x,) + deps)[0]


def local(
    batch_count,
    tokens,
    lengths,
    w_query,
    w_key,
    w_value,
    w_out,
    conv_taps,
    w_up,
    b_up,
    w_down,
    gain_attn,
    shift_attn,
    gain_ffn,
    shift_ffn,
    grad_out,
):
    tokens = tokens[0]
    grad_out = grad_out[0]
    count, width = tokens.shape
    ext = count + 128
    length = lengths[0]
    place = lax.axis_index("head")
    batch = lax.axis_index("batch")
    core = place & 1
    side = batch & 1
    info = jnp.stack([length, place * count, side]).astype(jnp.int32)
    gain_attn, shift_attn, gain_ffn, shift_ffn = (
        x.reshape(1, width) for x in (gain_attn, shift_attn, gain_ffn, shift_ffn)
    )
    vm, an = VMEM, ANY

    def hop_batch(x, step):
        return lax.ppermute(x, "batch", [(i, i ^ step) for i in range(batch_count)])

    def neighbours(x, other):
        first = core == 0
        far = lax.ppermute(jnp.where(first, x[:HALO], x[-HALO:]), "head", [(1, 2), (2, 1)])
        return jnp.where(first, far, other[-HALO:]), jnp.where(first, other[:HALO], far)

    marks = jnp.arange(LANDMARKS + 1, dtype=jnp.int32) * length // LANDMARKS
    positions = info[1] + jnp.arange(count, dtype=jnp.int32)
    member = (positions[None, :] >= marks[:-1, None]) & (positions[None, :] < marks[1:, None])
    pooled = jnp.dot(member.astype(bf16), tokens, preferred_element_type=f32)
    pooled = (pooled / (marks[1:] - marks[:-1]).astype(f32)[:, None]).astype(bf16)
    pools = [pooled] + [hop(pooled, n) for n in (1, 2, 3)]

    taps = jnp.pad(conv_taps, ((0, 0), (0, width - TAPS)))
    taps_back = jnp.pad(conv_taps[:, ::-1], ((0, 0), (0, width - TAPS)))
    small_own = jnp.concatenate([b_up[None], taps, taps_back, jnp.zeros((1, width), f32)], axis=0)
    term1 = small_own.astype(bf16)
    rest = small_own - lax.reduce_precision(small_own, 8, 7)
    term2 = rest.astype(bf16)
    term3 = (rest - lax.reduce_precision(rest, 8, 7)).astype(bf16)
    wt_own = jnp.concatenate(
        [w_query.T, w_key.T, w_value.T, term1, term2, term3, jnp.zeros((8, width), bf16)], axis=0
    )
    tokens_other = hop(tokens, 2)
    before, behind = neighbours(tokens, tokens_other)

    def column_half(own):
        return lax.dynamic_slice_in_dim(own, side * (width // 2), width // 2, 1)

    wt_other = hop(wt_own, 2)
    wt_across = hop(after(column_half(wt_own), *pools), 1)
    lm_own, pooled_low, iterates = call(
        landmark_kernel,
        [((64, 3 * GROUP), f32), ((64, width), bf16), ((NEWTON, 4, 3, 64, 64), f32)],
        [(vm, x) for x in pools] + [(vm, wt_own)],
        flops=int(1e9),
        size=4 << 20,
        name="landmarks",
    )
    lm_own = after(lm_own, wt_across, before, behind)
    lm_across = hop(lm_own, 1)
    wt_across_x = hop_batch(after(wt_across, pooled_low), 1)
    lm = jnp.stack([lm_own, lm_across, hop(lm_own, 2), hop(lm_across, 2)])
    wt = [wt_own, wt_across, wt_across_x, wt_other, hop(wt_across, 2), hop(wt_across_x, 2)]

    def small_of(block):
        return sum(block[576 + 8 * n : 584 + 8 * n].astype(f32) for n in range(3))

    def small_joined(near, far):
        near, far = small_of(near), small_of(far)
        first = side == 0
        return jnp.concatenate([jnp.where(first, near, far), jnp.where(first, far, near)], axis=1)

    small = jnp.stack(
        [small_of(wt[0]), small_joined(wt[1], wt[2]), small_of(wt[3]), small_joined(wt[4], wt[5])]
    )
    out_up_own = jnp.concatenate([w_out, after(w_up, pooled)], axis=0)
    out_up_across = hop(after(column_half(out_up_own), lm_across), 1)
    down_across = hop(after(column_half(w_down), lm_across), 1)
    q, k, v = call(
        project_kernel,
        [((4, count, GROUP), bf16), ((4, count, GROUP), bf16), ((4, ext, GROUP), bf16)],
        [(vm, info), (vm, tokens), (vm, before), (vm, behind)] + [(an, w) for w in wt],
        [pltpu.VMEM((4, 3 * GROUP, width), bf16), pltpu.SemaphoreType.DMA((4, 3, 2))],
        flops=2 * count * width * 3072,
        size=8 << 20,
        smem=(0,),
        name="project",
    )
    out_up_across_x = hop_batch(after(out_up_across, q), 1)
    (pay,) = call(
        third_kernel,
        [((4, 64, GROUP), bf16)],
        [(vm, info), (vm, lm), (vm, k), (vm, v)],
        flops=int(1e9),
        size=3 << 20,
        smem=(0,),
        name="third",
    )
    pays = [pay, hop(pay, 1), hop(pay, 2), hop(pay, 3)]
    ctx, wst, x_mid = call(
        context_kernel,
        [((4, count, GROUP), bf16), ((4, 64, GROUP), f32), ((4, 64, GROUP), f32)],
        [(vm, p) for p in pays] + [(vm, lm), (vm, q), (vm, v), (vm, small)],
        flops=int(3e9),
        size=5 << 20,
        name="context",
    )
    out_up_far = after((out_up_across, out_up_across_x), ctx)
    out_up = [out_up_across, out_up_across_x, hop(after(out_up_own, q), 2), hop(out_up_far[0], 2), hop(out_up_far[1], 2)]
    down_across_x = hop_batch(after(down_across, ctx), 1)
    wo = [(an, w) for w in [w_out] + out_up]
    wu = [(an, w) for w in [w_up] + out_up]
    out_scratch = [pltpu.VMEM((4, GROUP, width), bf16), pltpu.SemaphoreType.DMA((4, 1, 2))]
    wide = [pltpu.VMEM((4, width, width), bf16), pltpu.SemaphoreType.DMA((4, 1, 2))]
    acc = [pltpu.VMEM((count, width), f32)]

    pre, normed, normed_low = call(
        attended_kernel,
        [((count, width), f32), ((count, width), f32), ((count, width), bf16)],
        [(vm, info), (vm, ctx), (vm, tokens), (vm, gain_attn), (vm, shift_attn)] + wo,
        out_scratch,
        flops=2 * count * width * width,
        size=6 << 20,
        smem=(0,),
        name="attended",
    )
    down_far = after((down_across, down_across_x), normed_low)
    down = [down_across, down_across_x, hop(after(w_down, ctx), 2), hop(down_far[0], 2), hop(down_far[1], 2)]
    wd = [(an, w) for w in [w_down] + down]
    hidden, slope, hidden_send = call(
        up_kernel,
        [((4, count, width), bf16), ((4, count, width), bf16), ((3, count, width), bf16)],
        [(vm, info), (vm, normed_low), (vm, small)] + wu,
        wide,
        flops=2 * count * width * 3072,
        size=12 << 20,
        smem=(0,),
        name="up",
    )
    hidden_other = hop(hidden_send, 2)
    output, d_sum, gd, sums_ffn = call(
        down_kernel,
        [((count, width), bf16), ((count, width), f32), ((count, width), bf16), ((8, width), f32)],
        [(vm, info), (vm, hidden), (vm, normed), (vm, grad_out), (vm, gain_ffn), (vm, shift_ffn)] + wd,
        wide + acc,
        flops=2 * count * width * 3072,
        size=14 << 20,
        smem=(0,),
        name="down",
    )

    steps = [1 << n for n in range(batch_count.bit_length() - 1)]
    down_order = steps[:2] + ["y"] + steps[2:]
    up_order = steps[1:2] + steps[:1] + ["y"] + steps[2:]

    def bit(step):
        return (batch // step) & 1

    def send(x, step):
        return hop(x, 1) if step == "y" else hop_batch(x, step)

    def chain(pieces, step):
        received = [send(pieces[0], step)]
        for piece in pieces[1:]:
            received.append(send(after(piece, received[-1]), step))
        return received

    def add_all(kept, received):
        return [(a.astype(f32) + b.astype(f32)).astype(bf16) for a, b in zip(kept, received)]

    def split_for(pieces, step):
        if step == "y":
            return pieces[:1], pieces[1:]
        rows = pieces[0].shape[0] // 2
        kept = [lax.dynamic_slice_in_dim(x, bit(step) * rows, rows, 0) for x in pieces]
        sent = [lax.dynamic_slice_in_dim(x, (1 - bit(step)) * rows, rows, 0) for x in pieces]
        if len(pieces) > 1:
            sent = [jnp.stack(sent)]
        return kept, sent

    def exchange(pieces, step):
        kept, sent = split_for(pieces, step)
        received = send(sent[0], step)
        return kept, [received] if received.ndim == 2 else [received[n] for n in range(len(kept))]

    def grow(x, step):
        other = hop_batch(x, step)
        mine_last = bit(step) == 1
        return jnp.concatenate([jnp.where(mine_last, other, x), jnp.where(mine_last, x, other)], axis=0)

    def rest_of(order, done):
        back = [step for step in order if step != "y"][::-1]
        return [lambda x, step=step: add_all(*exchange(x, step)) for step in order[done:]] + [
            lambda x, step=step: [grow(x[0], step)] for step in back
        ]

    du, du_send, sums_up = call(
        hidden_back_kernel,
        [((4, count, width), bf16), ((3, count, width), bf16), ((4, 8, width), f32)],
        [(vm, info), (vm, gd), (vm, slope)] + wd,
        wide,
        flops=2 * count * width * 3072,
        size=12 << 20,
        smem=(0,),
        name="hidden_back",
    )
    du_other = hop(du_send, 2)
    mine = jnp.stack([bit(down_order[0]), bit(up_order[0])])
    operands = (hidden, hidden_other, gd, du_other, du, normed_low)
    ((down_sent0, down_sent1, up_sent0, up_sent1),) = call_many([feed_grad(1 - mine, *operands)], "grad_sent")
    down_first = send(down_sent0, down_order[0])
    up_first = send(up_sent0, up_order[0])
    kept, (d_res, ga, sums_attn) = call_many(
        [
            feed_grad(mine, hidden, hidden_other, after(gd, down_sent0), du_other, du, normed_low),
            (
                residual_back_kernel,
                [((count, width), f32), ((count, width), bf16), ((8, width), f32)],
                [(vm, info), (vm, du), (vm, d_sum), (vm, pre), (vm, gain_attn)] + wu,
                wide + acc,
                (0,),
            ),
        ],
        "grad_kept",
    )
    down_kept, up_kept = kept[:2], kept[2:]
    ga, down_first, up_first = after((ga, down_first, up_first), d_res)
    ga_other = hop(ga, 2)
    ga_before, ga_behind = neighbours(ga, ga_other)
    down_second = send(after(down_sent1, down_first), down_order[0])
    up_second = send(after(up_sent1, up_first), up_order[0])
    dx, dq, dkl, dv_conv, dtaps = call(
        first_back_kernel,
        [
            ((4, 64, GROUP), f32),
            ((4, count, GROUP), bf16),
            ((4, 64, GROUP), f32),
            ((4, count, GROUP), f32),
            ((4, 8, GROUP), f32),
        ],
        [(vm, info), (vm, after(ga, down_first, up_first)), (vm, ga_before), (vm, ga_behind)]
        + wo
        + [(vm, lm), (vm, q), (vm, v), (vm, small), (vm, x_mid)],
        out_scratch + [pltpu.VMEM((ext, width), bf16), pltpu.VMEM((ext, GROUP), f32)],
        flops=int(5e9),
        size=10 << 20,
        smem=(0,),
        name="first_back",
    )

    def swap_core(x):
        other = hop(x, 2)
        return x.astype(f32) + jnp.concatenate([other[2:4], other[0:2]], axis=0).astype(f32)

    dx, down_second, up_second = after((dx, down_second, up_second), dtaps)
    dx = swap_core(after(dx, down_second, up_second))
    down_sent, up_sent = [down_first, down_second], [up_first, up_second]
    d_down = exchange(add_all(down_kept, down_sent), down_order[1])
    d_up = exchange(add_all(up_kept, up_sent), up_order[1])
    dx_across = hop(dx, 1)
    dx, dx_across, d_down, d_up = after((dx, dx_across, d_down, d_up), dx_across)
    d_down = exchange(add_all(*d_down), down_order[2])
    d_up = exchange(add_all(*d_up), up_order[2])
    dx, dx_across = after((dx, dx_across), d_down[0], d_up[0])
    joint, joint_send, partial = call(
        third_back_kernel,
        [((4, count, 3 * GROUP), bf16), ((2, count, 4 * GROUP), bf16), ((4, 64, 2 * GROUP), f32)],
        [(vm, info), (vm, dx), (vm, dx_across), (vm, lm), (vm, wst), (vm, k), (vm, v), (vm, dv_conv), (vm, dq)]
        + [(vm, dkl), (vm, ctx)],
        flops=int(5e9),
        size=8 << 20,
        smem=(0,),
        name="third_back",
    )
    joint_other = hop(after(joint_send, d_down[1], d_up[1]), 2)
    d_down, d_up = after((d_down, d_up), partial)
    d_down, d_up = add_all(*d_down), add_all(*d_up)
    operands = (after(joint, *d_down, *d_up), joint_other, ctx, tokens, tokens_other, ga, ga_other)
    sent = joint_grad(*operands, 1, "grad_joint_sent")
    joint_first = send(sent[0], "y")
    d_down, d_up = after((d_down, d_up), *sent)
    d_down, d_up = exchange(d_down, down_order[3]), exchange(d_up, up_order[3])
    (partial,) = call(
        inverse_back_kernel,
        [((4, 64, 2 * GROUP), bf16)],
        [(vm, dx), (vm, dx_across), (vm, wst), (vm, lm_own), (vm, iterates), (vm, after(partial, *sent))],
        flops=int(1e9),
        size=4 << 20,
        name="inverse_back",
    )
    partial = after(partial, joint_first, d_down[1], d_up[1])
    d_down, d_up = after((d_down, d_up), partial)
    d_down, d_up = add_all(*d_down), add_all(*d_up)
    partial = swap_core(partial).astype(bf16)
    partial_across = hop(partial, 1)
    down_rest, up_rest = rest_of(down_order, 4), rest_of(up_order, 4)
    if EARLY >= 1:
        d_down, d_up = down_rest[0](d_down), up_rest[0](d_up)
        partial, partial_across = after((partial, partial_across), partial_across, d_down[0], d_up[0])
        down_rest, up_rest = down_rest[1:], up_rest[1:]
    else:
        partial, partial_across = after((partial, partial_across), partial_across)
    joint_second = send(after(sent[1], partial_across), "y")
    joint_sent = [joint_first, joint_second]
    joint_kept = joint_grad(*after(operands, partial), 0, "grad_joint_kept")
    if EARLY >= 2:
        d_down, d_up = down_rest[0](d_down), up_rest[0](d_up)
        down_rest, up_rest = down_rest[1:], up_rest[1:]
    (d_tokens,) = call(
        token_back_kernel,
        [((count, width), f32)],
        [(vm, info), (vm, partial), (vm, partial_across), (vm, joint), (vm, d_res)] + [(an, w) for w in wt],
        [pltpu.VMEM((4, 3 * GROUP, width), bf16), pltpu.SemaphoreType.DMA((4, 3, 2))],
        flops=2 * count * width * 3072,
        size=10 << 20,
        smem=(0,),
        name="token_back",
    )
    landmark_own = (partial[0].astype(f32) + partial_across[1].astype(f32)).astype(bf16)
    low_rank = dot(landmark_own, pooled_low, TN)
    low_rank = jnp.concatenate([low_rank[0:192], low_rank[GROUP : GROUP + 192]], axis=0)
    d_first = (joint_kept[0].astype(f32) + joint_sent[0].astype(f32) + low_rank).astype(bf16)
    d_second = (joint_kept[1].astype(f32) + joint_sent[1].astype(f32)).astype(bf16)
    norms = jnp.concatenate([sums_attn[0:2], sums_ffn[0:2]], axis=0)
    dtaps = jnp.pad(dtaps[:, 1:4], ((0, 0), (0, 0), (0, width - GROUP)))
    minor = jnp.concatenate([sums_up[:, 0:1], dtaps, jnp.broadcast_to(norms, (4, 4, width))], axis=1)
    minor = after(minor, joint_second)
    minor = minor[0:2] + hop(minor[2:4], 2)
    minor = minor[0] + hop(minor[1], 1)
    orders = [steps, steps[1:2] + steps[:1] + steps[2:]]
    values = [[d_first], [d_second], d_down, d_up, [minor]]
    tasks = [
        rest_of(orders[0], 0),
        rest_of(orders[1], 0),
        down_rest,
        up_rest,
        [lambda x: x] * LATE + [lambda x, step=step: [x[0] + hop_batch(x[0], step)] for step in steps],
    ]
    for turn in range(max(len(task) for task in tasks)):
        anchors = (values[0][0], values[1][0]) + ((d_tokens,) if turn == 0 else ())
        values = [
            task[turn](after(value, *anchors)) if turn < len(task) else value for value, task in zip(values, tasks)
        ]
    d_parts = [values[0][0].astype(f32), values[1][0].astype(f32)]
    d_w_down, d_w_up = values[2][0].astype(f32), values[3][0].astype(f32)
    minor = values[4][0]
    d_w_query, d_w_key = d_parts[0][0:192].T, d_parts[0][192:384].T
    d_w_value, d_w_out = d_parts[1][0:192].T, d_parts[1][192:384]

    return (
        output[None],
        d_tokens[None],
        d_w_query,
        d_w_key,
        d_w_value,
        d_w_out,
        minor[1:4, 0:TAPS],
        d_w_up,
        minor[0],
        d_w_down,
        minor[4],
        minor[5],
        minor[6],
        minor[7],
    )


def solution(mesh):
    return jax.shard_map(
        functools.partial(local, mesh.shape["batch"]),
        mesh=mesh,
        in_specs=(
            P("batch", "head", None),
            P("batch"),
            P(None, "head"),
            P(None, "head"),
            P(None, "head"),
            P("head", None),
            P("head", None),
            P(None, "head"),
            P("head"),
            P("head", None),
            P(),
            P(),
            P(),
            P(),
            P("batch", "head", None),
        ),
        out_specs=(
            P("batch", "head", None),
            P("batch", "head", None),
            P(None, "head"),
            P(None, "head"),
            P(None, "head"),
            P("head", None),
            P("head", None),
            P(None, "head"),
            P("head"),
            P("head", None),
            P(),
            P(),
            P(),
            P(),
        ),
        check_vma=False,
    )
```

```python
import functools

import jax
import jax.numpy as jnp
from jax import lax
from jax.experimental import pallas as pl
from jax.experimental.pallas import tpu as pltpu
from jax.sharding import PartitionSpec as P

f32 = jnp.float32
bf16 = jnp.bfloat16
HEAD_DIM = 64
LANDMARKS = 64
NEWTON = 6
TAPS = 65
HALO = TAPS // 2
EARLY = 1
LATE = 0
IDLE = 1
GROUP = 256
NN = ((1,), (0,))
NT = ((1,), (1,))
TN = ((0,), (0,))
VMEM = pltpu.VMEM
ANY = pl.ANY


def dot(a, b, dims=NN):
    return lax.dot_general(a, b, (dims, ((), ())), preferred_element_type=f32)


def split(x):
    high = x.astype(bf16)
    return high, (x - high.astype(f32)).astype(bf16)


def mm(a, b, dims=NN):
    a_high, a_low = split(a)
    b_high, b_low = split(b)
    return dot(a_high, b_high, dims) + (dot(a_high, b_low, dims) + dot(a_low, b_high, dims))


def mm_left(a, b, dims=NN):
    a_high, a_low = split(a)
    return dot(a_high, b, dims) + dot(a_low, b, dims)


def iota(shape, dim):
    return lax.broadcasted_iota(jnp.int32, shape, dim)


def call(body, outs, ins, scratch=(), flops=0, size=0, limit=40, name=None, smem=()):
    specs = [
        pl.BlockSpec(memory_space=pltpu.SMEM) if i in smem else pl.BlockSpec(memory_space=space)
        for i, (space, _) in enumerate(ins)
    ]
    return pl.pallas_call(
        body,
        out_shape=[jax.ShapeDtypeStruct(s, d) for s, d in outs],
        in_specs=specs,
        out_specs=[pl.BlockSpec(memory_space=VMEM)] * len(outs),
        scratch_shapes=list(scratch),
        compiler_params=pltpu.CompilerParams(vmem_limit_bytes=limit << 20),
        cost_estimate=pl.CostEstimate(flops=flops, bytes_accessed=size, transcendentals=0),
        name=name,
    )(*[value for _, value in ins])


def call_many(parts, name):
    ins = [value for part in parts for value in part[2]]
    outs = [value for part in parts for value in part[1]]
    scratch = [value for part in parts for value in part[3]]
    smem, first = [], 0
    for part in parts:
        smem += [first + i for i in part[4]]
        first += len(part[2])

    def body(*refs):
        groups = [refs[: len(ins)], refs[len(ins) : len(ins) + len(outs)], refs[len(ins) + len(outs) :]]
        at = [0, 0, 0]
        for part in parts:
            mine = []
            for group, kind in ((0, 2), (1, 1), (2, 3)):
                mine += groups[group][at[group] : at[group] + len(part[kind])]
                at[group] += len(part[kind])
            part[0](*mine)

    results = call(body, outs, ins, scratch, flops=int(5e9), size=10 << 20, name=name, smem=tuple(smem), limit=48)
    split_results, first = [], 0
    for part in parts:
        split_results.append(results[first : first + len(part[1])])
        first += len(part[1])
    return split_results


def block_mask():
    return (iota((GROUP, GROUP), 0) >> 6) == (iota((GROUP, GROUP), 1) >> 6)


def spread(x):
    return jnp.where(block_mask(), jnp.concatenate([x, x, x, x], axis=0), 0.0)


def fold(x):
    kept = jnp.where(block_mask(), x, 0.0)
    return kept[0:64] + kept[64:128] + kept[128:192]


def rows_of(info, count, first):
    return info[1] + first + iota((count, 1), 0)


def landmark_kernel(p0, p1, p2, p3, wt, lm, pool, chain):
    pooled = (p0[...].astype(f32) + p1[...].astype(f32)) + (p2[...].astype(f32) + p3[...].astype(f32))
    pool[...] = pooled.astype(bf16)
    high, low = split(pooled)
    both = jnp.concatenate([high, low], axis=0)
    lm[...] = jnp.zeros_like(lm)
    matrices, starts = [], []
    for head in range(3):
        pair = []
        for kind in range(2):
            rows = wt[kind * 192 + head * 64 : kind * 192 + head * 64 + 64]
            out = dot(both, rows, NT)
            out = out[0:64] + out[64:128]
            lm[:, kind * GROUP + head * 64 : kind * GROUP + head * 64 + 64] = out
            pair.append(out)
        scores = mm(pair[0], pair[1], NT) * 0.125
        raised = jnp.exp(scores - jnp.max(scores, axis=1, keepdims=True))
        matrix = raised / jnp.sum(raised, axis=1, keepdims=True)
        column = jnp.max(jnp.sum(matrix, axis=0, keepdims=True), axis=1, keepdims=True)
        row = jnp.max(jnp.sum(matrix, axis=1, keepdims=True), axis=0, keepdims=True)
        matrices.append(matrix)
        starts.append(matrix.T / (column * row))
    eye = (iota((64, 64), 0) == iota((64, 64), 1)).astype(f32)

    def step(it, iterates):
        results = []
        for head in range(3):
            z = iterates[head]
            product = mm(matrices[head], z)
            inner1 = 7.0 * eye - product
            inner2 = 15.0 * eye - mm(product, inner1)
            inner3 = 13.0 * eye - mm(product, inner2)
            chain[it, 0, head] = z
            chain[it, 1, head] = product
            chain[it, 2, head] = inner2
            chain[it, 3, head] = inner3
            results.append(0.25 * mm(z, inner3))
        return tuple(results)

    finals = lax.fori_loop(0, NEWTON, step, tuple(starts))
    for head in range(3):
        lm[:, 2 * GROUP + head * 64 : 2 * GROUP + head * 64 + 64] = finals[head]


def inverse_back_kernel(x0, x1, wst_all, lm, chain, partial, out):
    total = x0[0] + x1[1]
    eye = (iota((64, 64), 0) == iota((64, 64), 1)).astype(f32)
    weight = wst_all[0]
    out[...] = partial[...].astype(bf16)
    grads, matrices, queries, keys = [], [], [], []
    for head in range(3):
        at = slice(head * 64, head * 64 + 64)
        grads.append(mm(total[:, at], weight[:, at], NT))
        query = lm[:, head * 64 : head * 64 + 64]
        key = lm[:, GROUP + head * 64 : GROUP + head * 64 + 64]
        scores = mm(query, key, NT) * 0.125
        raised = jnp.exp(scores - jnp.max(scores, axis=1, keepdims=True))
        matrices.append(raised / jnp.sum(raised, axis=1, keepdims=True))
        queries.append(query)
        keys.append(key)

    def step(count, carried):
        it = NEWTON - 1 - count
        results = []
        for head in range(3):
            dz_next, da = carried[2 * head], carried[2 * head + 1]
            z = chain[it, 0, head]
            product = chain[it, 1, head]
            inner1 = 7.0 * eye - product
            inner2 = chain[it, 2, head]
            inner3 = chain[it, 3, head]
            dz_next = 0.25 * dz_next
            dz = mm(dz_next, inner3, NT)
            d3 = -mm(z, dz_next, TN)
            d2 = -mm(product, d3, TN)
            d1 = mm(product, d2, TN)
            dp = mm(d3, inner2, NT) + mm(d2, inner1, NT) - d1
            da = da + mm(dp, z, NT)
            dz = dz + mm(matrices[head], dp, TN)
            results += [dz, da]
        return tuple(results)

    first = []
    for head in range(3):
        first += [grads[head], jnp.zeros((64, 64), f32)]
    last = lax.fori_loop(0, NEWTON, step, tuple(first))
    for head in range(3):
        dz, da = last[2 * head], last[2 * head + 1]
        matrix = matrices[head]
        columns = jnp.sum(matrix, axis=0, keepdims=True)
        rows = jnp.sum(matrix, axis=1, keepdims=True)
        column = jnp.max(columns, axis=1, keepdims=True)
        row = jnp.max(rows, axis=0, keepdims=True)
        scale = 1.0 / (column * row)
        da = da + dz.T * scale
        d_scale = -jnp.sum(jnp.sum(dz * matrix.T, axis=1, keepdims=True), axis=0, keepdims=True) * scale * scale
        column_hit = (columns == column).astype(f32)
        row_hit = (rows == row).astype(f32)
        da = da + d_scale * row * column_hit / jnp.sum(column_hit, axis=1, keepdims=True)
        da = da + d_scale * column * row_hit / jnp.sum(row_hit, axis=0, keepdims=True)
        ds = matrix * (da - jnp.sum(da * matrix, axis=1, keepdims=True)) * 0.125
        for at, value in ((head * 64, mm(ds, keys[head])), (GROUP + head * 64, mm(ds, queries[head], TN))):
            out[0, :, at : at + 64] = (partial[0, :, at : at + 64] + value).astype(bf16)


PROJECTION = ((0, 192, 0), (192, 192, GROUP), (384, 192, 2 * GROUP))


def split_copies(refs, parts, held, sems, side):
    own, across, across_x, other, both, both_x = refs
    half = own.shape[1] // 2
    mine = pl.ds(pl.multiple_of(side * half, half), half)
    rest = pl.ds(pl.multiple_of((1 - side) * half, half), half)
    blocks = [[], [], [], []]
    for n, (row, rows, to) in enumerate(parts):
        first = pl.ds(row - parts[0][0], rows)
        source, to = pl.ds(row, rows), pl.ds(to, rows)
        blocks[0].append(pltpu.make_async_copy(own.at[first], held.at[0, to], sems.at[0, n, 0]))
        blocks[2].append(pltpu.make_async_copy(other.at[source], held.at[2, to], sems.at[2, n, 0]))
        for i, near, far in ((1, across, across_x), (3, both, both_x)):
            blocks[i].append(pltpu.make_async_copy(near.at[source], held.at[i, to, mine], sems.at[i, n, 0]))
            blocks[i].append(pltpu.make_async_copy(far.at[source], held.at[i, to, rest], sems.at[i, n, 1]))
    return blocks


def start(copies):
    for block in copies:
        for copy in block:
            copy.start()


def wait(copies, i):
    for block in range(4):

        @pl.when(i == block)
        def _():
            for copy in copies[block]:
                copy.wait()


def zero_gaps(held, kinds):
    for i in range(4):
        for kind in range(kinds):
            held[i, kind * GROUP + 192 : kind * GROUP + 256, :] = jnp.zeros((64, held.shape[2]), bf16)


def project_kernel(info, tokens, before, after, w0, w1, w2, w3, w4, w5, q_out, k_out, v_out, held, sems):
    count = tokens.shape[0]
    copies = split_copies((w0, w1, w2, w3, w4, w5), PROJECTION, held, sems, info[2])
    start(copies)
    zero_gaps(held, 3)
    valid = (rows_of(info, count, 0) < info[0]).astype(f32)
    valid_before = (rows_of(info, HALO, -HALO) < info[0]).astype(f32)
    valid_after = (rows_of(info, HALO, count) < info[0]).astype(f32)

    def body(i, _):
        wait(copies, i)
        for kind, out in ((0, q_out), (1, k_out)):
            out[i] = (dot(tokens[...], held[i, kind * GROUP : kind * GROUP + GROUP], NT) * valid).astype(bf16)
        wv = held[i, 2 * GROUP : 3 * GROUP]
        v_out[i, HALO : HALO + count] = (dot(tokens[...], wv, NT) * valid).astype(bf16)
        v_out[i, 0:HALO] = (dot(before[...], wv, NT) * valid_before).astype(bf16)
        v_out[i, HALO + count : 2 * HALO + count] = (dot(after[...], wv, NT) * valid_after).astype(bf16)
        v_out[i, 2 * HALO + count :] = jnp.zeros((v_out.shape[1] - 2 * HALO - count, GROUP), bf16)
        return 0

    lax.fori_loop(0, 4, body, 0)


def third_scores(info, lm, k_ref, i):
    count = k_ref.shape[1]
    valid = info[1] + iota((1, count), 1) < info[0]
    queries = spread(lm[i, :, 0:GROUP])
    return jnp.where(valid, mm_left(queries, k_ref[i], NT) * 0.125, -1e30)


def third_kernel(info, lm, k_ref, v_ref, pay):
    count = k_ref.shape[1]
    lane = iota((64, GROUP), 1)

    def body(i, _):
        scores = third_scores(info, lm, k_ref, i)
        top = jnp.max(scores, axis=1, keepdims=True)
        raised = jnp.exp(scores - top)
        total = jnp.sum(raised, axis=1, keepdims=True)
        packed = fold(mm_left(raised, v_ref[i, HALO : HALO + count]) / total)
        for stat, base in ((top, 192), (total, 216)):
            for term in range(3):
                part = stat.astype(bf16).astype(f32)
                stat = stat - part
                for head in range(3):
                    packed = jnp.where(lane == base + 8 * term + head, part[head * 64 : head * 64 + 64], packed)
        pay[i] = packed.astype(bf16)
        return 0

    lax.fori_loop(0, 4, body, 0)


def first_scores(lm, q_ref, i):
    keys = spread(lm[i, :, GROUP : 2 * GROUP])
    count = q_ref.shape[1]
    scores = (mm_left(keys, q_ref[i], NT) * 0.125).reshape(4, 64, count)
    raised = jnp.exp(scores - jnp.max(scores, axis=1, keepdims=True))
    return raised / jnp.sum(raised, axis=1, keepdims=True)


def toeplitz(row):
    return pltpu.roll(jnp.broadcast_to(row, (128, GROUP)), 0, 1, stride=1, stride_axis=0)


def head_select(x, rows):
    lane = iota((rows, GROUP), 1) >> 6
    out = jnp.where(lane == 0, x[0:rows], 0.0)
    out = jnp.where(lane == 1, x[rows : 2 * rows], out)
    return jnp.where(lane == 2, x[2 * rows : 3 * rows], out)


def context_kernel(p0, p1, p2, p3, lm, q_ref, v_ref, small, ctx, wst, x_out):
    count = q_ref.shape[1]
    lane = iota((64, GROUP), 1)

    def body(i, _):
        parts = [p[i ^ n].astype(f32) for n, p in enumerate((p0, p1, p2, p3))]

        def stat(part, at):
            return part[:, at : at + 1] + part[:, at + 8 : at + 9] + part[:, at + 16 : at + 17]

        factors = [jnp.zeros((64, GROUP), f32) for _ in range(4)]
        stats = jnp.zeros((64, GROUP), f32)
        for head in range(3):
            tops = [stat(part, 192 + head) for part in parts]
            top = jnp.maximum(jnp.maximum(tops[0], tops[1]), jnp.maximum(tops[2], tops[3]))
            scales = [stat(part, 216 + head) * jnp.exp(t - top) for part, t in zip(parts, tops)]
            total = sum(scales)
            mine = (lane >> 6) == head
            factors = [jnp.where(mine, s / total, f) for s, f in zip(scales, factors)]
            stats = jnp.where(lane == 192 + head, top, stats)
            stats = jnp.where(lane == 196 + head, total, stats)
        weight = sum(part * f for part, f in zip(parts, factors))
        wst[i] = jnp.where(lane < 192, weight, stats)
        mixed = mm(spread(lm[i, :, 2 * GROUP : 3 * GROUP]), spread(weight))
        x_out[i] = fold(mixed)
        first = first_scores(lm, q_ref, i).reshape(GROUP, count)
        main = mm(first, mixed, TN)
        bands = [toeplitz(small[i, 1 + head : 2 + head, 0:GROUP]) for head in range(3)]
        high, low = split(jnp.concatenate(bands, axis=0))
        for block in range(count // 128):
            window = v_ref[i, block * 128 : block * 128 + 256]
            conv = dot(high, window) + dot(low, window)
            ctx[i, block * 128 : block * 128 + 128] = (
                main[block * 128 : block * 128 + 128] + head_select(conv, 128)
            ).astype(bf16)
        return 0

    lax.fori_loop(0, 4, body, 0)


def first_back_kernel(
    info, g_ref, before, after, o0, o1, o2, o3, o4, o5, lm, q_ref, v_ref, small, x_in, dx, dq, dkl, dv, dtaps, held, sems, ext, dctx
):
    count = g_ref.shape[0]
    width = g_ref.shape[1]
    copies = split_copies((o0, o1, o2, o3, o4, o5), ((0, 192, 0),), held, sems, info[2])
    start(copies)
    zero_gaps(held, 1)
    valid = (rows_of(info, count, 0) < info[0]).astype(f32)
    ext[0:HALO] = before[...]
    ext[HALO : HALO + count] = g_ref[...]
    ext[HALO + count : 2 * HALO + count] = after[...]
    ext[2 * HALO + count :] = jnp.zeros((ext.shape[0] - 2 * HALO - count, width), bf16)
    lane = iota((128, GROUP), 1) >> 6
    flip = (iota((128, 128), 0) + iota((128, 128), 1) == 127).astype(bf16)

    def body(i, _):
        wait(copies, i)
        dctx[...] = dot(ext[...], held[i], NT)
        own = dctx[HALO : HALO + count]
        own_high = own.astype(bf16)
        first = first_scores(lm, q_ref, i)
        flat = first.reshape(GROUP, count)
        dx[i] = fold(dot(flat.astype(bf16), own_high))
        dfirst = dot(spread(x_in[i]).astype(bf16), own_high, NT)
        dfirst = dfirst.reshape(4, 64, count)
        ds = first * (dfirst - jnp.sum(first * dfirst, axis=1, keepdims=True)) * 0.125
        ds = ds.reshape(GROUP, count).astype(bf16)
        keys = (spread(lm[i, :, GROUP : 2 * GROUP])).astype(bf16)
        dquery = dot(ds, keys, TN)
        dq[i] = (dquery * valid).astype(bf16)
        dkl[i] = fold(dot(ds, q_ref[i]))
        bands = [toeplitz(small[i, 4 + head : 5 + head, 0:GROUP]) for head in range(3)]
        high = jnp.concatenate(bands, axis=0).astype(bf16)
        gram = jnp.zeros((384, GROUP), f32)
        for block in range(count // 128):
            conv = dot(high, dctx[block * 128 : block * 128 + 256].astype(bf16))
            dv[i, block * 128 : block * 128 + 128] = head_select(conv, 128)
            piece = dctx[HALO + block * 128 : HALO + block * 128 + 128]
            stacked = jnp.concatenate([jnp.where(lane == head, piece, 0.0) for head in range(3)], axis=0)
            gram = gram + dot(stacked.astype(bf16), v_ref[i, block * 128 : block * 128 + 256], NT)
        dtaps[i] = jnp.zeros((8, GROUP), f32)
        for head in range(3):
            part_high, part_low = split(gram[head * 128 : head * 128 + 128])
            upturned = dot(flip, part_high) + dot(flip, part_low)
            straight = pltpu.roll(upturned, GROUP - 127, 1, stride=1, stride_axis=0)
            summed = jnp.sum(straight, axis=0, keepdims=True)
            dtaps[i, 1 + head : 2 + head, :] = jnp.where(iota((1, GROUP), 1) < TAPS, summed, 0.0)
        return 0

    lax.fori_loop(0, 4, body, 0)


def third_back_kernel(info, x0, x1, lm, wst, k_ref, v_ref, dvc, dq, dkl, ctx, joint, send, partial):
    count = k_ref.shape[1]
    valid = (rows_of(info, count, 0) < info[0]).astype(f32)
    none = jnp.zeros((64, 1), f32)

    def body(i, _):
        dx = spread(x0[i] + x1[i ^ 1])
        dweight = mm(spread(lm[i, :, 2 * GROUP : 3 * GROUP]), dx, TN)
        stats = wst[i]
        weight = spread(jnp.where(iota((64, GROUP), 1) < 192, stats, 0.0))
        inner = jnp.sum(dweight * weight, axis=1, keepdims=True)
        top = jnp.concatenate([stats[:, 192 + head : 193 + head] for head in range(3)] + [none], axis=0)
        total = jnp.concatenate([stats[:, 196 + head : 197 + head] for head in range(3)] + [none + 1.0], axis=0)
        scores = third_scores(info, lm, k_ref, i)
        third = jnp.exp(scores - top) / total
        dw_high = dweight.astype(bf16)
        values = v_ref[i, HALO : HALO + count]
        dthird = dot(dw_high, values, NT)
        ds = (third * (dthird - inner) * 0.125).astype(bf16)
        queries = (spread(lm[i, :, 0:GROUP])).astype(bf16)
        dkey = dot(ds, queries, TN)
        partial[i, :, 0:GROUP] = fold(dot(ds, k_ref[i]))
        partial[i, :, GROUP : 2 * GROUP] = dkl[i]
        dvalues = dot(third.astype(bf16), dw_high, TN)
        joint[i, :, 0:GROUP] = dq[i]
        joint[i, :, GROUP : 2 * GROUP] = (dkey * valid).astype(bf16)
        joint[i, :, 2 * GROUP : 3 * GROUP] = ((dvalues + dvc[i]) * valid).astype(bf16)

        @pl.when(i >= 2)
        def _():
            send[i - 2, :, 0 : 3 * GROUP] = joint[i]
            send[i - 2, :, 3 * GROUP : 4 * GROUP] = ctx[i]

        return 0

    lax.fori_loop(0, 4, body, 0)


def token_back_kernel(info, l0, l1, joint, dres, w0, w1, w2, w3, w4, w5, out, held, sems):
    copies = split_copies((w0, w1, w2, w3, w4, w5), PROJECTION, held, sems, info[2])
    start(copies)
    zero_gaps(held, 3)
    count = joint.shape[1]
    mark = iota((1, 64), 1)
    low = (mark * info[0]) >> 6
    high = ((mark + 1) * info[0]) >> 6
    pos = rows_of(info, count, 0)
    member = ((pos >= low) & (pos < high)).astype(bf16)
    row = iota((64, 1), 0)
    width = ((((row + 1) * info[0]) >> 6) - ((row * info[0]) >> 6)).astype(f32)
    out[...] = dres[...]

    def body(i, pooled):
        wait(copies, i)
        out[...] += dot(joint[i], held[i])
        marks = (l0[i].astype(f32) + l1[i ^ 1].astype(f32)) / width
        return pooled + mm_left(marks, held[i, 0 : 2 * GROUP])

    pooled = lax.fori_loop(0, 4, body, jnp.zeros((64, out.shape[1]), f32))
    pooled_high, pooled_low = split(pooled)
    out[...] += dot(member, pooled_high) + dot(member, pooled_low)


def moments(x):
    centered = x - jnp.mean(x, axis=-1, keepdims=True)
    variance = jnp.mean(centered * centered, axis=-1, keepdims=True)
    inverse = lax.rsqrt(variance + 1e-05)
    return centered * inverse, inverse


def attended_kernel(info, ctx, tokens, gain, shift, o0, o1, o2, o3, o4, o5, pre, normed, low, held, sems):
    copies = split_copies((o0, o1, o2, o3, o4, o5), ((0, 192, 0),), held, sems, info[2])
    start(copies)
    zero_gaps(held, 1)
    pre[...] = tokens[...].astype(f32)

    def body(i, _):
        wait(copies, i)
        pre[...] += dot(ctx[i], held[i])
        return 0

    lax.fori_loop(0, 4, body, 0)
    unit, _ = moments(pre[...])
    result = unit * gain[...] + shift[...]
    normed[...] = result
    low[...] = result.astype(bf16)


def gelu_parts(u):
    cdf = 0.5 + 0.5 * lax.erf(u * 0.7071067811865476)
    pdf = jnp.exp(u * u * -0.5) * 0.3989422804014327
    return u * cdf, cdf + u * pdf


def up_kernel(info, low, small, w0, w1, w2, w3, w4, w5, hidden, slope, send, held, sems):
    copies = split_copies((w0, w1, w2, w3, w4, w5), ((192, held.shape[1], 0),), held, sems, info[2])
    start(copies)

    def body(i, _):
        wait(copies, i)
        for chunk in range(3):
            at = slice(chunk * 256, chunk * 256 + 256)
            upward = dot(low[...], held[i, :, at]) + small[i, 0:1, at]
            value, derivative = gelu_parts(upward)
            hidden[i, :, at] = value.astype(bf16)
            slope[i, :, at] = derivative.astype(bf16)

        @pl.when(i >= 2)
        def _():
            send[i - 2] = hidden[i]

        return 0

    send[2] = low[...]
    lax.fori_loop(0, 4, body, 0)


def norm_back(g, gain, unit, inverse):
    scaled = g * gain
    mean1 = jnp.mean(scaled, axis=-1, keepdims=True)
    mean2 = jnp.mean(scaled * unit, axis=-1, keepdims=True)
    return (scaled - mean1 - unit * mean2) * inverse


def down_kernel(info, hidden, normed, grad, gain, shift, w0, w1, w2, w3, w4, w5, out, dsum, dlow, sums, held, sems, acc):
    copies = split_copies((w0, w1, w2, w3, w4, w5), ((0, held.shape[1], 0),), held, sems, info[2])
    start(copies)
    acc[...] = normed[...]

    def body(i, _):
        wait(copies, i)
        acc[...] += dot(hidden[i], held[i])
        return 0

    lax.fori_loop(0, 4, body, 0)
    unit, inverse = moments(acc[...])
    out[...] = (unit * gain[...] + shift[...]).astype(bf16)
    g = grad[...].astype(f32)
    back = norm_back(g, gain[...], unit, inverse)
    dsum[...] = back
    dlow[...] = back.astype(bf16)
    sums[...] = jnp.zeros_like(sums)
    sums[0:1] = jnp.sum(g * unit, axis=0, keepdims=True)
    sums[1:2] = jnp.sum(g, axis=0, keepdims=True)


def hidden_back_kernel(info, dlow, slope, w0, w1, w2, w3, w4, w5, du, send, sums, held, sems):
    copies = split_copies((w0, w1, w2, w3, w4, w5), ((0, held.shape[1], 0),), held, sems, info[2])
    start(copies)
    sums[...] = jnp.zeros_like(sums)

    def body(i, _):
        wait(copies, i)
        for chunk in range(3):
            at = slice(chunk * 256, chunk * 256 + 256)
            back = dot(dlow[...], held[i, at, :], NT) * slope[i, :, at].astype(f32)
            back = back.astype(bf16)
            du[i, :, at] = back
            sums[i, 0:1, at] = jnp.sum(back.astype(f32), axis=0, keepdims=True)

        @pl.when(i >= 2)
        def _():
            send[i - 2] = du[i]

        return 0

    send[2] = dlow[...]
    lax.fori_loop(0, 4, body, 0)


def residual_back_kernel(info, du, dsum, pre, gain, w0, w1, w2, w3, w4, w5, dres, dlow, sums, held, sems, acc):
    copies = split_copies((w0, w1, w2, w3, w4, w5), ((192, held.shape[1], 0),), held, sems, info[2])
    start(copies)
    acc[...] = dsum[...]

    def body(i, _):
        wait(copies, i)
        acc[...] += dot(du[i], held[i], NT)
        return 0

    lax.fori_loop(0, 4, body, 0)
    unit, inverse = moments(pre[...])
    g = acc[...]
    back = norm_back(g, gain[...], unit, inverse)
    dres[...] = back
    dlow[...] = back.astype(bf16)
    sums[...] = jnp.zeros_like(sums)
    sums[0:1] = jnp.sum(g * unit, axis=0, keepdims=True)
    sums[1:2] = jnp.sum(g, axis=0, keepdims=True)


def feed_grad_kernel(
    pick, hidden, hidden_other, gd, du_other, du, low, down0, down1, up0, up1, left, right, sems
):
    half = left.shape[-1]
    copies = []

    def bring(source, target):
        copy = pltpu.make_async_copy(source, target, sems.at[len(copies)])
        copy.start()
        copies.append(copy)

    for part, sources in ((0, (hidden.at[0], hidden_other.at[0], hidden.at[1], hidden_other.at[1])), (1, (low, hidden_other.at[2]))):
        columns = pl.ds(pl.multiple_of(pick[part] * half, half), half)
        for n, source in enumerate(sources):
            bring(source.at[:, columns], left.at[4 * part + n])
        if part == 0:
            bring(gd, right.at[0])
            bring(du_other.at[2], right.at[1])
        else:
            for j in range(2):
                bring(du.at[j], right.at[2 + 2 * j])
                bring(du_other.at[j], right.at[3 + 2 * j])
    for copy in copies[:6]:
        copy.wait()

    def body(n, _):
        @pl.when(n == 2)
        def _():
            for copy in copies[6:]:
                copy.wait()

        down = n < 2
        at_left = jnp.where(down, 2 * n, 4)
        at_right = jnp.where(down, 0, 2 * n - 2)
        total = dot(left[at_left], right[at_right], TN) + dot(left[at_left + 1], right[at_right + 1], TN)
        total = total.astype(bf16)
        for k, out in enumerate((down0, down1, up0, up1)):

            @pl.when(n == k)
            def _():
                out[...] = total

        return 0

    lax.fori_loop(0, 4, body, 0)


def feed_grad(pick, hidden, hidden_other, gd, du_other, du, low):
    count, width = gd.shape
    return (
        feed_grad_kernel,
        [((width // 2, width), bf16)] * 4,
        [(VMEM, pick.astype(jnp.int32))] + [(ANY, x) for x in (hidden, hidden_other, gd, du_other, du, low)],
        [
            pltpu.VMEM((6, count, width // 2), bf16),
            pltpu.VMEM((6, count, width), bf16),
            pltpu.SemaphoreType.DMA((12,)),
        ],
        (0,),
    )


def joint_grad_kernel(joint, other, ctx, tokens, tokens_other, g, g_other, first, second):
    def body(kind, _):
        at = pl.ds(pl.multiple_of(kind * GROUP, GROUP), GROUP)
        total = dot(joint[0, :, at], tokens[...], TN) + dot(other[0, :, at], tokens_other[...], TN)
        total = total[0:192].astype(bf16)

        @pl.when(kind < 2)
        def _():
            first[pl.ds(pl.multiple_of(kind * 192, 192), 192)] = total

        @pl.when(kind == 2)
        def _():
            second[0:192] = total

        return 0

    lax.fori_loop(0, 3, body, 0)
    total = dot(ctx[0], g[...], TN) + dot(other[0, :, 3 * GROUP : 4 * GROUP], g_other[...], TN)
    second[192:384] = total[0:192].astype(bf16)


def joint_grad(joint, other, ctx, tokens, tokens_other, g, g_other, block, name):
    count, width = tokens.shape
    whole = pl.BlockSpec((count, width), lambda j: (0, 0))
    return pl.pallas_call(
        joint_grad_kernel,
        grid=(1,),
        out_shape=[jax.ShapeDtypeStruct((width // 2, width), bf16)] * 2,
        in_specs=[
            pl.BlockSpec((1, count, 3 * GROUP), lambda j: (block, 0, 0)),
            pl.BlockSpec((1, count, 4 * GROUP), lambda j: (block, 0, 0)),
            pl.BlockSpec((1, count, GROUP), lambda j: (block, 0, 0)),
            whole,
            whole,
            whole,
            whole,
        ],
        out_specs=[pl.BlockSpec((width // 2, width), lambda j: (0, 0))] * 2,
        compiler_params=pltpu.CompilerParams(vmem_limit_bytes=40 << 20),
        cost_estimate=pl.CostEstimate(flops=16 * count * GROUP * width, bytes_accessed=8 << 20, transcendentals=0),
        name=name,
    )(joint, other, ctx, tokens, tokens_other, g, g_other)


HOP = {1: 2, 2: 1, 3: 3}


def hop(x, step):
    return lax.ppermute(x, "head", [(i, i ^ HOP[step]) for i in range(4)])


def after(x, *deps):
    return lax.optimization_barrier((x,) + deps)[0]


def local(
    batch_count,
    tokens,
    lengths,
    w_query,
    w_key,
    w_value,
    w_out,
    conv_taps,
    w_up,
    b_up,
    w_down,
    gain_attn,
    shift_attn,
    gain_ffn,
    shift_ffn,
    grad_out,
):
    tokens = tokens[0]
    grad_out = grad_out[0]
    count, width = tokens.shape
    ext = count + 128
    length = lengths[0]
    place = lax.axis_index("head")
    batch = lax.axis_index("batch")
    core = place & 1
    side = batch & 1
    info = jnp.stack([length, place * count, side]).astype(jnp.int32)
    gain_attn, shift_attn, gain_ffn, shift_ffn = (
        x.reshape(1, width) for x in (gain_attn, shift_attn, gain_ffn, shift_ffn)
    )
    vm, an = VMEM, ANY

    def hop_batch(x, step):
        return lax.ppermute(x, "batch", [(i, i ^ step) for i in range(batch_count)])

    def neighbours(x, other):
        first = core == 0
        far = lax.ppermute(jnp.where(first, x[:HALO], x[-HALO:]), "head", [(1, 2), (2, 1)])
        return jnp.where(first, far, other[-HALO:]), jnp.where(first, other[:HALO], far)

    marks = jnp.arange(LANDMARKS + 1, dtype=jnp.int32) * length // LANDMARKS
    positions = info[1] + jnp.arange(count, dtype=jnp.int32)
    member = (positions[None, :] >= marks[:-1, None]) & (positions[None, :] < marks[1:, None])
    pooled = jnp.dot(member.astype(bf16), tokens, preferred_element_type=f32)
    pooled = (pooled / (marks[1:] - marks[:-1]).astype(f32)[:, None]).astype(bf16)
    pools = [pooled] + [hop(pooled, n) for n in (1, 2, 3)]

    taps = jnp.pad(conv_taps, ((0, 0), (0, width - TAPS)))
    taps_back = jnp.pad(conv_taps[:, ::-1], ((0, 0), (0, width - TAPS)))
    small_own = jnp.concatenate([b_up[None], taps, taps_back, jnp.zeros((1, width), f32)], axis=0)
    term1 = small_own.astype(bf16)
    rest = small_own - lax.reduce_precision(small_own, 8, 7)
    term2 = rest.astype(bf16)
    term3 = (rest - lax.reduce_precision(rest, 8, 7)).astype(bf16)
    wt_own = jnp.concatenate(
        [w_query.T, w_key.T, w_value.T, term1, term2, term3, jnp.zeros((8, width), bf16)], axis=0
    )
    tokens_other = hop(tokens, 2)
    before, behind = neighbours(tokens, tokens_other)

    def column_half(own):
        return lax.dynamic_slice_in_dim(own, side * (width // 2), width // 2, 1)

    wt_other = hop(wt_own, 2)
    wt_across = hop(after(column_half(wt_own), *pools), 1)
    lm_own, pooled_low, iterates = call(
        landmark_kernel,
        [((64, 3 * GROUP), f32), ((64, width), bf16), ((NEWTON, 4, 3, 64, 64), f32)],
        [(vm, x) for x in pools] + [(vm, wt_own)],
        flops=int(1e9),
        size=4 << 20,
        name="landmarks",
    )
    lm_own = after(lm_own, wt_across, before, behind)
    lm_across = hop(lm_own, 1)
    wt_across_x = hop_batch(after(wt_across, pooled_low), 1)
    lm = jnp.stack([lm_own, lm_across, hop(lm_own, 2), hop(lm_across, 2)])
    wt = [wt_own, wt_across, wt_across_x, wt_other, hop(wt_across, 2), hop(wt_across_x, 2)]

    def small_of(block):
        return sum(block[576 + 8 * n : 584 + 8 * n].astype(f32) for n in range(3))

    def small_joined(near, far):
        near, far = small_of(near), small_of(far)
        first = side == 0
        return jnp.concatenate([jnp.where(first, near, far), jnp.where(first, far, near)], axis=1)

    small = jnp.stack(
        [small_of(wt[0]), small_joined(wt[1], wt[2]), small_of(wt[3]), small_joined(wt[4], wt[5])]
    )
    out_up_own = jnp.concatenate([w_out, after(w_up, pooled)], axis=0)
    out_up_across = hop(after(column_half(out_up_own), lm_across), 1)
    down_across = hop(after(column_half(w_down), lm_across), 1)
    q, k, v = call(
        project_kernel,
        [((4, count, GROUP), bf16), ((4, count, GROUP), bf16), ((4, ext, GROUP), bf16)],
        [(vm, info), (vm, tokens), (vm, before), (vm, behind)] + [(an, w) for w in wt],
        [pltpu.VMEM((4, 3 * GROUP, width), bf16), pltpu.SemaphoreType.DMA((4, 3, 2))],
        flops=2 * count * width * 3072,
        size=8 << 20,
        smem=(0,),
        name="project",
    )
    out_up_across_x = hop_batch(after(out_up_across, q), 1)
    (pay,) = call(
        third_kernel,
        [((4, 64, GROUP), bf16)],
        [(vm, info), (vm, lm), (vm, k), (vm, v)],
        flops=int(1e9),
        size=3 << 20,
        smem=(0,),
        name="third",
    )
    pays = [pay, hop(pay, 1), hop(pay, 2), hop(pay, 3)]
    ctx, wst, x_mid = call(
        context_kernel,
        [((4, count, GROUP), bf16), ((4, 64, GROUP), f32), ((4, 64, GROUP), f32)],
        [(vm, p) for p in pays] + [(vm, lm), (vm, q), (vm, v), (vm, small)],
        flops=int(3e9),
        size=5 << 20,
        name="context",
    )
    out_up_far = after((out_up_across, out_up_across_x), ctx)
    out_up = [out_up_across, out_up_across_x, hop(after(out_up_own, q), 2), hop(out_up_far[0], 2), hop(out_up_far[1], 2)]
    down_across_x = hop_batch(after(down_across, ctx), 1)
    wo = [(an, w) for w in [w_out] + out_up]
    wu = [(an, w) for w in [w_up] + out_up]
    out_scratch = [pltpu.VMEM((4, GROUP, width), bf16), pltpu.SemaphoreType.DMA((4, 1, 2))]
    wide = [pltpu.VMEM((4, width, width), bf16), pltpu.SemaphoreType.DMA((4, 1, 2))]
    acc = [pltpu.VMEM((count, width), f32)]

    pre, normed, normed_low = call(
        attended_kernel,
        [((count, width), f32), ((count, width), f32), ((count, width), bf16)],
        [(vm, info), (vm, ctx), (vm, tokens), (vm, gain_attn), (vm, shift_attn)] + wo,
        out_scratch,
        flops=2 * count * width * width,
        size=6 << 20,
        smem=(0,),
        name="attended",
    )
    down_far = after((down_across, down_across_x), normed_low)
    down = [down_across, down_across_x, hop(after(w_down, ctx), 2), hop(down_far[0], 2), hop(down_far[1], 2)]
    wd = [(an, w) for w in [w_down] + down]
    hidden, slope, hidden_send = call(
        up_kernel,
        [((4, count, width), bf16), ((4, count, width), bf16), ((3, count, width), bf16)],
        [(vm, info), (vm, normed_low), (vm, small)] + wu,
        wide,
        flops=2 * count * width * 3072,
        size=12 << 20,
        smem=(0,),
        name="up",
    )
    hidden_other = hop(hidden_send, 2)
    output, d_sum, gd, sums_ffn = call(
        down_kernel,
        [((count, width), bf16), ((count, width), f32), ((count, width), bf16), ((8, width), f32)],
        [(vm, info), (vm, hidden), (vm, normed), (vm, grad_out), (vm, gain_ffn), (vm, shift_ffn)] + wd,
        wide + acc,
        flops=2 * count * width * 3072,
        size=14 << 20,
        smem=(0,),
        name="down",
    )

    steps = [1 << n for n in range(batch_count.bit_length() - 1)]
    down_order = steps[:2] + ["y"] + steps[2:]
    up_order = steps[1:2] + steps[:1] + ["y"] + steps[2:]

    def bit(step):
        return (batch // step) & 1

    def send(x, step):
        return hop(x, 1) if step == "y" else hop_batch(x, step)

    def chain(pieces, step):
        received = [send(pieces[0], step)]
        for piece in pieces[1:]:
            received.append(send(after(piece, received[-1]), step))
        return received

    def add_all(kept, received):
        return [(a.astype(f32) + b.astype(f32)).astype(bf16) for a, b in zip(kept, received)]

    def split_for(pieces, step):
        if step == "y":
            return pieces[:1], pieces[1:]
        rows = pieces[0].shape[0] // 2
        kept = [lax.dynamic_slice_in_dim(x, bit(step) * rows, rows, 0) for x in pieces]
        sent = [lax.dynamic_slice_in_dim(x, (1 - bit(step)) * rows, rows, 0) for x in pieces]
        if len(pieces) > 1:
            sent = [jnp.stack(sent)]
        return kept, sent

    def exchange(pieces, step):
        kept, sent = split_for(pieces, step)
        received = send(sent[0], step)
        return kept, [received] if received.ndim == 2 else [received[n] for n in range(len(kept))]

    def grow(x, step):
        other = hop_batch(x, step)
        mine_last = bit(step) == 1
        return jnp.concatenate([jnp.where(mine_last, other, x), jnp.where(mine_last, x, other)], axis=0)

    def grow_first(x, step):
        return [x[0], hop_batch(x[0][: x[0].shape[0] // 2], step)]

    def grow_second(x, step):
        own, other = x
        other = jnp.concatenate([other, hop_batch(own[own.shape[0] // 2 :], step)], axis=0)
        mine_last = bit(step) == 1
        return [jnp.concatenate([jnp.where(mine_last, other, own), jnp.where(mine_last, own, other)], axis=0)]

    def in_two(task, order):
        return task[:-1] + [lambda x: x] * IDLE + [lambda x: grow_first(x, order[0]), lambda x: grow_second(x, order[0])]

    def rest_of(order, done):
        back = [step for step in order if step != "y"][::-1]
        return [lambda x, step=step: add_all(*exchange(x, step)) for step in order[done:]] + [
            lambda x, step=step: [grow(x[0], step)] for step in back
        ]

    du, du_send, sums_up = call(
        hidden_back_kernel,
        [((4, count, width), bf16), ((3, count, width), bf16), ((4, 8, width), f32)],
        [(vm, info), (vm, gd), (vm, slope)] + wd,
        wide,
        flops=2 * count * width * 3072,
        size=12 << 20,
        smem=(0,),
        name="hidden_back",
    )
    du_other = hop(du_send, 2)
    mine = jnp.stack([bit(down_order[0]), bit(up_order[0])])
    operands = (hidden, hidden_other, gd, du_other, du, normed_low)
    ((down_sent0, down_sent1, up_sent0, up_sent1),) = call_many([feed_grad(1 - mine, *operands)], "grad_sent")
    down_first = send(down_sent0, down_order[0])
    up_first = send(up_sent0, up_order[0])
    kept, (d_res, ga, sums_attn) = call_many(
        [
            feed_grad(mine, hidden, hidden_other, after(gd, down_sent0), du_other, du, normed_low),
            (
                residual_back_kernel,
                [((count, width), f32), ((count, width), bf16), ((8, width), f32)],
                [(vm, info), (vm, du), (vm, d_sum), (vm, pre), (vm, gain_attn)] + wu,
                wide + acc,
                (0,),
            ),
        ],
        "grad_kept",
    )
    down_kept, up_kept = kept[:2], kept[2:]
    ga, down_first, up_first = after((ga, down_first, up_first), d_res)
    ga_other = hop(ga, 2)
    ga_before, ga_behind = neighbours(ga, ga_other)
    down_second = send(after(down_sent1, down_first), down_order[0])
    up_second = send(after(up_sent1, up_first), up_order[0])
    dx, dq, dkl, dv_conv, dtaps = call(
        first_back_kernel,
        [
            ((4, 64, GROUP), f32),
            ((4, count, GROUP), bf16),
            ((4, 64, GROUP), f32),
            ((4, count, GROUP), f32),
            ((4, 8, GROUP), f32),
        ],
        [(vm, info), (vm, after(ga, down_first, up_first)), (vm, ga_before), (vm, ga_behind)]
        + wo
        + [(vm, lm), (vm, q), (vm, v), (vm, small), (vm, x_mid)],
        out_scratch + [pltpu.VMEM((ext, width), bf16), pltpu.VMEM((ext, GROUP), f32)],
        flops=int(5e9),
        size=10 << 20,
        smem=(0,),
        name="first_back",
    )

    def swap_core(x):
        other = hop(x, 2)
        return x.astype(f32) + jnp.concatenate([other[2:4], other[0:2]], axis=0).astype(f32)

    dx, down_second, up_second = after((dx, down_second, up_second), dtaps)
    dx = swap_core(after(dx, down_second, up_second))
    down_sent, up_sent = [down_first, down_second], [up_first, up_second]
    d_down = exchange(add_all(down_kept, down_sent), down_order[1])
    d_up = exchange(add_all(up_kept, up_sent), up_order[1])
    dx_across = hop(dx, 1)
    dx, dx_across, d_down, d_up = after((dx, dx_across, d_down, d_up), dx_across)
    d_down = exchange(add_all(*d_down), down_order[2])
    d_up = exchange(add_all(*d_up), up_order[2])
    dx, dx_across = after((dx, dx_across), d_down[0], d_up[0])
    joint, joint_send, partial = call(
        third_back_kernel,
        [((4, count, 3 * GROUP), bf16), ((2, count, 4 * GROUP), bf16), ((4, 64, 2 * GROUP), f32)],
        [(vm, info), (vm, dx), (vm, dx_across), (vm, lm), (vm, wst), (vm, k), (vm, v), (vm, dv_conv), (vm, dq)]
        + [(vm, dkl), (vm, ctx)],
        flops=int(5e9),
        size=8 << 20,
        smem=(0,),
        name="third_back",
    )
    joint_other = hop(after(joint_send, d_down[1], d_up[1]), 2)
    d_down, d_up = after((d_down, d_up), partial)
    d_down, d_up = add_all(*d_down), add_all(*d_up)
    operands = (after(joint, *d_down, *d_up), joint_other, ctx, tokens, tokens_other, ga, ga_other)
    sent = joint_grad(*operands, 1, "grad_joint_sent")
    joint_first = send(sent[0], "y")
    d_down, d_up = after((d_down, d_up), *sent)
    d_down, d_up = exchange(d_down, down_order[3]), exchange(d_up, up_order[3])
    (partial,) = call(
        inverse_back_kernel,
        [((4, 64, 2 * GROUP), bf16)],
        [(vm, dx), (vm, dx_across), (vm, wst), (vm, lm_own), (vm, iterates), (vm, after(partial, *sent))],
        flops=int(1e9),
        size=4 << 20,
        name="inverse_back",
    )
    partial = after(partial, joint_first, d_down[1], d_up[1])
    d_down, d_up = after((d_down, d_up), partial)
    d_down, d_up = add_all(*d_down), add_all(*d_up)
    partial = swap_core(partial).astype(bf16)
    partial_across = hop(partial, 1)
    down_rest, up_rest = rest_of(down_order, 4), rest_of(up_order, 4)
    if EARLY >= 1:
        d_down, d_up = after((d_down, d_up), partial)
        d_down, d_up = down_rest[0](d_down), up_rest[0](d_up)
        partial, partial_across = after((partial, partial_across), partial_across, d_down[0], d_up[0])
        down_rest, up_rest = down_rest[1:], up_rest[1:]
    else:
        partial, partial_across = after((partial, partial_across), partial_across)
    joint_second = send(after(sent[1], partial_across), "y")
    joint_sent = [joint_first, joint_second]
    joint_kept = joint_grad(*after(operands, partial), 0, "grad_joint_kept")
    if EARLY >= 2:
        d_down, d_up = down_rest[0](d_down), up_rest[0](d_up)
        down_rest, up_rest = down_rest[1:], up_rest[1:]
    (d_tokens,) = call(
        token_back_kernel,
        [((count, width), f32)],
        [(vm, info), (vm, partial), (vm, partial_across), (vm, joint), (vm, d_res)] + [(an, w) for w in wt],
        [pltpu.VMEM((4, 3 * GROUP, width), bf16), pltpu.SemaphoreType.DMA((4, 3, 2))],
        flops=2 * count * width * 3072,
        size=10 << 20,
        smem=(0,),
        name="token_back",
    )
    landmark_own = (partial[0].astype(f32) + partial_across[1].astype(f32)).astype(bf16)
    low_rank = dot(landmark_own, pooled_low, TN)
    low_rank = jnp.concatenate([low_rank[0:192], low_rank[GROUP : GROUP + 192]], axis=0)
    d_first = (joint_kept[0].astype(f32) + joint_sent[0].astype(f32) + low_rank).astype(bf16)
    d_second = (joint_kept[1].astype(f32) + joint_sent[1].astype(f32)).astype(bf16)
    norms = jnp.concatenate([sums_attn[0:2], sums_ffn[0:2]], axis=0)
    dtaps = jnp.pad(dtaps[:, 1:4], ((0, 0), (0, 0), (0, width - GROUP)))
    minor = jnp.concatenate([sums_up[:, 0:1], dtaps, jnp.broadcast_to(norms, (4, 4, width))], axis=1)
    minor = after(minor, joint_second)
    minor = minor[0:2] + hop(minor[2:4], 2)
    minor = minor[0] + hop(minor[1], 1)
    orders = [steps, steps[1:2] + steps[:1] + steps[2:]]
    values = [[d_first], [d_second], d_down, d_up, [minor]]
    tasks = [
        rest_of(orders[0], 0),
        rest_of(orders[1], 0),
        in_two(down_rest, down_order),
        in_two(up_rest, up_order),
        [lambda x: x] * LATE + [lambda x, step=step: [x[0] + hop_batch(x[0], step)] for step in steps],
    ]
    for turn in range(max(len(task) for task in tasks)):
        anchors = (values[0][0], values[1][0]) + ((d_tokens,) if turn == 0 else ())
        if turn == IDLE + 2:
            anchors += (values[2][-1], values[3][-1])
        values = [
            task[turn](after(value, *anchors)) if turn < len(task) else value for value, task in zip(values, tasks)
        ]
    d_parts = [values[0][0].astype(f32), values[1][0].astype(f32)]
    d_w_down, d_w_up = values[2][0].astype(f32), values[3][0].astype(f32)
    minor = values[4][0]
    d_w_query, d_w_key = d_parts[0][0:192].T, d_parts[0][192:384].T
    d_w_value, d_w_out = d_parts[1][0:192].T, d_parts[1][192:384]

    return (
        output[None],
        d_tokens[None],
        d_w_query,
        d_w_key,
        d_w_value,
        d_w_out,
        minor[1:4, 0:TAPS],
        d_w_up,
        minor[0],
        d_w_down,
        minor[4],
        minor[5],
        minor[6],
        minor[7],
    )


def solution(mesh):
    return jax.shard_map(
        functools.partial(local, mesh.shape["batch"]),
        mesh=mesh,
        in_specs=(
            P("batch", "head", None),
            P("batch"),
            P(None, "head"),
            P(None, "head"),
            P(None, "head"),
            P("head", None),
            P("head", None),
            P(None, "head"),
            P("head"),
            P("head", None),
            P(),
            P(),
            P(),
            P(),
            P("batch", "head", None),
        ),
        out_specs=(
            P("batch", "head", None),
            P("batch", "head", None),
            P(None, "head"),
            P(None, "head"),
            P(None, "head"),
            P("head", None),
            P("head", None),
            P(None, "head"),
            P("head"),
            P("head", None),
            P(),
            P(),
            P(),
            P(),
        ),
        check_vma=False,
    )
```

```python
import functools

import jax
import jax.numpy as jnp
from jax import lax
from jax.experimental import pallas as pl
from jax.experimental.pallas import tpu as pltpu
from jax.sharding import PartitionSpec as P

f32 = jnp.float32
bf16 = jnp.bfloat16
HEAD_DIM = 64
LANDMARKS = 64
NEWTON = 6
TAPS = 65
HALO = TAPS // 2
EARLY = 1
LATE = 2
IDLE = 1
GROUP = 256
NN = ((1,), (0,))
NT = ((1,), (1,))
TN = ((0,), (0,))
VMEM = pltpu.VMEM
ANY = pl.ANY


def dot(a, b, dims=NN):
    return lax.dot_general(a, b, (dims, ((), ())), preferred_element_type=f32)


def split(x):
    high = x.astype(bf16)
    return high, (x - high.astype(f32)).astype(bf16)


def mm(a, b, dims=NN):
    a_high, a_low = split(a)
    b_high, b_low = split(b)
    return dot(a_high, b_high, dims) + (dot(a_high, b_low, dims) + dot(a_low, b_high, dims))


def mm_left(a, b, dims=NN):
    a_high, a_low = split(a)
    return dot(a_high, b, dims) + dot(a_low, b, dims)


def iota(shape, dim):
    return lax.broadcasted_iota(jnp.int32, shape, dim)


def call(body, outs, ins, scratch=(), flops=0, size=0, limit=40, name=None, smem=()):
    specs = [
        pl.BlockSpec(memory_space=pltpu.SMEM) if i in smem else pl.BlockSpec(memory_space=space)
        for i, (space, _) in enumerate(ins)
    ]
    return pl.pallas_call(
        body,
        out_shape=[jax.ShapeDtypeStruct(s, d) for s, d in outs],
        in_specs=specs,
        out_specs=[pl.BlockSpec(memory_space=VMEM)] * len(outs),
        scratch_shapes=list(scratch),
        compiler_params=pltpu.CompilerParams(vmem_limit_bytes=limit << 20),
        cost_estimate=pl.CostEstimate(flops=flops, bytes_accessed=size, transcendentals=0),
        name=name,
    )(*[value for _, value in ins])


def call_many(parts, name):
    ins = [value for part in parts for value in part[2]]
    outs = [value for part in parts for value in part[1]]
    scratch = [value for part in parts for value in part[3]]
    smem, first = [], 0
    for part in parts:
        smem += [first + i for i in part[4]]
        first += len(part[2])

    def body(*refs):
        groups = [refs[: len(ins)], refs[len(ins) : len(ins) + len(outs)], refs[len(ins) + len(outs) :]]
        at = [0, 0, 0]
        for part in parts:
            mine = []
            for group, kind in ((0, 2), (1, 1), (2, 3)):
                mine += groups[group][at[group] : at[group] + len(part[kind])]
                at[group] += len(part[kind])
            part[0](*mine)

    results = call(body, outs, ins, scratch, flops=int(5e9), size=10 << 20, name=name, smem=tuple(smem), limit=48)
    split_results, first = [], 0
    for part in parts:
        split_results.append(results[first : first + len(part[1])])
        first += len(part[1])
    return split_results


def block_mask():
    return (iota((GROUP, GROUP), 0) >> 6) == (iota((GROUP, GROUP), 1) >> 6)


def spread(x):
    return jnp.where(block_mask(), jnp.concatenate([x, x, x, x], axis=0), 0.0)


def fold(x):
    kept = jnp.where(block_mask(), x, 0.0)
    return kept[0:64] + kept[64:128] + kept[128:192]


def rows_of(info, count, first):
    return info[1] + first + iota((count, 1), 0)


def landmark_kernel(p0, p1, p2, p3, wt, lm, pool, chain):
    pooled = (p0[...].astype(f32) + p1[...].astype(f32)) + (p2[...].astype(f32) + p3[...].astype(f32))
    pool[...] = pooled.astype(bf16)
    high, low = split(pooled)
    both = jnp.concatenate([high, low], axis=0)
    lm[...] = jnp.zeros_like(lm)
    matrices, starts = [], []
    for head in range(3):
        pair = []
        for kind in range(2):
            rows = wt[kind * 192 + head * 64 : kind * 192 + head * 64 + 64]
            out = dot(both, rows, NT)
            out = out[0:64] + out[64:128]
            lm[:, kind * GROUP + head * 64 : kind * GROUP + head * 64 + 64] = out
            pair.append(out)
        scores = mm(pair[0], pair[1], NT) * 0.125
        raised = jnp.exp(scores - jnp.max(scores, axis=1, keepdims=True))
        matrix = raised / jnp.sum(raised, axis=1, keepdims=True)
        column = jnp.max(jnp.sum(matrix, axis=0, keepdims=True), axis=1, keepdims=True)
        row = jnp.max(jnp.sum(matrix, axis=1, keepdims=True), axis=0, keepdims=True)
        matrices.append(matrix)
        starts.append(matrix.T / (column * row))
    eye = (iota((64, 64), 0) == iota((64, 64), 1)).astype(f32)

    def step(it, iterates):
        results = []
        for head in range(3):
            z = iterates[head]
            product = mm(matrices[head], z)
            inner1 = 7.0 * eye - product
            inner2 = 15.0 * eye - mm(product, inner1)
            inner3 = 13.0 * eye - mm(product, inner2)
            chain[it, 0, head] = z
            chain[it, 1, head] = product
            chain[it, 2, head] = inner2
            chain[it, 3, head] = inner3
            results.append(0.25 * mm(z, inner3))
        return tuple(results)

    finals = lax.fori_loop(0, NEWTON, step, tuple(starts))
    for head in range(3):
        lm[:, 2 * GROUP + head * 64 : 2 * GROUP + head * 64 + 64] = finals[head]


def inverse_back_kernel(x0, x1, wst_all, lm, chain, partial, out):
    total = x0[0] + x1[1]
    eye = (iota((64, 64), 0) == iota((64, 64), 1)).astype(f32)
    weight = wst_all[0]
    out[...] = partial[...].astype(bf16)
    grads, matrices, queries, keys = [], [], [], []
    for head in range(3):
        at = slice(head * 64, head * 64 + 64)
        grads.append(mm(total[:, at], weight[:, at], NT))
        query = lm[:, head * 64 : head * 64 + 64]
        key = lm[:, GROUP + head * 64 : GROUP + head * 64 + 64]
        scores = mm(query, key, NT) * 0.125
        raised = jnp.exp(scores - jnp.max(scores, axis=1, keepdims=True))
        matrices.append(raised / jnp.sum(raised, axis=1, keepdims=True))
        queries.append(query)
        keys.append(key)

    def step(count, carried):
        it = NEWTON - 1 - count
        results = []
        for head in range(3):
            dz_next, da = carried[2 * head], carried[2 * head + 1]
            z = chain[it, 0, head]
            product = chain[it, 1, head]
            inner1 = 7.0 * eye - product
            inner2 = chain[it, 2, head]
            inner3 = chain[it, 3, head]
            dz_next = 0.25 * dz_next
            dz = mm(dz_next, inner3, NT)
            d3 = -mm(z, dz_next, TN)
            d2 = -mm(product, d3, TN)
            d1 = mm(product, d2, TN)
            dp = mm(d3, inner2, NT) + mm(d2, inner1, NT) - d1
            da = da + mm(dp, z, NT)
            dz = dz + mm(matrices[head], dp, TN)
            results += [dz, da]
        return tuple(results)

    first = []
    for head in range(3):
        first += [grads[head], jnp.zeros((64, 64), f32)]
    last = lax.fori_loop(0, NEWTON, step, tuple(first))
    for head in range(3):
        dz, da = last[2 * head], last[2 * head + 1]
        matrix = matrices[head]
        columns = jnp.sum(matrix, axis=0, keepdims=True)
        rows = jnp.sum(matrix, axis=1, keepdims=True)
        column = jnp.max(columns, axis=1, keepdims=True)
        row = jnp.max(rows, axis=0, keepdims=True)
        scale = 1.0 / (column * row)
        da = da + dz.T * scale
        d_scale = -jnp.sum(jnp.sum(dz * matrix.T, axis=1, keepdims=True), axis=0, keepdims=True) * scale * scale
        column_hit = (columns == column).astype(f32)
        row_hit = (rows == row).astype(f32)
        da = da + d_scale * row * column_hit / jnp.sum(column_hit, axis=1, keepdims=True)
        da = da + d_scale * column * row_hit / jnp.sum(row_hit, axis=0, keepdims=True)
        ds = matrix * (da - jnp.sum(da * matrix, axis=1, keepdims=True)) * 0.125
        for at, value in ((head * 64, mm(ds, keys[head])), (GROUP + head * 64, mm(ds, queries[head], TN))):
            out[0, :, at : at + 64] = (partial[0, :, at : at + 64] + value).astype(bf16)


PROJECTION = ((0, 192, 0), (192, 192, GROUP), (384, 192, 2 * GROUP))


def split_copies(refs, parts, held, sems, side):
    own, across, across_x, other, both, both_x = refs
    half = own.shape[1] // 2
    mine = pl.ds(pl.multiple_of(side * half, half), half)
    rest = pl.ds(pl.multiple_of((1 - side) * half, half), half)
    blocks = [[], [], [], []]
    for n, (row, rows, to) in enumerate(parts):
        first = pl.ds(row - parts[0][0], rows)
        source, to = pl.ds(row, rows), pl.ds(to, rows)
        blocks[0].append(pltpu.make_async_copy(own.at[first], held.at[0, to], sems.at[0, n, 0]))
        blocks[2].append(pltpu.make_async_copy(other.at[source], held.at[2, to], sems.at[2, n, 0]))
        for i, near, far in ((1, across, across_x), (3, both, both_x)):
            blocks[i].append(pltpu.make_async_copy(near.at[source], held.at[i, to, mine], sems.at[i, n, 0]))
            blocks[i].append(pltpu.make_async_copy(far.at[source], held.at[i, to, rest], sems.at[i, n, 1]))
    return blocks


def start(copies):
    for block in copies:
        for copy in block:
            copy.start()


def wait(copies, i):
    for block in range(4):

        @pl.when(i == block)
        def _():
            for copy in copies[block]:
                copy.wait()


def zero_gaps(held, kinds):
    for i in range(4):
        for kind in range(kinds):
            held[i, kind * GROUP + 192 : kind * GROUP + 256, :] = jnp.zeros((64, held.shape[2]), bf16)


def project_kernel(info, tokens, before, after, w0, w1, w2, w3, w4, w5, q_out, k_out, v_out, held, sems):
    count = tokens.shape[0]
    copies = split_copies((w0, w1, w2, w3, w4, w5), PROJECTION, held, sems, info[2])
    start(copies)
    zero_gaps(held, 3)
    valid = (rows_of(info, count, 0) < info[0]).astype(f32)
    valid_before = (rows_of(info, HALO, -HALO) < info[0]).astype(f32)
    valid_after = (rows_of(info, HALO, count) < info[0]).astype(f32)

    def body(i, _):
        wait(copies, i)
        for kind, out in ((0, q_out), (1, k_out)):
            out[i] = (dot(tokens[...], held[i, kind * GROUP : kind * GROUP + GROUP], NT) * valid).astype(bf16)
        wv = held[i, 2 * GROUP : 3 * GROUP]
        v_out[i, HALO : HALO + count] = (dot(tokens[...], wv, NT) * valid).astype(bf16)
        v_out[i, 0:HALO] = (dot(before[...], wv, NT) * valid_before).astype(bf16)
        v_out[i, HALO + count : 2 * HALO + count] = (dot(after[...], wv, NT) * valid_after).astype(bf16)
        v_out[i, 2 * HALO + count :] = jnp.zeros((v_out.shape[1] - 2 * HALO - count, GROUP), bf16)
        return 0

    lax.fori_loop(0, 4, body, 0)


def third_scores(info, lm, k_ref, i):
    count = k_ref.shape[1]
    valid = info[1] + iota((1, count), 1) < info[0]
    queries = spread(lm[i, :, 0:GROUP])
    return jnp.where(valid, mm_left(queries, k_ref[i], NT) * 0.125, -1e30)


def third_kernel(info, lm, k_ref, v_ref, pay):
    count = k_ref.shape[1]
    lane = iota((64, GROUP), 1)

    def body(i, _):
        scores = third_scores(info, lm, k_ref, i)
        top = jnp.max(scores, axis=1, keepdims=True)
        raised = jnp.exp(scores - top)
        total = jnp.sum(raised, axis=1, keepdims=True)
        packed = fold(mm_left(raised, v_ref[i, HALO : HALO + count]) / total)
        for stat, base in ((top, 192), (total, 216)):
            for term in range(3):
                part = stat.astype(bf16).astype(f32)
                stat = stat - part
                for head in range(3):
                    packed = jnp.where(lane == base + 8 * term + head, part[head * 64 : head * 64 + 64], packed)
        pay[i] = packed.astype(bf16)
        return 0

    lax.fori_loop(0, 4, body, 0)


def first_scores(lm, q_ref, i):
    keys = spread(lm[i, :, GROUP : 2 * GROUP])
    count = q_ref.shape[1]
    scores = (mm_left(keys, q_ref[i], NT) * 0.125).reshape(4, 64, count)
    raised = jnp.exp(scores - jnp.max(scores, axis=1, keepdims=True))
    return raised / jnp.sum(raised, axis=1, keepdims=True)


def toeplitz(row):
    return pltpu.roll(jnp.broadcast_to(row, (128, GROUP)), 0, 1, stride=1, stride_axis=0)


def head_select(x, rows):
    lane = iota((rows, GROUP), 1) >> 6
    out = jnp.where(lane == 0, x[0:rows], 0.0)
    out = jnp.where(lane == 1, x[rows : 2 * rows], out)
    return jnp.where(lane == 2, x[2 * rows : 3 * rows], out)


def context_kernel(p0, p1, p2, p3, lm, q_ref, v_ref, small, ctx, wst, x_out):
    count = q_ref.shape[1]
    lane = iota((64, GROUP), 1)

    def body(i, _):
        parts = [p[i ^ n].astype(f32) for n, p in enumerate((p0, p1, p2, p3))]

        def stat(part, at):
            return part[:, at : at + 1] + part[:, at + 8 : at + 9] + part[:, at + 16 : at + 17]

        factors = [jnp.zeros((64, GROUP), f32) for _ in range(4)]
        stats = jnp.zeros((64, GROUP), f32)
        for head in range(3):
            tops = [stat(part, 192 + head) for part in parts]
            top = jnp.maximum(jnp.maximum(tops[0], tops[1]), jnp.maximum(tops[2], tops[3]))
            scales = [stat(part, 216 + head) * jnp.exp(t - top) for part, t in zip(parts, tops)]
            total = sum(scales)
            mine = (lane >> 6) == head
            factors = [jnp.where(mine, s / total, f) for s, f in zip(scales, factors)]
            stats = jnp.where(lane == 192 + head, top, stats)
            stats = jnp.where(lane == 196 + head, total, stats)
        weight = sum(part * f for part, f in zip(parts, factors))
        wst[i] = jnp.where(lane < 192, weight, stats)
        mixed = mm(spread(lm[i, :, 2 * GROUP : 3 * GROUP]), spread(weight))
        x_out[i] = fold(mixed)
        first = first_scores(lm, q_ref, i).reshape(GROUP, count)
        main = mm(first, mixed, TN)
        bands = [toeplitz(small[i, 1 + head : 2 + head, 0:GROUP]) for head in range(3)]
        high, low = split(jnp.concatenate(bands, axis=0))
        for block in range(count // 128):
            window = v_ref[i, block * 128 : block * 128 + 256]
            conv = dot(high, window) + dot(low, window)
            ctx[i, block * 128 : block * 128 + 128] = (
                main[block * 128 : block * 128 + 128] + head_select(conv, 128)
            ).astype(bf16)
        return 0

    lax.fori_loop(0, 4, body, 0)


def first_back_kernel(
    info, g_ref, before, after, o0, o1, o2, o3, o4, o5, lm, q_ref, v_ref, small, x_in, dx, dq, dkl, dv, dtaps, held, sems, ext, dctx
):
    count = g_ref.shape[0]
    width = g_ref.shape[1]
    copies = split_copies((o0, o1, o2, o3, o4, o5), ((0, 192, 0),), held, sems, info[2])
    start(copies)
    zero_gaps(held, 1)
    valid = (rows_of(info, count, 0) < info[0]).astype(f32)
    ext[0:HALO] = before[...]
    ext[HALO : HALO + count] = g_ref[...]
    ext[HALO + count : 2 * HALO + count] = after[...]
    ext[2 * HALO + count :] = jnp.zeros((ext.shape[0] - 2 * HALO - count, width), bf16)
    lane = iota((128, GROUP), 1) >> 6
    flip = (iota((128, 128), 0) + iota((128, 128), 1) == 127).astype(bf16)

    def body(i, _):
        wait(copies, i)
        dctx[...] = dot(ext[...], held[i], NT)
        own = dctx[HALO : HALO + count]
        own_high = own.astype(bf16)
        first = first_scores(lm, q_ref, i)
        flat = first.reshape(GROUP, count)
        dx[i] = fold(dot(flat.astype(bf16), own_high))
        dfirst = dot(spread(x_in[i]).astype(bf16), own_high, NT)
        dfirst = dfirst.reshape(4, 64, count)
        ds = first * (dfirst - jnp.sum(first * dfirst, axis=1, keepdims=True)) * 0.125
        ds = ds.reshape(GROUP, count).astype(bf16)
        keys = (spread(lm[i, :, GROUP : 2 * GROUP])).astype(bf16)
        dquery = dot(ds, keys, TN)
        dq[i] = (dquery * valid).astype(bf16)
        dkl[i] = fold(dot(ds, q_ref[i]))
        bands = [toeplitz(small[i, 4 + head : 5 + head, 0:GROUP]) for head in range(3)]
        high = jnp.concatenate(bands, axis=0).astype(bf16)
        gram = jnp.zeros((384, GROUP), f32)
        for block in range(count // 128):
            conv = dot(high, dctx[block * 128 : block * 128 + 256].astype(bf16))
            dv[i, block * 128 : block * 128 + 128] = head_select(conv, 128)
            piece = dctx[HALO + block * 128 : HALO + block * 128 + 128]
            stacked = jnp.concatenate([jnp.where(lane == head, piece, 0.0) for head in range(3)], axis=0)
            gram = gram + dot(stacked.astype(bf16), v_ref[i, block * 128 : block * 128 + 256], NT)
        dtaps[i] = jnp.zeros((8, GROUP), f32)
        for head in range(3):
            part_high, part_low = split(gram[head * 128 : head * 128 + 128])
            upturned = dot(flip, part_high) + dot(flip, part_low)
            straight = pltpu.roll(upturned, GROUP - 127, 1, stride=1, stride_axis=0)
            summed = jnp.sum(straight, axis=0, keepdims=True)
            dtaps[i, 1 + head : 2 + head, :] = jnp.where(iota((1, GROUP), 1) < TAPS, summed, 0.0)
        return 0

    lax.fori_loop(0, 4, body, 0)


def third_back_kernel(info, x0, x1, lm, wst, k_ref, v_ref, dvc, dq, dkl, ctx, joint, send, partial):
    count = k_ref.shape[1]
    valid = (rows_of(info, count, 0) < info[0]).astype(f32)
    none = jnp.zeros((64, 1), f32)

    def body(i, _):
        dx = spread(x0[i] + x1[i ^ 1])
        dweight = mm(spread(lm[i, :, 2 * GROUP : 3 * GROUP]), dx, TN)
        stats = wst[i]
        weight = spread(jnp.where(iota((64, GROUP), 1) < 192, stats, 0.0))
        inner = jnp.sum(dweight * weight, axis=1, keepdims=True)
        top = jnp.concatenate([stats[:, 192 + head : 193 + head] for head in range(3)] + [none], axis=0)
        total = jnp.concatenate([stats[:, 196 + head : 197 + head] for head in range(3)] + [none + 1.0], axis=0)
        scores = third_scores(info, lm, k_ref, i)
        third = jnp.exp(scores - top) / total
        dw_high = dweight.astype(bf16)
        values = v_ref[i, HALO : HALO + count]
        dthird = dot(dw_high, values, NT)
        ds = (third * (dthird - inner) * 0.125).astype(bf16)
        queries = (spread(lm[i, :, 0:GROUP])).astype(bf16)
        dkey = dot(ds, queries, TN)
        partial[i, :, 0:GROUP] = fold(dot(ds, k_ref[i]))
        partial[i, :, GROUP : 2 * GROUP] = dkl[i]
        dvalues = dot(third.astype(bf16), dw_high, TN)
        joint[i, :, 0:GROUP] = dq[i]
        joint[i, :, GROUP : 2 * GROUP] = (dkey * valid).astype(bf16)
        joint[i, :, 2 * GROUP : 3 * GROUP] = ((dvalues + dvc[i]) * valid).astype(bf16)

        @pl.when(i >= 2)
        def _():
            send[i - 2, :, 0 : 3 * GROUP] = joint[i]
            send[i - 2, :, 3 * GROUP : 4 * GROUP] = ctx[i]

        return 0

    lax.fori_loop(0, 4, body, 0)


def token_back_kernel(info, l0, l1, joint, dres, w0, w1, w2, w3, w4, w5, out, held, sems):
    copies = split_copies((w0, w1, w2, w3, w4, w5), PROJECTION, held, sems, info[2])
    start(copies)
    zero_gaps(held, 3)
    count = joint.shape[1]
    mark = iota((1, 64), 1)
    low = (mark * info[0]) >> 6
    high = ((mark + 1) * info[0]) >> 6
    pos = rows_of(info, count, 0)
    member = ((pos >= low) & (pos < high)).astype(bf16)
    row = iota((64, 1), 0)
    width = ((((row + 1) * info[0]) >> 6) - ((row * info[0]) >> 6)).astype(f32)
    out[...] = dres[...]

    def body(i, pooled):
        wait(copies, i)
        out[...] += dot(joint[i], held[i])
        marks = (l0[i].astype(f32) + l1[i ^ 1].astype(f32)) / width
        return pooled + mm_left(marks, held[i, 0 : 2 * GROUP])

    pooled = lax.fori_loop(0, 4, body, jnp.zeros((64, out.shape[1]), f32))
    pooled_high, pooled_low = split(pooled)
    out[...] += dot(member, pooled_high) + dot(member, pooled_low)


def moments(x):
    centered = x - jnp.mean(x, axis=-1, keepdims=True)
    variance = jnp.mean(centered * centered, axis=-1, keepdims=True)
    inverse = lax.rsqrt(variance + 1e-05)
    return centered * inverse, inverse


def attended_kernel(info, ctx, tokens, gain, shift, o0, o1, o2, o3, o4, o5, pre, normed, low, held, sems):
    copies = split_copies((o0, o1, o2, o3, o4, o5), ((0, 192, 0),), held, sems, info[2])
    start(copies)
    zero_gaps(held, 1)
    pre[...] = tokens[...].astype(f32)

    def body(i, _):
        wait(copies, i)
        pre[...] += dot(ctx[i], held[i])
        return 0

    lax.fori_loop(0, 4, body, 0)
    unit, _ = moments(pre[...])
    result = unit * gain[...] + shift[...]
    normed[...] = result
    low[...] = result.astype(bf16)


def gelu_parts(u):
    cdf = 0.5 + 0.5 * lax.erf(u * 0.7071067811865476)
    pdf = jnp.exp(u * u * -0.5) * 0.3989422804014327
    return u * cdf, cdf + u * pdf


def up_kernel(info, low, small, w0, w1, w2, w3, w4, w5, hidden, slope, send, held, sems):
    copies = split_copies((w0, w1, w2, w3, w4, w5), ((192, held.shape[1], 0),), held, sems, info[2])
    start(copies)

    def body(i, _):
        wait(copies, i)
        for chunk in range(3):
            at = slice(chunk * 256, chunk * 256 + 256)
            upward = dot(low[...], held[i, :, at]) + small[i, 0:1, at]
            value, derivative = gelu_parts(upward)
            hidden[i, :, at] = value.astype(bf16)
            slope[i, :, at] = derivative.astype(bf16)

        @pl.when(i >= 2)
        def _():
            send[i - 2] = hidden[i]

        return 0

    send[2] = low[...]
    lax.fori_loop(0, 4, body, 0)


def norm_back(g, gain, unit, inverse):
    scaled = g * gain
    mean1 = jnp.mean(scaled, axis=-1, keepdims=True)
    mean2 = jnp.mean(scaled * unit, axis=-1, keepdims=True)
    return (scaled - mean1 - unit * mean2) * inverse


def down_kernel(info, hidden, normed, grad, gain, shift, w0, w1, w2, w3, w4, w5, out, dsum, dlow, sums, held, sems, acc):
    copies = split_copies((w0, w1, w2, w3, w4, w5), ((0, held.shape[1], 0),), held, sems, info[2])
    start(copies)
    acc[...] = normed[...]

    def body(i, _):
        wait(copies, i)
        acc[...] += dot(hidden[i], held[i])
        return 0

    lax.fori_loop(0, 4, body, 0)
    unit, inverse = moments(acc[...])
    out[...] = (unit * gain[...] + shift[...]).astype(bf16)
    g = grad[...].astype(f32)
    back = norm_back(g, gain[...], unit, inverse)
    dsum[...] = back
    dlow[...] = back.astype(bf16)
    sums[...] = jnp.zeros_like(sums)
    sums[0:1] = jnp.sum(g * unit, axis=0, keepdims=True)
    sums[1:2] = jnp.sum(g, axis=0, keepdims=True)


def hidden_back_kernel(info, dlow, slope, w0, w1, w2, w3, w4, w5, du, send, sums, held, sems):
    copies = split_copies((w0, w1, w2, w3, w4, w5), ((0, held.shape[1], 0),), held, sems, info[2])
    start(copies)
    sums[...] = jnp.zeros_like(sums)

    def body(i, _):
        wait(copies, i)
        for chunk in range(3):
            at = slice(chunk * 256, chunk * 256 + 256)
            back = dot(dlow[...], held[i, at, :], NT) * slope[i, :, at].astype(f32)
            back = back.astype(bf16)
            du[i, :, at] = back
            sums[i, 0:1, at] = jnp.sum(back.astype(f32), axis=0, keepdims=True)

        @pl.when(i >= 2)
        def _():
            send[i - 2] = du[i]

        return 0

    send[2] = dlow[...]
    lax.fori_loop(0, 4, body, 0)


def residual_back_kernel(info, du, dsum, pre, gain, w0, w1, w2, w3, w4, w5, dres, dlow, sums, held, sems, acc):
    copies = split_copies((w0, w1, w2, w3, w4, w5), ((192, held.shape[1], 0),), held, sems, info[2])
    start(copies)
    acc[...] = dsum[...]

    def body(i, _):
        wait(copies, i)
        acc[...] += dot(du[i], held[i], NT)
        return 0

    lax.fori_loop(0, 4, body, 0)
    unit, inverse = moments(pre[...])
    g = acc[...]
    back = norm_back(g, gain[...], unit, inverse)
    dres[...] = back
    dlow[...] = back.astype(bf16)
    sums[...] = jnp.zeros_like(sums)
    sums[0:1] = jnp.sum(g * unit, axis=0, keepdims=True)
    sums[1:2] = jnp.sum(g, axis=0, keepdims=True)


def feed_grad_kernel(
    pick, hidden, hidden_other, gd, du_other, du, low, down0, down1, up0, up1, left, right, sems
):
    half = left.shape[-1]
    copies = []

    def bring(source, target):
        copy = pltpu.make_async_copy(source, target, sems.at[len(copies)])
        copy.start()
        copies.append(copy)

    for part, sources in ((0, (hidden.at[0], hidden_other.at[0], hidden.at[1], hidden_other.at[1])), (1, (low, hidden_other.at[2]))):
        columns = pl.ds(pl.multiple_of(pick[part] * half, half), half)
        for n, source in enumerate(sources):
            bring(source.at[:, columns], left.at[4 * part + n])
        if part == 0:
            bring(gd, right.at[0])
            bring(du_other.at[2], right.at[1])
        else:
            for j in range(2):
                bring(du.at[j], right.at[2 + 2 * j])
                bring(du_other.at[j], right.at[3 + 2 * j])
    for copy in copies[:6]:
        copy.wait()

    def body(n, _):
        @pl.when(n == 2)
        def _():
            for copy in copies[6:]:
                copy.wait()

        down = n < 2
        at_left = jnp.where(down, 2 * n, 4)
        at_right = jnp.where(down, 0, 2 * n - 2)
        total = dot(left[at_left], right[at_right], TN) + dot(left[at_left + 1], right[at_right + 1], TN)
        total = total.astype(bf16)
        for k, out in enumerate((down0, down1, up0, up1)):

            @pl.when(n == k)
            def _():
                out[...] = total

        return 0

    lax.fori_loop(0, 4, body, 0)


def feed_grad(pick, hidden, hidden_other, gd, du_other, du, low):
    count, width = gd.shape
    return (
        feed_grad_kernel,
        [((width // 2, width), bf16)] * 4,
        [(VMEM, pick.astype(jnp.int32))] + [(ANY, x) for x in (hidden, hidden_other, gd, du_other, du, low)],
        [
            pltpu.VMEM((6, count, width // 2), bf16),
            pltpu.VMEM((6, count, width), bf16),
            pltpu.SemaphoreType.DMA((12,)),
        ],
        (0,),
    )


def joint_grad_kernel(joint, other, ctx, tokens, tokens_other, g, g_other, first, second):
    def body(kind, _):
        at = pl.ds(pl.multiple_of(kind * GROUP, GROUP), GROUP)
        total = dot(joint[0, :, at], tokens[...], TN) + dot(other[0, :, at], tokens_other[...], TN)
        total = total[0:192].astype(bf16)

        @pl.when(kind < 2)
        def _():
            first[pl.ds(pl.multiple_of(kind * 192, 192), 192)] = total

        @pl.when(kind == 2)
        def _():
            second[0:192] = total

        return 0

    lax.fori_loop(0, 3, body, 0)
    total = dot(ctx[0], g[...], TN) + dot(other[0, :, 3 * GROUP : 4 * GROUP], g_other[...], TN)
    second[192:384] = total[0:192].astype(bf16)


def joint_grad(joint, other, ctx, tokens, tokens_other, g, g_other, block, name):
    count, width = tokens.shape
    whole = pl.BlockSpec((count, width), lambda j: (0, 0))
    return pl.pallas_call(
        joint_grad_kernel,
        grid=(1,),
        out_shape=[jax.ShapeDtypeStruct((width // 2, width), bf16)] * 2,
        in_specs=[
            pl.BlockSpec((1, count, 3 * GROUP), lambda j: (block, 0, 0)),
            pl.BlockSpec((1, count, 4 * GROUP), lambda j: (block, 0, 0)),
            pl.BlockSpec((1, count, GROUP), lambda j: (block, 0, 0)),
            whole,
            whole,
            whole,
            whole,
        ],
        out_specs=[pl.BlockSpec((width // 2, width), lambda j: (0, 0))] * 2,
        compiler_params=pltpu.CompilerParams(vmem_limit_bytes=40 << 20),
        cost_estimate=pl.CostEstimate(flops=16 * count * GROUP * width, bytes_accessed=8 << 20, transcendentals=0),
        name=name,
    )(joint, other, ctx, tokens, tokens_other, g, g_other)


HOP = {1: 2, 2: 1, 3: 3}


def hop(x, step):
    return lax.ppermute(x, "head", [(i, i ^ HOP[step]) for i in range(4)])


def after(x, *deps):
    return lax.optimization_barrier((x,) + deps)[0]


def local(
    batch_count,
    tokens,
    lengths,
    w_query,
    w_key,
    w_value,
    w_out,
    conv_taps,
    w_up,
    b_up,
    w_down,
    gain_attn,
    shift_attn,
    gain_ffn,
    shift_ffn,
    grad_out,
):
    tokens = tokens[0]
    grad_out = grad_out[0]
    count, width = tokens.shape
    ext = count + 128
    length = lengths[0]
    place = lax.axis_index("head")
    batch = lax.axis_index("batch")
    core = place & 1
    side = batch & 1
    info = jnp.stack([length, place * count, side]).astype(jnp.int32)
    gain_attn, shift_attn, gain_ffn, shift_ffn = (
        x.reshape(1, width) for x in (gain_attn, shift_attn, gain_ffn, shift_ffn)
    )
    vm, an = VMEM, ANY

    def hop_batch(x, step):
        return lax.ppermute(x, "batch", [(i, i ^ step) for i in range(batch_count)])

    def neighbours(x, other):
        first = core == 0
        far = lax.ppermute(jnp.where(first, x[:HALO], x[-HALO:]), "head", [(1, 2), (2, 1)])
        return jnp.where(first, far, other[-HALO:]), jnp.where(first, other[:HALO], far)

    marks = jnp.arange(LANDMARKS + 1, dtype=jnp.int32) * length // LANDMARKS
    positions = info[1] + jnp.arange(count, dtype=jnp.int32)
    member = (positions[None, :] >= marks[:-1, None]) & (positions[None, :] < marks[1:, None])
    pooled = jnp.dot(member.astype(bf16), tokens, preferred_element_type=f32)
    pooled = (pooled / (marks[1:] - marks[:-1]).astype(f32)[:, None]).astype(bf16)
    pools = [pooled] + [hop(pooled, n) for n in (1, 2, 3)]

    taps = jnp.pad(conv_taps, ((0, 0), (0, width - TAPS)))
    taps_back = jnp.pad(conv_taps[:, ::-1], ((0, 0), (0, width - TAPS)))
    small_own = jnp.concatenate([b_up[None], taps, taps_back, jnp.zeros((1, width), f32)], axis=0)
    term1 = small_own.astype(bf16)
    rest = small_own - lax.reduce_precision(small_own, 8, 7)
    term2 = rest.astype(bf16)
    term3 = (rest - lax.reduce_precision(rest, 8, 7)).astype(bf16)
    wt_own = jnp.concatenate(
        [w_query.T, w_key.T, w_value.T, term1, term2, term3, jnp.zeros((8, width), bf16)], axis=0
    )
    tokens_other = hop(tokens, 2)
    before, behind = neighbours(tokens, tokens_other)

    def column_half(own):
        return lax.dynamic_slice_in_dim(own, side * (width // 2), width // 2, 1)

    wt_other = hop(wt_own, 2)
    wt_across = hop(after(column_half(wt_own), *pools), 1)
    lm_own, pooled_low, iterates = call(
        landmark_kernel,
        [((64, 3 * GROUP), f32), ((64, width), bf16), ((NEWTON, 4, 3, 64, 64), f32)],
        [(vm, x) for x in pools] + [(vm, wt_own)],
        flops=int(1e9),
        size=4 << 20,
        name="landmarks",
    )
    lm_own = after(lm_own, wt_across, before, behind)
    lm_across = hop(lm_own, 1)
    wt_across_x = hop_batch(after(wt_across, pooled_low), 1)
    lm = jnp.stack([lm_own, lm_across, hop(lm_own, 2), hop(lm_across, 2)])
    wt = [wt_own, wt_across, wt_across_x, wt_other, hop(wt_across, 2), hop(wt_across_x, 2)]

    def small_of(block):
        return sum(block[576 + 8 * n : 584 + 8 * n].astype(f32) for n in range(3))

    def small_joined(near, far):
        near, far = small_of(near), small_of(far)
        first = side == 0
        return jnp.concatenate([jnp.where(first, near, far), jnp.where(first, far, near)], axis=1)

    small = jnp.stack(
        [small_of(wt[0]), small_joined(wt[1], wt[2]), small_of(wt[3]), small_joined(wt[4], wt[5])]
    )
    out_up_own = jnp.concatenate([w_out, after(w_up, pooled)], axis=0)
    out_up_across = hop(after(column_half(out_up_own), lm_across), 1)
    down_across = hop(after(column_half(w_down), lm_across), 1)
    q, k, v = call(
        project_kernel,
        [((4, count, GROUP), bf16), ((4, count, GROUP), bf16), ((4, ext, GROUP), bf16)],
        [(vm, info), (vm, tokens), (vm, before), (vm, behind)] + [(an, w) for w in wt],
        [pltpu.VMEM((4, 3 * GROUP, width), bf16), pltpu.SemaphoreType.DMA((4, 3, 2))],
        flops=2 * count * width * 3072,
        size=8 << 20,
        smem=(0,),
        name="project",
    )
    out_up_across_x = hop_batch(after(out_up_across, q), 1)
    (pay,) = call(
        third_kernel,
        [((4, 64, GROUP), bf16)],
        [(vm, info), (vm, lm), (vm, k), (vm, v)],
        flops=int(1e9),
        size=3 << 20,
        smem=(0,),
        name="third",
    )
    pays = [pay, hop(pay, 1), hop(pay, 2), hop(pay, 3)]
    ctx, wst, x_mid = call(
        context_kernel,
        [((4, count, GROUP), bf16), ((4, 64, GROUP), f32), ((4, 64, GROUP), f32)],
        [(vm, p) for p in pays] + [(vm, lm), (vm, q), (vm, v), (vm, small)],
        flops=int(3e9),
        size=5 << 20,
        name="context",
    )
    out_up_far = after((out_up_across, out_up_across_x), ctx)
    out_up = [out_up_across, out_up_across_x, hop(after(out_up_own, q), 2), hop(out_up_far[0], 2), hop(out_up_far[1], 2)]
    down_across_x = hop_batch(after(down_across, ctx), 1)
    wo = [(an, w) for w in [w_out] + out_up]
    wu = [(an, w) for w in [w_up] + out_up]
    out_scratch = [pltpu.VMEM((4, GROUP, width), bf16), pltpu.SemaphoreType.DMA((4, 1, 2))]
    wide = [pltpu.VMEM((4, width, width), bf16), pltpu.SemaphoreType.DMA((4, 1, 2))]
    acc = [pltpu.VMEM((count, width), f32)]

    pre, normed, normed_low = call(
        attended_kernel,
        [((count, width), f32), ((count, width), f32), ((count, width), bf16)],
        [(vm, info), (vm, ctx), (vm, tokens), (vm, gain_attn), (vm, shift_attn)] + wo,
        out_scratch,
        flops=2 * count * width * width,
        size=6 << 20,
        smem=(0,),
        name="attended",
    )
    down_far = after((down_across, down_across_x), normed_low)
    down = [down_across, down_across_x, hop(after(w_down, ctx), 2), hop(down_far[0], 2), hop(down_far[1], 2)]
    wd = [(an, w) for w in [w_down] + down]
    hidden, slope, hidden_send = call(
        up_kernel,
        [((4, count, width), bf16), ((4, count, width), bf16), ((3, count, width), bf16)],
        [(vm, info), (vm, normed_low), (vm, small)] + wu,
        wide,
        flops=2 * count * width * 3072,
        size=12 << 20,
        smem=(0,),
        name="up",
    )
    hidden_other = hop(hidden_send, 2)
    output, d_sum, gd, sums_ffn = call(
        down_kernel,
        [((count, width), bf16), ((count, width), f32), ((count, width), bf16), ((8, width), f32)],
        [(vm, info), (vm, hidden), (vm, normed), (vm, grad_out), (vm, gain_ffn), (vm, shift_ffn)] + wd,
        wide + acc,
        flops=2 * count * width * 3072,
        size=14 << 20,
        smem=(0,),
        name="down",
    )

    steps = [1 << n for n in range(batch_count.bit_length() - 1)]
    down_order = steps[:2] + ["y"] + steps[2:]
    up_order = steps[1:2] + steps[:1] + ["y"] + steps[2:]

    def bit(step):
        return (batch // step) & 1

    def send(x, step):
        return hop(x, 1) if step == "y" else hop_batch(x, step)

    def chain(pieces, step):
        received = [send(pieces[0], step)]
        for piece in pieces[1:]:
            received.append(send(after(piece, received[-1]), step))
        return received

    def add_all(kept, received):
        return [(a.astype(f32) + b.astype(f32)).astype(bf16) for a, b in zip(kept, received)]

    def split_for(pieces, step):
        if step == "y":
            return pieces[:1], pieces[1:]
        rows = pieces[0].shape[0] // 2
        kept = [lax.dynamic_slice_in_dim(x, bit(step) * rows, rows, 0) for x in pieces]
        sent = [lax.dynamic_slice_in_dim(x, (1 - bit(step)) * rows, rows, 0) for x in pieces]
        if len(pieces) > 1:
            sent = [jnp.stack(sent)]
        return kept, sent

    def exchange(pieces, step):
        kept, sent = split_for(pieces, step)
        received = send(sent[0], step)
        return kept, [received] if received.ndim == 2 else [received[n] for n in range(len(kept))]

    def grow(x, step):
        other = hop_batch(x, step)
        mine_last = bit(step) == 1
        return jnp.concatenate([jnp.where(mine_last, other, x), jnp.where(mine_last, x, other)], axis=0)

    def grow_first(x, step):
        return [x[0], hop_batch(x[0][: x[0].shape[0] // 2], step)]

    def grow_second(x, step):
        own, other = x
        other = jnp.concatenate([other, hop_batch(own[own.shape[0] // 2 :], step)], axis=0)
        mine_last = bit(step) == 1
        return [jnp.concatenate([jnp.where(mine_last, other, own), jnp.where(mine_last, own, other)], axis=0)]

    def in_two(task, order):
        return task[:-1] + [lambda x: x] * IDLE + [lambda x: grow_first(x, order[0]), lambda x: grow_second(x, order[0])]

    def rest_of(order, done):
        back = [step for step in order if step != "y"][::-1]
        return [lambda x, step=step: add_all(*exchange(x, step)) for step in order[done:]] + [
            lambda x, step=step: [grow(x[0], step)] for step in back
        ]

    du, du_send, sums_up = call(
        hidden_back_kernel,
        [((4, count, width), bf16), ((3, count, width), bf16), ((4, 8, width), f32)],
        [(vm, info), (vm, gd), (vm, slope)] + wd,
        wide,
        flops=2 * count * width * 3072,
        size=12 << 20,
        smem=(0,),
        name="hidden_back",
    )
    du_other = hop(du_send, 2)
    mine = jnp.stack([bit(down_order[0]), bit(up_order[0])])
    operands = (hidden, hidden_other, gd, du_other, du, normed_low)
    ((down_sent0, down_sent1, up_sent0, up_sent1),) = call_many([feed_grad(1 - mine, *operands)], "grad_sent")
    down_first = send(down_sent0, down_order[0])
    up_first = send(up_sent0, up_order[0])
    kept, (d_res, ga, sums_attn) = call_many(
        [
            feed_grad(mine, hidden, hidden_other, after(gd, down_sent0), du_other, du, normed_low),
            (
                residual_back_kernel,
                [((count, width), f32), ((count, width), bf16), ((8, width), f32)],
                [(vm, info), (vm, du), (vm, d_sum), (vm, pre), (vm, gain_attn)] + wu,
                wide + acc,
                (0,),
            ),
        ],
        "grad_kept",
    )
    down_kept, up_kept = kept[:2], kept[2:]
    ga, down_first, up_first = after((ga, down_first, up_first), d_res)
    ga_other = hop(ga, 2)
    ga_before, ga_behind = neighbours(ga, ga_other)
    down_second = send(after(down_sent1, down_first), down_order[0])
    up_second = send(after(up_sent1, up_first), up_order[0])
    dx, dq, dkl, dv_conv, dtaps = call(
        first_back_kernel,
        [
            ((4, 64, GROUP), f32),
            ((4, count, GROUP), bf16),
            ((4, 64, GROUP), f32),
            ((4, count, GROUP), f32),
            ((4, 8, GROUP), f32),
        ],
        [(vm, info), (vm, after(ga, down_first, up_first)), (vm, ga_before), (vm, ga_behind)]
        + wo
        + [(vm, lm), (vm, q), (vm, v), (vm, small), (vm, x_mid)],
        out_scratch + [pltpu.VMEM((ext, width), bf16), pltpu.VMEM((ext, GROUP), f32)],
        flops=int(5e9),
        size=10 << 20,
        smem=(0,),
        name="first_back",
    )

    def swap_core(x):
        other = hop(x, 2)
        return x.astype(f32) + jnp.concatenate([other[2:4], other[0:2]], axis=0).astype(f32)

    dx, down_second, up_second = after((dx, down_second, up_second), dtaps)
    dx = swap_core(after(dx, down_second, up_second))
    down_sent, up_sent = [down_first, down_second], [up_first, up_second]
    d_down = exchange(add_all(down_kept, down_sent), down_order[1])
    d_up = exchange(add_all(up_kept, up_sent), up_order[1])
    dx_across = hop(dx, 1)
    dx, dx_across, d_down, d_up = after((dx, dx_across, d_down, d_up), dx_across)
    d_down = exchange(add_all(*d_down), down_order[2])
    d_up = exchange(add_all(*d_up), up_order[2])
    dx, dx_across = after((dx, dx_across), d_down[0], d_up[0])
    joint, joint_send, partial = call(
        third_back_kernel,
        [((4, count, 3 * GROUP), bf16), ((2, count, 4 * GROUP), bf16), ((4, 64, 2 * GROUP), f32)],
        [(vm, info), (vm, dx), (vm, dx_across), (vm, lm), (vm, wst), (vm, k), (vm, v), (vm, dv_conv), (vm, dq)]
        + [(vm, dkl), (vm, ctx)],
        flops=int(5e9),
        size=8 << 20,
        smem=(0,),
        name="third_back",
    )
    joint_other = hop(after(joint_send, d_down[1], d_up[1]), 2)
    d_down, d_up = after((d_down, d_up), partial)
    d_down, d_up = add_all(*d_down), add_all(*d_up)
    operands = (after(joint, *d_down, *d_up), joint_other, ctx, tokens, tokens_other, ga, ga_other)
    sent = joint_grad(*operands, 1, "grad_joint_sent")
    joint_first = send(sent[0], "y")
    d_down, d_up = after((d_down, d_up), *sent)
    d_down, d_up = exchange(d_down, down_order[3]), exchange(d_up, up_order[3])
    (partial,) = call(
        inverse_back_kernel,
        [((4, 64, 2 * GROUP), bf16)],
        [(vm, dx), (vm, dx_across), (vm, wst), (vm, lm_own), (vm, iterates), (vm, after(partial, *sent))],
        flops=int(1e9),
        size=4 << 20,
        name="inverse_back",
    )
    partial = after(partial, joint_first, d_down[1], d_up[1])
    d_down, d_up = after((d_down, d_up), partial)
    d_down, d_up = add_all(*d_down), add_all(*d_up)
    partial = swap_core(partial).astype(bf16)
    partial_across = hop(partial, 1)
    down_rest, up_rest = rest_of(down_order, 4), rest_of(up_order, 4)
    if EARLY >= 1:
        d_down, d_up = after((d_down, d_up), partial)
        d_down, d_up = down_rest[0](d_down), up_rest[0](d_up)
        partial, partial_across = after((partial, partial_across), partial_across)
        down_rest, up_rest = down_rest[1:], up_rest[1:]
    else:
        partial, partial_across = after((partial, partial_across), partial_across)
    joint_second = send(after(sent[1], partial_across), "y")
    joint_sent = [joint_first, joint_second]
    joint_kept = joint_grad(*after(operands, partial), 0, "grad_joint_kept")
    if EARLY >= 2:
        d_down, d_up = down_rest[0](d_down), up_rest[0](d_up)
        down_rest, up_rest = down_rest[1:], up_rest[1:]
    (d_tokens,) = call(
        token_back_kernel,
        [((count, width), f32)],
        [(vm, info), (vm, partial), (vm, partial_across), (vm, joint), (vm, d_res)] + [(an, w) for w in wt],
        [pltpu.VMEM((4, 3 * GROUP, width), bf16), pltpu.SemaphoreType.DMA((4, 3, 2))],
        flops=2 * count * width * 3072,
        size=10 << 20,
        smem=(0,),
        name="token_back",
    )
    landmark_own = (partial[0].astype(f32) + partial_across[1].astype(f32)).astype(bf16)
    low_rank = dot(landmark_own, pooled_low, TN)
    low_rank = jnp.concatenate([low_rank[0:192], low_rank[GROUP : GROUP + 192]], axis=0)
    d_first = (joint_kept[0].astype(f32) + joint_sent[0].astype(f32) + low_rank).astype(bf16)
    d_second = (joint_kept[1].astype(f32) + joint_sent[1].astype(f32)).astype(bf16)
    norms = jnp.concatenate([sums_attn[0:2], sums_ffn[0:2]], axis=0)
    dtaps = jnp.pad(dtaps[:, 1:4], ((0, 0), (0, 0), (0, width - GROUP)))
    minor = jnp.concatenate([sums_up[:, 0:1], dtaps, jnp.broadcast_to(norms, (4, 4, width))], axis=1)
    minor = after(minor, joint_second)
    minor = minor[0:2] + hop(minor[2:4], 2)
    minor = minor[0] + hop(minor[1], 1)
    orders = [steps, steps[1:2] + steps[:1] + steps[2:]]
    values = [[d_first], [d_second], d_down, d_up, [minor]]
    tasks = [
        rest_of(orders[0], 0),
        rest_of(orders[1], 0),
        in_two(down_rest, down_order),
        in_two(up_rest, up_order),
        [lambda x: x] * LATE + [lambda x, step=step: [x[0] + hop_batch(x[0], step)] for step in steps],
    ]
    for turn in range(max(len(task) for task in tasks)):
        anchors = (values[0][0], values[1][0]) + ((d_tokens,) if turn == 0 else ())
        if turn == IDLE + 2:
            anchors += (values[2][-1], values[3][-1])
        values = [
            task[turn](after(value, *anchors)) if turn < len(task) else value for value, task in zip(values, tasks)
        ]
    d_parts = [values[0][0].astype(f32), values[1][0].astype(f32)]
    d_w_down, d_w_up = values[2][0].astype(f32), values[3][0].astype(f32)
    minor = values[4][0]
    d_w_query, d_w_key = d_parts[0][0:192].T, d_parts[0][192:384].T
    d_w_value, d_w_out = d_parts[1][0:192].T, d_parts[1][192:384]

    return (
        output[None],
        d_tokens[None],
        d_w_query,
        d_w_key,
        d_w_value,
        d_w_out,
        minor[1:4, 0:TAPS],
        d_w_up,
        minor[0],
        d_w_down,
        minor[4],
        minor[5],
        minor[6],
        minor[7],
    )


def solution(mesh):
    return jax.shard_map(
        functools.partial(local, mesh.shape["batch"]),
        mesh=mesh,
        in_specs=(
            P("batch", "head", None),
            P("batch"),
            P(None, "head"),
            P(None, "head"),
            P(None, "head"),
            P("head", None),
            P("head", None),
            P(None, "head"),
            P("head"),
            P("head", None),
            P(),
            P(),
            P(),
            P(),
            P("batch", "head", None),
        ),
        out_specs=(
            P("batch", "head", None),
            P("batch", "head", None),
            P(None, "head"),
            P(None, "head"),
            P(None, "head"),
            P("head", None),
            P("head", None),
            P(None, "head"),
            P("head"),
            P("head", None),
            P(),
            P(),
            P(),
            P(),
        ),
        check_vma=False,
    )
```

```python
import functools

import jax
import jax.numpy as jnp
from jax import lax
from jax.experimental import pallas as pl
from jax.experimental.pallas import tpu as pltpu
from jax.sharding import PartitionSpec as P

f32 = jnp.float32
bf16 = jnp.bfloat16
HEAD_DIM = 64
LANDMARKS = 64
NEWTON = 6
TAPS = 65
HALO = TAPS // 2
EARLY = 1
LATE = 2
IDLE = 0
GROUP = 256
NN = ((1,), (0,))
NT = ((1,), (1,))
TN = ((0,), (0,))
VMEM = pltpu.VMEM
ANY = pl.ANY


def dot(a, b, dims=NN):
    return lax.dot_general(a, b, (dims, ((), ())), preferred_element_type=f32)


def split(x):
    high = x.astype(bf16)
    return high, (x - high.astype(f32)).astype(bf16)


def mm(a, b, dims=NN):
    a_high, a_low = split(a)
    b_high, b_low = split(b)
    return dot(a_high, b_high, dims) + (dot(a_high, b_low, dims) + dot(a_low, b_high, dims))


def mm_left(a, b, dims=NN):
    a_high, a_low = split(a)
    return dot(a_high, b, dims) + dot(a_low, b, dims)


def iota(shape, dim):
    return lax.broadcasted_iota(jnp.int32, shape, dim)


def call(body, outs, ins, scratch=(), flops=0, size=0, limit=40, name=None, smem=()):
    specs = [
        pl.BlockSpec(memory_space=pltpu.SMEM) if i in smem else pl.BlockSpec(memory_space=space)
        for i, (space, _) in enumerate(ins)
    ]
    return pl.pallas_call(
        body,
        out_shape=[jax.ShapeDtypeStruct(s, d) for s, d in outs],
        in_specs=specs,
        out_specs=[pl.BlockSpec(memory_space=VMEM)] * len(outs),
        scratch_shapes=list(scratch),
        compiler_params=pltpu.CompilerParams(vmem_limit_bytes=limit << 20),
        cost_estimate=pl.CostEstimate(flops=flops, bytes_accessed=size, transcendentals=0),
        name=name,
    )(*[value for _, value in ins])


def call_many(parts, name):
    ins = [value for part in parts for value in part[2]]
    outs = [value for part in parts for value in part[1]]
    scratch = [value for part in parts for value in part[3]]
    smem, first = [], 0
    for part in parts:
        smem += [first + i for i in part[4]]
        first += len(part[2])

    def body(*refs):
        groups = [refs[: len(ins)], refs[len(ins) : len(ins) + len(outs)], refs[len(ins) + len(outs) :]]
        at = [0, 0, 0]
        for part in parts:
            mine = []
            for group, kind in ((0, 2), (1, 1), (2, 3)):
                mine += groups[group][at[group] : at[group] + len(part[kind])]
                at[group] += len(part[kind])
            part[0](*mine)

    results = call(body, outs, ins, scratch, flops=int(5e9), size=10 << 20, name=name, smem=tuple(smem), limit=48)
    split_results, first = [], 0
    for part in parts:
        split_results.append(results[first : first + len(part[1])])
        first += len(part[1])
    return split_results


def block_mask():
    return (iota((GROUP, GROUP), 0) >> 6) == (iota((GROUP, GROUP), 1) >> 6)


def spread(x):
    return jnp.where(block_mask(), jnp.concatenate([x, x, x, x], axis=0), 0.0)


def fold(x):
    kept = jnp.where(block_mask(), x, 0.0)
    return kept[0:64] + kept[64:128] + kept[128:192]


def rows_of(info, count, first):
    return info[1] + first + iota((count, 1), 0)


def landmark_kernel(p0, p1, p2, p3, wt, lm, pool, chain):
    pooled = (p0[...].astype(f32) + p1[...].astype(f32)) + (p2[...].astype(f32) + p3[...].astype(f32))
    pool[...] = pooled.astype(bf16)
    high, low = split(pooled)
    both = jnp.concatenate([high, low], axis=0)
    lm[...] = jnp.zeros_like(lm)
    matrices, starts = [], []
    for head in range(3):
        pair = []
        for kind in range(2):
            rows = wt[kind * 192 + head * 64 : kind * 192 + head * 64 + 64]
            out = dot(both, rows, NT)
            out = out[0:64] + out[64:128]
            lm[:, kind * GROUP + head * 64 : kind * GROUP + head * 64 + 64] = out
            pair.append(out)
        scores = mm(pair[0], pair[1], NT) * 0.125
        raised = jnp.exp(scores - jnp.max(scores, axis=1, keepdims=True))
        matrix = raised / jnp.sum(raised, axis=1, keepdims=True)
        column = jnp.max(jnp.sum(matrix, axis=0, keepdims=True), axis=1, keepdims=True)
        row = jnp.max(jnp.sum(matrix, axis=1, keepdims=True), axis=0, keepdims=True)
        matrices.append(matrix)
        starts.append(matrix.T / (column * row))
    eye = (iota((64, 64), 0) == iota((64, 64), 1)).astype(f32)

    def step(it, iterates):
        results = []
        for head in range(3):
            z = iterates[head]
            product = mm(matrices[head], z)
            inner1 = 7.0 * eye - product
            inner2 = 15.0 * eye - mm(product, inner1)
            inner3 = 13.0 * eye - mm(product, inner2)
            chain[it, 0, head] = z
            chain[it, 1, head] = product
            chain[it, 2, head] = inner2
            chain[it, 3, head] = inner3
            results.append(0.25 * mm(z, inner3))
        return tuple(results)

    finals = lax.fori_loop(0, NEWTON, step, tuple(starts))
    for head in range(3):
        lm[:, 2 * GROUP + head * 64 : 2 * GROUP + head * 64 + 64] = finals[head]


def inverse_back_kernel(x0, x1, wst_all, lm, chain, partial, out):
    total = x0[0] + x1[1]
    eye = (iota((64, 64), 0) == iota((64, 64), 1)).astype(f32)
    weight = wst_all[0]
    out[...] = partial[...].astype(bf16)
    grads, matrices, queries, keys = [], [], [], []
    for head in range(3):
        at = slice(head * 64, head * 64 + 64)
        grads.append(mm(total[:, at], weight[:, at], NT))
        query = lm[:, head * 64 : head * 64 + 64]
        key = lm[:, GROUP + head * 64 : GROUP + head * 64 + 64]
        scores = mm(query, key, NT) * 0.125
        raised = jnp.exp(scores - jnp.max(scores, axis=1, keepdims=True))
        matrices.append(raised / jnp.sum(raised, axis=1, keepdims=True))
        queries.append(query)
        keys.append(key)

    def step(count, carried):
        it = NEWTON - 1 - count
        results = []
        for head in range(3):
            dz_next, da = carried[2 * head], carried[2 * head + 1]
            z = chain[it, 0, head]
            product = chain[it, 1, head]
            inner1 = 7.0 * eye - product
            inner2 = chain[it, 2, head]
            inner3 = chain[it, 3, head]
            dz_next = 0.25 * dz_next
            dz = mm(dz_next, inner3, NT)
            d3 = -mm(z, dz_next, TN)
            d2 = -mm(product, d3, TN)
            d1 = mm(product, d2, TN)
            dp = mm(d3, inner2, NT) + mm(d2, inner1, NT) - d1
            da = da + mm(dp, z, NT)
            dz = dz + mm(matrices[head], dp, TN)
            results += [dz, da]
        return tuple(results)

    first = []
    for head in range(3):
        first += [grads[head], jnp.zeros((64, 64), f32)]
    last = lax.fori_loop(0, NEWTON, step, tuple(first))
    for head in range(3):
        dz, da = last[2 * head], last[2 * head + 1]
        matrix = matrices[head]
        columns = jnp.sum(matrix, axis=0, keepdims=True)
        rows = jnp.sum(matrix, axis=1, keepdims=True)
        column = jnp.max(columns, axis=1, keepdims=True)
        row = jnp.max(rows, axis=0, keepdims=True)
        scale = 1.0 / (column * row)
        da = da + dz.T * scale
        d_scale = -jnp.sum(jnp.sum(dz * matrix.T, axis=1, keepdims=True), axis=0, keepdims=True) * scale * scale
        column_hit = (columns == column).astype(f32)
        row_hit = (rows == row).astype(f32)
        da = da + d_scale * row * column_hit / jnp.sum(column_hit, axis=1, keepdims=True)
        da = da + d_scale * column * row_hit / jnp.sum(row_hit, axis=0, keepdims=True)
        ds = matrix * (da - jnp.sum(da * matrix, axis=1, keepdims=True)) * 0.125
        for at, value in ((head * 64, mm(ds, keys[head])), (GROUP + head * 64, mm(ds, queries[head], TN))):
            out[0, :, at : at + 64] = (partial[0, :, at : at + 64] + value).astype(bf16)


PROJECTION = ((0, 192, 0), (192, 192, GROUP), (384, 192, 2 * GROUP))


def split_copies(refs, parts, held, sems, side):
    own, across, across_x, other, both, both_x = refs
    half = own.shape[1] // 2
    mine = pl.ds(pl.multiple_of(side * half, half), half)
    rest = pl.ds(pl.multiple_of((1 - side) * half, half), half)
    blocks = [[], [], [], []]
    for n, (row, rows, to) in enumerate(parts):
        first = pl.ds(row - parts[0][0], rows)
        source, to = pl.ds(row, rows), pl.ds(to, rows)
        blocks[0].append(pltpu.make_async_copy(own.at[first], held.at[0, to], sems.at[0, n, 0]))
        blocks[2].append(pltpu.make_async_copy(other.at[source], held.at[2, to], sems.at[2, n, 0]))
        for i, near, far in ((1, across, across_x), (3, both, both_x)):
            blocks[i].append(pltpu.make_async_copy(near.at[source], held.at[i, to, mine], sems.at[i, n, 0]))
            blocks[i].append(pltpu.make_async_copy(far.at[source], held.at[i, to, rest], sems.at[i, n, 1]))
    return blocks


def start(copies):
    for block in copies:
        for copy in block:
            copy.start()


def wait(copies, i):
    for block in range(4):

        @pl.when(i == block)
        def _():
            for copy in copies[block]:
                copy.wait()


def zero_gaps(held, kinds):
    for i in range(4):
        for kind in range(kinds):
            held[i, kind * GROUP + 192 : kind * GROUP + 256, :] = jnp.zeros((64, held.shape[2]), bf16)


def project_kernel(info, tokens, before, after, w0, w1, w2, w3, w4, w5, q_out, k_out, v_out, held, sems):
    count = tokens.shape[0]
    copies = split_copies((w0, w1, w2, w3, w4, w5), PROJECTION, held, sems, info[2])
    start(copies)
    zero_gaps(held, 3)
    valid = (rows_of(info, count, 0) < info[0]).astype(f32)
    valid_before = (rows_of(info, HALO, -HALO) < info[0]).astype(f32)
    valid_after = (rows_of(info, HALO, count) < info[0]).astype(f32)

    def body(i, _):
        wait(copies, i)
        for kind, out in ((0, q_out), (1, k_out)):
            out[i] = (dot(tokens[...], held[i, kind * GROUP : kind * GROUP + GROUP], NT) * valid).astype(bf16)
        wv = held[i, 2 * GROUP : 3 * GROUP]
        v_out[i, HALO : HALO + count] = (dot(tokens[...], wv, NT) * valid).astype(bf16)
        v_out[i, 0:HALO] = (dot(before[...], wv, NT) * valid_before).astype(bf16)
        v_out[i, HALO + count : 2 * HALO + count] = (dot(after[...], wv, NT) * valid_after).astype(bf16)
        v_out[i, 2 * HALO + count :] = jnp.zeros((v_out.shape[1] - 2 * HALO - count, GROUP), bf16)
        return 0

    lax.fori_loop(0, 4, body, 0)


def third_scores(info, lm, k_ref, i):
    count = k_ref.shape[1]
    valid = info[1] + iota((1, count), 1) < info[0]
    queries = spread(lm[i, :, 0:GROUP])
    return jnp.where(valid, mm_left(queries, k_ref[i], NT) * 0.125, -1e30)


def third_kernel(info, lm, k_ref, v_ref, pay):
    count = k_ref.shape[1]
    lane = iota((64, GROUP), 1)

    def body(i, _):
        scores = third_scores(info, lm, k_ref, i)
        top = jnp.max(scores, axis=1, keepdims=True)
        raised = jnp.exp(scores - top)
        total = jnp.sum(raised, axis=1, keepdims=True)
        packed = fold(mm_left(raised, v_ref[i, HALO : HALO + count]) / total)
        for stat, base in ((top, 192), (total, 216)):
            for term in range(3):
                part = stat.astype(bf16).astype(f32)
                stat = stat - part
                for head in range(3):
                    packed = jnp.where(lane == base + 8 * term + head, part[head * 64 : head * 64 + 64], packed)
        pay[i] = packed.astype(bf16)
        return 0

    lax.fori_loop(0, 4, body, 0)


def first_scores(lm, q_ref, i):
    keys = spread(lm[i, :, GROUP : 2 * GROUP])
    count = q_ref.shape[1]
    scores = (mm_left(keys, q_ref[i], NT) * 0.125).reshape(4, 64, count)
    raised = jnp.exp(scores - jnp.max(scores, axis=1, keepdims=True))
    return raised / jnp.sum(raised, axis=1, keepdims=True)


def toeplitz(row):
    return pltpu.roll(jnp.broadcast_to(row, (128, GROUP)), 0, 1, stride=1, stride_axis=0)


def head_select(x, rows):
    lane = iota((rows, GROUP), 1) >> 6
    out = jnp.where(lane == 0, x[0:rows], 0.0)
    out = jnp.where(lane == 1, x[rows : 2 * rows], out)
    return jnp.where(lane == 2, x[2 * rows : 3 * rows], out)


def context_kernel(p0, p1, p2, p3, lm, q_ref, v_ref, small, ctx, wst, x_out):
    count = q_ref.shape[1]
    lane = iota((64, GROUP), 1)

    def body(i, _):
        parts = [p[i ^ n].astype(f32) for n, p in enumerate((p0, p1, p2, p3))]

        def stat(part, at):
            return part[:, at : at + 1] + part[:, at + 8 : at + 9] + part[:, at + 16 : at + 17]

        factors = [jnp.zeros((64, GROUP), f32) for _ in range(4)]
        stats = jnp.zeros((64, GROUP), f32)
        for head in range(3):
            tops = [stat(part, 192 + head) for part in parts]
            top = jnp.maximum(jnp.maximum(tops[0], tops[1]), jnp.maximum(tops[2], tops[3]))
            scales = [stat(part, 216 + head) * jnp.exp(t - top) for part, t in zip(parts, tops)]
            total = sum(scales)
            mine = (lane >> 6) == head
            factors = [jnp.where(mine, s / total, f) for s, f in zip(scales, factors)]
            stats = jnp.where(lane == 192 + head, top, stats)
            stats = jnp.where(lane == 196 + head, total, stats)
        weight = sum(part * f for part, f in zip(parts, factors))
        wst[i] = jnp.where(lane < 192, weight, stats)
        mixed = mm(spread(lm[i, :, 2 * GROUP : 3 * GROUP]), spread(weight))
        x_out[i] = fold(mixed)
        first = first_scores(lm, q_ref, i).reshape(GROUP, count)
        main = mm(first, mixed, TN)
        bands = [toeplitz(small[i, 1 + head : 2 + head, 0:GROUP]) for head in range(3)]
        high, low = split(jnp.concatenate(bands, axis=0))
        for block in range(count // 128):
            window = v_ref[i, block * 128 : block * 128 + 256]
            conv = dot(high, window) + dot(low, window)
            ctx[i, block * 128 : block * 128 + 128] = (
                main[block * 128 : block * 128 + 128] + head_select(conv, 128)
            ).astype(bf16)
        return 0

    lax.fori_loop(0, 4, body, 0)


def first_back_kernel(
    info, g_ref, before, after, o0, o1, o2, o3, o4, o5, lm, q_ref, v_ref, small, x_in, dx, dq, dkl, dv, dtaps, held, sems, ext, dctx
):
    count = g_ref.shape[0]
    width = g_ref.shape[1]
    copies = split_copies((o0, o1, o2, o3, o4, o5), ((0, 192, 0),), held, sems, info[2])
    start(copies)
    zero_gaps(held, 1)
    valid = (rows_of(info, count, 0) < info[0]).astype(f32)
    ext[0:HALO] = before[...]
    ext[HALO : HALO + count] = g_ref[...]
    ext[HALO + count : 2 * HALO + count] = after[...]
    ext[2 * HALO + count :] = jnp.zeros((ext.shape[0] - 2 * HALO - count, width), bf16)
    lane = iota((128, GROUP), 1) >> 6
    flip = (iota((128, 128), 0) + iota((128, 128), 1) == 127).astype(bf16)

    def body(i, _):
        wait(copies, i)
        dctx[...] = dot(ext[...], held[i], NT)
        own = dctx[HALO : HALO + count]
        own_high = own.astype(bf16)
        first = first_scores(lm, q_ref, i)
        flat = first.reshape(GROUP, count)
        dx[i] = fold(dot(flat.astype(bf16), own_high))
        dfirst = dot(spread(x_in[i]).astype(bf16), own_high, NT)
        dfirst = dfirst.reshape(4, 64, count)
        ds = first * (dfirst - jnp.sum(first * dfirst, axis=1, keepdims=True)) * 0.125
        ds = ds.reshape(GROUP, count).astype(bf16)
        keys = (spread(lm[i, :, GROUP : 2 * GROUP])).astype(bf16)
        dquery = dot(ds, keys, TN)
        dq[i] = (dquery * valid).astype(bf16)
        dkl[i] = fold(dot(ds, q_ref[i]))
        bands = [toeplitz(small[i, 4 + head : 5 + head, 0:GROUP]) for head in range(3)]
        high = jnp.concatenate(bands, axis=0).astype(bf16)
        gram = jnp.zeros((384, GROUP), f32)
        for block in range(count // 128):
            conv = dot(high, dctx[block * 128 : block * 128 + 256].astype(bf16))
            dv[i, block * 128 : block * 128 + 128] = head_select(conv, 128)
            piece = dctx[HALO + block * 128 : HALO + block * 128 + 128]
            stacked = jnp.concatenate([jnp.where(lane == head, piece, 0.0) for head in range(3)], axis=0)
            gram = gram + dot(stacked.astype(bf16), v_ref[i, block * 128 : block * 128 + 256], NT)
        dtaps[i] = jnp.zeros((8, GROUP), f32)
        for head in range(3):
            part_high, part_low = split(gram[head * 128 : head * 128 + 128])
            upturned = dot(flip, part_high) + dot(flip, part_low)
            straight = pltpu.roll(upturned, GROUP - 127, 1, stride=1, stride_axis=0)
            summed = jnp.sum(straight, axis=0, keepdims=True)
            dtaps[i, 1 + head : 2 + head, :] = jnp.where(iota((1, GROUP), 1) < TAPS, summed, 0.0)
        return 0

    lax.fori_loop(0, 4, body, 0)


def third_back_kernel(info, x0, x1, lm, wst, k_ref, v_ref, dvc, dq, dkl, ctx, joint, send, partial):
    count = k_ref.shape[1]
    valid = (rows_of(info, count, 0) < info[0]).astype(f32)
    none = jnp.zeros((64, 1), f32)

    def body(i, _):
        dx = spread(x0[i] + x1[i ^ 1])
        dweight = mm(spread(lm[i, :, 2 * GROUP : 3 * GROUP]), dx, TN)
        stats = wst[i]
        weight = spread(jnp.where(iota((64, GROUP), 1) < 192, stats, 0.0))
        inner = jnp.sum(dweight * weight, axis=1, keepdims=True)
        top = jnp.concatenate([stats[:, 192 + head : 193 + head] for head in range(3)] + [none], axis=0)
        total = jnp.concatenate([stats[:, 196 + head : 197 + head] for head in range(3)] + [none + 1.0], axis=0)
        scores = third_scores(info, lm, k_ref, i)
        third = jnp.exp(scores - top) / total
        dw_high = dweight.astype(bf16)
        values = v_ref[i, HALO : HALO + count]
        dthird = dot(dw_high, values, NT)
        ds = (third * (dthird - inner) * 0.125).astype(bf16)
        queries = (spread(lm[i, :, 0:GROUP])).astype(bf16)
        dkey = dot(ds, queries, TN)
        partial[i, :, 0:GROUP] = fold(dot(ds, k_ref[i]))
        partial[i, :, GROUP : 2 * GROUP] = dkl[i]
        dvalues = dot(third.astype(bf16), dw_high, TN)
        joint[i, :, 0:GROUP] = dq[i]
        joint[i, :, GROUP : 2 * GROUP] = (dkey * valid).astype(bf16)
        joint[i, :, 2 * GROUP : 3 * GROUP] = ((dvalues + dvc[i]) * valid).astype(bf16)

        @pl.when(i >= 2)
        def _():
            send[i - 2, :, 0 : 3 * GROUP] = joint[i]
            send[i - 2, :, 3 * GROUP : 4 * GROUP] = ctx[i]

        return 0

    lax.fori_loop(0, 4, body, 0)


def token_back_kernel(info, l0, l1, joint, dres, w0, w1, w2, w3, w4, w5, out, held, sems):
    copies = split_copies((w0, w1, w2, w3, w4, w5), PROJECTION, held, sems, info[2])
    start(copies)
    zero_gaps(held, 3)
    count = joint.shape[1]
    mark = iota((1, 64), 1)
    low = (mark * info[0]) >> 6
    high = ((mark + 1) * info[0]) >> 6
    pos = rows_of(info, count, 0)
    member = ((pos >= low) & (pos < high)).astype(bf16)
    row = iota((64, 1), 0)
    width = ((((row + 1) * info[0]) >> 6) - ((row * info[0]) >> 6)).astype(f32)
    out[...] = dres[...]

    def body(i, pooled):
        wait(copies, i)
        out[...] += dot(joint[i], held[i])
        marks = (l0[i].astype(f32) + l1[i ^ 1].astype(f32)) / width
        return pooled + mm_left(marks, held[i, 0 : 2 * GROUP])

    pooled = lax.fori_loop(0, 4, body, jnp.zeros((64, out.shape[1]), f32))
    pooled_high, pooled_low = split(pooled)
    out[...] += dot(member, pooled_high) + dot(member, pooled_low)


def moments(x):
    centered = x - jnp.mean(x, axis=-1, keepdims=True)
    variance = jnp.mean(centered * centered, axis=-1, keepdims=True)
    inverse = lax.rsqrt(variance + 1e-05)
    return centered * inverse, inverse


def attended_kernel(info, ctx, tokens, gain, shift, o0, o1, o2, o3, o4, o5, pre, normed, low, held, sems):
    copies = split_copies((o0, o1, o2, o3, o4, o5), ((0, 192, 0),), held, sems, info[2])
    start(copies)
    zero_gaps(held, 1)
    pre[...] = tokens[...].astype(f32)

    def body(i, _):
        wait(copies, i)
        pre[...] += dot(ctx[i], held[i])
        return 0

    lax.fori_loop(0, 4, body, 0)
    unit, _ = moments(pre[...])
    result = unit * gain[...] + shift[...]
    normed[...] = result
    low[...] = result.astype(bf16)


def gelu_parts(u):
    cdf = 0.5 + 0.5 * lax.erf(u * 0.7071067811865476)
    pdf = jnp.exp(u * u * -0.5) * 0.3989422804014327
    return u * cdf, cdf + u * pdf


def up_kernel(info, low, small, w0, w1, w2, w3, w4, w5, hidden, slope, send, held, sems):
    copies = split_copies((w0, w1, w2, w3, w4, w5), ((192, held.shape[1], 0),), held, sems, info[2])
    start(copies)

    def body(i, _):
        wait(copies, i)
        for chunk in range(3):
            at = slice(chunk * 256, chunk * 256 + 256)
            upward = dot(low[...], held[i, :, at]) + small[i, 0:1, at]
            value, derivative = gelu_parts(upward)
            hidden[i, :, at] = value.astype(bf16)
            slope[i, :, at] = derivative.astype(bf16)

        @pl.when(i >= 2)
        def _():
            send[i - 2] = hidden[i]

        return 0

    send[2] = low[...]
    lax.fori_loop(0, 4, body, 0)


def norm_back(g, gain, unit, inverse):
    scaled = g * gain
    mean1 = jnp.mean(scaled, axis=-1, keepdims=True)
    mean2 = jnp.mean(scaled * unit, axis=-1, keepdims=True)
    return (scaled - mean1 - unit * mean2) * inverse


def down_kernel(info, hidden, normed, grad, gain, shift, w0, w1, w2, w3, w4, w5, out, dsum, dlow, sums, held, sems, acc):
    copies = split_copies((w0, w1, w2, w3, w4, w5), ((0, held.shape[1], 0),), held, sems, info[2])
    start(copies)
    acc[...] = normed[...]

    def body(i, _):
        wait(copies, i)
        acc[...] += dot(hidden[i], held[i])
        return 0

    lax.fori_loop(0, 4, body, 0)
    unit, inverse = moments(acc[...])
    out[...] = (unit * gain[...] + shift[...]).astype(bf16)
    g = grad[...].astype(f32)
    back = norm_back(g, gain[...], unit, inverse)
    dsum[...] = back
    dlow[...] = back.astype(bf16)
    sums[...] = jnp.zeros_like(sums)
    sums[0:1] = jnp.sum(g * unit, axis=0, keepdims=True)
    sums[1:2] = jnp.sum(g, axis=0, keepdims=True)


def hidden_back_kernel(info, dlow, slope, w0, w1, w2, w3, w4, w5, du, send, sums, held, sems):
    copies = split_copies((w0, w1, w2, w3, w4, w5), ((0, held.shape[1], 0),), held, sems, info[2])
    start(copies)
    sums[...] = jnp.zeros_like(sums)

    def body(i, _):
        wait(copies, i)
        for chunk in range(3):
            at = slice(chunk * 256, chunk * 256 + 256)
            back = dot(dlow[...], held[i, at, :], NT) * slope[i, :, at].astype(f32)
            back = back.astype(bf16)
            du[i, :, at] = back
            sums[i, 0:1, at] = jnp.sum(back.astype(f32), axis=0, keepdims=True)

        @pl.when(i >= 2)
        def _():
            send[i - 2] = du[i]

        return 0

    send[2] = dlow[...]
    lax.fori_loop(0, 4, body, 0)


def residual_back_kernel(info, du, dsum, pre, gain, w0, w1, w2, w3, w4, w5, dres, dlow, sums, held, sems, acc):
    copies = split_copies((w0, w1, w2, w3, w4, w5), ((192, held.shape[1], 0),), held, sems, info[2])
    start(copies)
    acc[...] = dsum[...]

    def body(i, _):
        wait(copies, i)
        acc[...] += dot(du[i], held[i], NT)
        return 0

    lax.fori_loop(0, 4, body, 0)
    unit, inverse = moments(pre[...])
    g = acc[...]
    back = norm_back(g, gain[...], unit, inverse)
    dres[...] = back
    dlow[...] = back.astype(bf16)
    sums[...] = jnp.zeros_like(sums)
    sums[0:1] = jnp.sum(g * unit, axis=0, keepdims=True)
    sums[1:2] = jnp.sum(g, axis=0, keepdims=True)


def feed_grad_kernel(
    pick, hidden, hidden_other, gd, du_other, du, low, down0, down1, up0, up1, left, right, sems
):
    half = left.shape[-1]
    copies = []

    def bring(source, target):
        copy = pltpu.make_async_copy(source, target, sems.at[len(copies)])
        copy.start()
        copies.append(copy)

    for part, sources in ((0, (hidden.at[0], hidden_other.at[0], hidden.at[1], hidden_other.at[1])), (1, (low, hidden_other.at[2]))):
        columns = pl.ds(pl.multiple_of(pick[part] * half, half), half)
        for n, source in enumerate(sources):
            bring(source.at[:, columns], left.at[4 * part + n])
        if part == 0:
            bring(gd, right.at[0])
            bring(du_other.at[2], right.at[1])
        else:
            for j in range(2):
                bring(du.at[j], right.at[2 + 2 * j])
                bring(du_other.at[j], right.at[3 + 2 * j])
    for copy in copies[:6]:
        copy.wait()

    def body(n, _):
        @pl.when(n == 2)
        def _():
            for copy in copies[6:]:
                copy.wait()

        down = n < 2
        at_left = jnp.where(down, 2 * n, 4)
        at_right = jnp.where(down, 0, 2 * n - 2)
        total = dot(left[at_left], right[at_right], TN) + dot(left[at_left + 1], right[at_right + 1], TN)
        total = total.astype(bf16)
        for k, out in enumerate((down0, down1, up0, up1)):

            @pl.when(n == k)
            def _():
                out[...] = total

        return 0

    lax.fori_loop(0, 4, body, 0)


def feed_grad(pick, hidden, hidden_other, gd, du_other, du, low):
    count, width = gd.shape
    return (
        feed_grad_kernel,
        [((width // 2, width), bf16)] * 4,
        [(VMEM, pick.astype(jnp.int32))] + [(ANY, x) for x in (hidden, hidden_other, gd, du_other, du, low)],
        [
            pltpu.VMEM((6, count, width // 2), bf16),
            pltpu.VMEM((6, count, width), bf16),
            pltpu.SemaphoreType.DMA((12,)),
        ],
        (0,),
    )


def joint_grad_kernel(joint, other, ctx, tokens, tokens_other, g, g_other, first, second):
    def body(kind, _):
        at = pl.ds(pl.multiple_of(kind * GROUP, GROUP), GROUP)
        total = dot(joint[0, :, at], tokens[...], TN) + dot(other[0, :, at], tokens_other[...], TN)
        total = total[0:192].astype(bf16)

        @pl.when(kind < 2)
        def _():
            first[pl.ds(pl.multiple_of(kind * 192, 192), 192)] = total

        @pl.when(kind == 2)
        def _():
            second[0:192] = total

        return 0

    lax.fori_loop(0, 3, body, 0)
    total = dot(ctx[0], g[...], TN) + dot(other[0, :, 3 * GROUP : 4 * GROUP], g_other[...], TN)
    second[192:384] = total[0:192].astype(bf16)


def joint_grad(joint, other, ctx, tokens, tokens_other, g, g_other, block, name):
    count, width = tokens.shape
    whole = pl.BlockSpec((count, width), lambda j: (0, 0))
    return pl.pallas_call(
        joint_grad_kernel,
        grid=(1,),
        out_shape=[jax.ShapeDtypeStruct((width // 2, width), bf16)] * 2,
        in_specs=[
            pl.BlockSpec((1, count, 3 * GROUP), lambda j: (block, 0, 0)),
            pl.BlockSpec((1, count, 4 * GROUP), lambda j: (block, 0, 0)),
            pl.BlockSpec((1, count, GROUP), lambda j: (block, 0, 0)),
            whole,
            whole,
            whole,
            whole,
        ],
        out_specs=[pl.BlockSpec((width // 2, width), lambda j: (0, 0))] * 2,
        compiler_params=pltpu.CompilerParams(vmem_limit_bytes=40 << 20),
        cost_estimate=pl.CostEstimate(flops=16 * count * GROUP * width, bytes_accessed=8 << 20, transcendentals=0),
        name=name,
    )(joint, other, ctx, tokens, tokens_other, g, g_other)


HOP = {1: 2, 2: 1, 3: 3}


def hop(x, step):
    return lax.ppermute(x, "head", [(i, i ^ HOP[step]) for i in range(4)])


def after(x, *deps):
    return lax.optimization_barrier((x,) + deps)[0]


def local(
    batch_count,
    tokens,
    lengths,
    w_query,
    w_key,
    w_value,
    w_out,
    conv_taps,
    w_up,
    b_up,
    w_down,
    gain_attn,
    shift_attn,
    gain_ffn,
    shift_ffn,
    grad_out,
):
    tokens = tokens[0]
    grad_out = grad_out[0]
    count, width = tokens.shape
    ext = count + 128
    length = lengths[0]
    place = lax.axis_index("head")
    batch = lax.axis_index("batch")
    core = place & 1
    side = batch & 1
    info = jnp.stack([length, place * count, side]).astype(jnp.int32)
    gain_attn, shift_attn, gain_ffn, shift_ffn = (
        x.reshape(1, width) for x in (gain_attn, shift_attn, gain_ffn, shift_ffn)
    )
    vm, an = VMEM, ANY

    def hop_batch(x, step):
        return lax.ppermute(x, "batch", [(i, i ^ step) for i in range(batch_count)])

    def neighbours(x, other):
        first = core == 0
        far = lax.ppermute(jnp.where(first, x[:HALO], x[-HALO:]), "head", [(1, 2), (2, 1)])
        return jnp.where(first, far, other[-HALO:]), jnp.where(first, other[:HALO], far)

    marks = jnp.arange(LANDMARKS + 1, dtype=jnp.int32) * length // LANDMARKS
    positions = info[1] + jnp.arange(count, dtype=jnp.int32)
    member = (positions[None, :] >= marks[:-1, None]) & (positions[None, :] < marks[1:, None])
    pooled = jnp.dot(member.astype(bf16), tokens, preferred_element_type=f32)
    pooled = (pooled / (marks[1:] - marks[:-1]).astype(f32)[:, None]).astype(bf16)
    pools = [pooled] + [hop(pooled, n) for n in (1, 2, 3)]

    taps = jnp.pad(conv_taps, ((0, 0), (0, width - TAPS)))
    taps_back = jnp.pad(conv_taps[:, ::-1], ((0, 0), (0, width - TAPS)))
    small_own = jnp.concatenate([b_up[None], taps, taps_back, jnp.zeros((1, width), f32)], axis=0)
    term1 = small_own.astype(bf16)
    rest = small_own - lax.reduce_precision(small_own, 8, 7)
    term2 = rest.astype(bf16)
    term3 = (rest - lax.reduce_precision(rest, 8, 7)).astype(bf16)
    wt_own = jnp.concatenate(
        [w_query.T, w_key.T, w_value.T, term1, term2, term3, jnp.zeros((8, width), bf16)], axis=0
    )
    tokens_other = hop(tokens, 2)
    before, behind = neighbours(tokens, tokens_other)

    def column_half(own):
        return lax.dynamic_slice_in_dim(own, side * (width // 2), width // 2, 1)

    wt_other = hop(wt_own, 2)
    wt_across = hop(after(column_half(wt_own), *pools), 1)
    lm_own, pooled_low, iterates = call(
        landmark_kernel,
        [((64, 3 * GROUP), f32), ((64, width), bf16), ((NEWTON, 4, 3, 64, 64), f32)],
        [(vm, x) for x in pools] + [(vm, wt_own)],
        flops=int(1e9),
        size=4 << 20,
        name="landmarks",
    )
    lm_own = after(lm_own, wt_across, before, behind)
    lm_across = hop(lm_own, 1)
    wt_across_x = hop_batch(after(wt_across, pooled_low), 1)
    lm = jnp.stack([lm_own, lm_across, hop(lm_own, 2), hop(lm_across, 2)])
    wt = [wt_own, wt_across, wt_across_x, wt_other, hop(wt_across, 2), hop(wt_across_x, 2)]

    def small_of(block):
        return sum(block[576 + 8 * n : 584 + 8 * n].astype(f32) for n in range(3))

    def small_joined(near, far):
        near, far = small_of(near), small_of(far)
        first = side == 0
        return jnp.concatenate([jnp.where(first, near, far), jnp.where(first, far, near)], axis=1)

    small = jnp.stack(
        [small_of(wt[0]), small_joined(wt[1], wt[2]), small_of(wt[3]), small_joined(wt[4], wt[5])]
    )
    out_up_own = jnp.concatenate([w_out, after(w_up, pooled)], axis=0)
    out_up_across = hop(after(column_half(out_up_own), lm_across), 1)
    down_across = hop(after(column_half(w_down), lm_across), 1)
    q, k, v = call(
        project_kernel,
        [((4, count, GROUP), bf16), ((4, count, GROUP), bf16), ((4, ext, GROUP), bf16)],
        [(vm, info), (vm, tokens), (vm, before), (vm, behind)] + [(an, w) for w in wt],
        [pltpu.VMEM((4, 3 * GROUP, width), bf16), pltpu.SemaphoreType.DMA((4, 3, 2))],
        flops=2 * count * width * 3072,
        size=8 << 20,
        smem=(0,),
        name="project",
    )
    out_up_across_x = hop_batch(after(out_up_across, q), 1)
    (pay,) = call(
        third_kernel,
        [((4, 64, GROUP), bf16)],
        [(vm, info), (vm, lm), (vm, k), (vm, v)],
        flops=int(1e9),
        size=3 << 20,
        smem=(0,),
        name="third",
    )
    pays = [pay, hop(pay, 1), hop(pay, 2), hop(pay, 3)]
    ctx, wst, x_mid = call(
        context_kernel,
        [((4, count, GROUP), bf16), ((4, 64, GROUP), f32), ((4, 64, GROUP), f32)],
        [(vm, p) for p in pays] + [(vm, lm), (vm, q), (vm, v), (vm, small)],
        flops=int(3e9),
        size=5 << 20,
        name="context",
    )
    out_up_far = after((out_up_across, out_up_across_x), ctx)
    out_up = [out_up_across, out_up_across_x, hop(after(out_up_own, q), 2), hop(out_up_far[0], 2), hop(out_up_far[1], 2)]
    down_across_x = hop_batch(after(down_across, ctx), 1)
    wo = [(an, w) for w in [w_out] + out_up]
    wu = [(an, w) for w in [w_up] + out_up]
    out_scratch = [pltpu.VMEM((4, GROUP, width), bf16), pltpu.SemaphoreType.DMA((4, 1, 2))]
    wide = [pltpu.VMEM((4, width, width), bf16), pltpu.SemaphoreType.DMA((4, 1, 2))]
    acc = [pltpu.VMEM((count, width), f32)]

    pre, normed, normed_low = call(
        attended_kernel,
        [((count, width), f32), ((count, width), f32), ((count, width), bf16)],
        [(vm, info), (vm, ctx), (vm, tokens), (vm, gain_attn), (vm, shift_attn)] + wo,
        out_scratch,
        flops=2 * count * width * width,
        size=6 << 20,
        smem=(0,),
        name="attended",
    )
    down_far = after((down_across, down_across_x), normed_low)
    down = [down_across, down_across_x, hop(after(w_down, ctx), 2), hop(down_far[0], 2), hop(down_far[1], 2)]
    wd = [(an, w) for w in [w_down] + down]
    hidden, slope, hidden_send = call(
        up_kernel,
        [((4, count, width), bf16), ((4, count, width), bf16), ((3, count, width), bf16)],
        [(vm, info), (vm, normed_low), (vm, small)] + wu,
        wide,
        flops=2 * count * width * 3072,
        size=12 << 20,
        smem=(0,),
        name="up",
    )
    hidden_other = hop(hidden_send, 2)
    output, d_sum, gd, sums_ffn = call(
        down_kernel,
        [((count, width), bf16), ((count, width), f32), ((count, width), bf16), ((8, width), f32)],
        [(vm, info), (vm, hidden), (vm, normed), (vm, grad_out), (vm, gain_ffn), (vm, shift_ffn)] + wd,
        wide + acc,
        flops=2 * count * width * 3072,
        size=14 << 20,
        smem=(0,),
        name="down",
    )

    steps = [1 << n for n in range(batch_count.bit_length() - 1)]
    down_order = steps[:2] + ["y"] + steps[2:]
    up_order = steps[1:2] + steps[:1] + ["y"] + steps[2:]

    def bit(step):
        return (batch // step) & 1

    def send(x, step):
        return hop(x, 1) if step == "y" else hop_batch(x, step)

    def chain(pieces, step):
        received = [send(pieces[0], step)]
        for piece in pieces[1:]:
            received.append(send(after(piece, received[-1]), step))
        return received

    def add_all(kept, received):
        return [(a.astype(f32) + b.astype(f32)).astype(bf16) for a, b in zip(kept, received)]

    def split_for(pieces, step):
        if step == "y":
            return pieces[:1], pieces[1:]
        rows = pieces[0].shape[0] // 2
        kept = [lax.dynamic_slice_in_dim(x, bit(step) * rows, rows, 0) for x in pieces]
        sent = [lax.dynamic_slice_in_dim(x, (1 - bit(step)) * rows, rows, 0) for x in pieces]
        if len(pieces) > 1:
            sent = [jnp.stack(sent)]
        return kept, sent

    def exchange(pieces, step):
        kept, sent = split_for(pieces, step)
        received = send(sent[0], step)
        return kept, [received] if received.ndim == 2 else [received[n] for n in range(len(kept))]

    def grow(x, step):
        other = hop_batch(x, step)
        mine_last = bit(step) == 1
        return jnp.concatenate([jnp.where(mine_last, other, x), jnp.where(mine_last, x, other)], axis=0)

    def grow_first(x, step):
        return [x[0], hop_batch(x[0][: x[0].shape[0] // 2], step)]

    def grow_second(x, step):
        own, other = x
        other = jnp.concatenate([other, hop_batch(own[own.shape[0] // 2 :], step)], axis=0)
        mine_last = bit(step) == 1
        return [jnp.concatenate([jnp.where(mine_last, other, own), jnp.where(mine_last, own, other)], axis=0)]

    def in_two(task, order):
        return task[:-1] + [lambda x: x] * IDLE + [lambda x: grow_first(x, order[0]), lambda x: grow_second(x, order[0])]

    def rest_of(order, done):
        back = [step for step in order if step != "y"][::-1]
        return [lambda x, step=step: add_all(*exchange(x, step)) for step in order[done:]] + [
            lambda x, step=step: [grow(x[0], step)] for step in back
        ]

    du, du_send, sums_up = call(
        hidden_back_kernel,
        [((4, count, width), bf16), ((3, count, width), bf16), ((4, 8, width), f32)],
        [(vm, info), (vm, gd), (vm, slope)] + wd,
        wide,
        flops=2 * count * width * 3072,
        size=12 << 20,
        smem=(0,),
        name="hidden_back",
    )
    du_other = hop(du_send, 2)
    mine = jnp.stack([bit(down_order[0]), bit(up_order[0])])
    operands = (hidden, hidden_other, gd, du_other, du, normed_low)
    ((down_sent0, down_sent1, up_sent0, up_sent1),) = call_many([feed_grad(1 - mine, *operands)], "grad_sent")
    down_first = send(down_sent0, down_order[0])
    up_first = send(up_sent0, up_order[0])
    kept, (d_res, ga, sums_attn) = call_many(
        [
            feed_grad(mine, hidden, hidden_other, after(gd, down_sent0), du_other, du, normed_low),
            (
                residual_back_kernel,
                [((count, width), f32), ((count, width), bf16), ((8, width), f32)],
                [(vm, info), (vm, du), (vm, d_sum), (vm, pre), (vm, gain_attn)] + wu,
                wide + acc,
                (0,),
            ),
        ],
        "grad_kept",
    )
    down_kept, up_kept = kept[:2], kept[2:]
    ga, down_first, up_first = after((ga, down_first, up_first), d_res)
    ga_other = hop(ga, 2)
    ga_before, ga_behind = neighbours(ga, ga_other)
    down_second = send(after(down_sent1, down_first), down_order[0])
    up_second = send(after(up_sent1, up_first), up_order[0])
    dx, dq, dkl, dv_conv, dtaps = call(
        first_back_kernel,
        [
            ((4, 64, GROUP), f32),
            ((4, count, GROUP), bf16),
            ((4, 64, GROUP), f32),
            ((4, count, GROUP), f32),
            ((4, 8, GROUP), f32),
        ],
        [(vm, info), (vm, after(ga, down_first, up_first)), (vm, ga_before), (vm, ga_behind)]
        + wo
        + [(vm, lm), (vm, q), (vm, v), (vm, small), (vm, x_mid)],
        out_scratch + [pltpu.VMEM((ext, width), bf16), pltpu.VMEM((ext, GROUP), f32)],
        flops=int(5e9),
        size=10 << 20,
        smem=(0,),
        name="first_back",
    )

    def swap_core(x):
        other = hop(x, 2)
        return x.astype(f32) + jnp.concatenate([other[2:4], other[0:2]], axis=0).astype(f32)

    dx, down_second, up_second = after((dx, down_second, up_second), dtaps)
    dx = swap_core(after(dx, down_second, up_second))
    down_sent, up_sent = [down_first, down_second], [up_first, up_second]
    d_down = exchange(add_all(down_kept, down_sent), down_order[1])
    d_up = exchange(add_all(up_kept, up_sent), up_order[1])
    dx_across = hop(dx, 1)
    dx, dx_across, d_down, d_up = after((dx, dx_across, d_down, d_up), dx_across)
    d_down = exchange(add_all(*d_down), down_order[2])
    d_up = exchange(add_all(*d_up), up_order[2])
    dx, dx_across = after((dx, dx_across), d_down[0], d_up[0])
    joint, joint_send, partial = call(
        third_back_kernel,
        [((4, count, 3 * GROUP), bf16), ((2, count, 4 * GROUP), bf16), ((4, 64, 2 * GROUP), f32)],
        [(vm, info), (vm, dx), (vm, dx_across), (vm, lm), (vm, wst), (vm, k), (vm, v), (vm, dv_conv), (vm, dq)]
        + [(vm, dkl), (vm, ctx)],
        flops=int(5e9),
        size=8 << 20,
        smem=(0,),
        name="third_back",
    )
    joint_other = hop(after(joint_send, d_down[1], d_up[1]), 2)
    d_down, d_up = after((d_down, d_up), partial)
    d_down, d_up = add_all(*d_down), add_all(*d_up)
    operands = (after(joint, *d_down, *d_up), joint_other, ctx, tokens, tokens_other, ga, ga_other)
    sent = joint_grad(*operands, 1, "grad_joint_sent")
    joint_first = send(sent[0], "y")
    d_down, d_up = after((d_down, d_up), *sent)
    d_down, d_up = exchange(d_down, down_order[3]), exchange(d_up, up_order[3])
    (partial,) = call(
        inverse_back_kernel,
        [((4, 64, 2 * GROUP), bf16)],
        [(vm, dx), (vm, dx_across), (vm, wst), (vm, lm_own), (vm, iterates), (vm, after(partial, *sent))],
        flops=int(1e9),
        size=4 << 20,
        name="inverse_back",
    )
    partial = after(partial, joint_first, d_down[1], d_up[1])
    d_down, d_up = after((d_down, d_up), partial)
    d_down, d_up = add_all(*d_down), add_all(*d_up)
    partial = swap_core(partial).astype(bf16)
    partial_across = hop(partial, 1)
    down_rest, up_rest = rest_of(down_order, 4), rest_of(up_order, 4)
    if EARLY >= 1:
        d_down, d_up = after((d_down, d_up), partial)
        d_down, d_up = down_rest[0](d_down), up_rest[0](d_up)
        partial, partial_across = after((partial, partial_across), partial_across)
        down_rest, up_rest = down_rest[1:], up_rest[1:]
    else:
        partial, partial_across = after((partial, partial_across), partial_across)
    joint_second = send(after(sent[1], partial_across), "y")
    joint_sent = [joint_first, joint_second]
    joint_kept = joint_grad(*after(operands, partial), 0, "grad_joint_kept")
    if EARLY >= 2:
        d_down, d_up = down_rest[0](d_down), up_rest[0](d_up)
        down_rest, up_rest = down_rest[1:], up_rest[1:]
    (d_tokens,) = call(
        token_back_kernel,
        [((count, width), f32)],
        [(vm, info), (vm, partial), (vm, partial_across), (vm, joint), (vm, d_res)] + [(an, w) for w in wt],
        [pltpu.VMEM((4, 3 * GROUP, width), bf16), pltpu.SemaphoreType.DMA((4, 3, 2))],
        flops=2 * count * width * 3072,
        size=10 << 20,
        smem=(0,),
        name="token_back",
    )
    landmark_own = (partial[0].astype(f32) + partial_across[1].astype(f32)).astype(bf16)
    low_rank = dot(landmark_own, pooled_low, TN)
    low_rank = jnp.concatenate([low_rank[0:192], low_rank[GROUP : GROUP + 192]], axis=0)
    d_first = (joint_kept[0].astype(f32) + joint_sent[0].astype(f32) + low_rank).astype(bf16)
    d_second = (joint_kept[1].astype(f32) + joint_sent[1].astype(f32)).astype(bf16)
    norms = jnp.concatenate([sums_attn[0:2], sums_ffn[0:2]], axis=0)
    dtaps = jnp.pad(dtaps[:, 1:4], ((0, 0), (0, 0), (0, width - GROUP)))
    minor = jnp.concatenate([sums_up[:, 0:1], dtaps, jnp.broadcast_to(norms, (4, 4, width))], axis=1)
    minor = after(minor, joint_second)
    minor = minor[0:2] + hop(minor[2:4], 2)
    minor = minor[0] + hop(minor[1], 1)
    orders = [steps, steps[1:2] + steps[:1] + steps[2:]]
    values = [[d_first], [d_second], d_down, d_up, [minor]]
    tasks = [
        rest_of(orders[0], 0),
        rest_of(orders[1], 0),
        in_two(down_rest, down_order),
        in_two(up_rest, up_order),
        [lambda x: x] * LATE + [lambda x, step=step: [x[0] + hop_batch(x[0], step)] for step in steps],
    ]
    for turn in range(max(len(task) for task in tasks)):
        anchors = (values[0][0], values[1][0]) + ((d_tokens,) if turn == 0 else ())
        if turn == IDLE + 2:
            anchors += (values[2][-1], values[3][-1])
        values = [
            task[turn](after(value, *anchors)) if turn < len(task) else value for value, task in zip(values, tasks)
        ]
    d_parts = [values[0][0].astype(f32), values[1][0].astype(f32)]
    d_w_down, d_w_up = values[2][0].astype(f32), values[3][0].astype(f32)
    minor = values[4][0]
    d_w_query, d_w_key = d_parts[0][0:192].T, d_parts[0][192:384].T
    d_w_value, d_w_out = d_parts[1][0:192].T, d_parts[1][192:384]

    return (
        output[None],
        d_tokens[None],
        d_w_query,
        d_w_key,
        d_w_value,
        d_w_out,
        minor[1:4, 0:TAPS],
        d_w_up,
        minor[0],
        d_w_down,
        minor[4],
        minor[5],
        minor[6],
        minor[7],
    )


def solution(mesh):
    return jax.shard_map(
        functools.partial(local, mesh.shape["batch"]),
        mesh=mesh,
        in_specs=(
            P("batch", "head", None),
            P("batch"),
            P(None, "head"),
            P(None, "head"),
            P(None, "head"),
            P("head", None),
            P("head", None),
            P(None, "head"),
            P("head"),
            P("head", None),
            P(),
            P(),
            P(),
            P(),
            P("batch", "head", None),
        ),
        out_specs=(
            P("batch", "head", None),
            P("batch", "head", None),
            P(None, "head"),
            P(None, "head"),
            P(None, "head"),
            P("head", None),
            P("head", None),
            P(None, "head"),
            P("head"),
            P("head", None),
            P(),
            P(),
            P(),
            P(),
        ),
        check_vma=False,
    )
```
